32 devices in a mesh: neuron: 4 (over y, core), frame: 4 (over z), half: 2 (over x).
Axes of the slice: x: 2, y: 2, z: 4, core: 2. Of those that a mesh axis runs over, the one named last changes fastest.
Arguments:
- calcium: bfloat16 [128, 4096], P('neuron', 'frame'), may hold values from 0.049804688 to 2
- trial_of_frame: int32 [4096], P('frame'), may hold values from 0 to 63, never falling along the last dimension, each value on 1 to 128 neighbouring positions
- trial_half: int32 [64], replicated, may hold values from 0 to 1, as said below
- loadings: float32 [2, 128, 2048], P('half', 'neuron'), may hold values from 0.0001 to 0.002
- profiles: float32 [2, 32, 4096], P('half', None, 'frame'), may hold values from 0.05 to 1
Outputs:
- loadings_out: float32 [2, 128, 2048], P('half', 'neuron')
- profiles_out: float32 [2, 32, 4096], P('half', None, 'frame')
- similarity: float32 [2, 32, 32], P('half')
The draws below stay inside these ranges and needn't reach their ends.
Inputs may be any that keep to these rules, and one draw needn't show every extreme that they name: `trial_half`: exactly half of the 64 trials are assigned to each half. `trial_of_frame`: trial numbers never fall along the frames; each trial covers 1 to 128 frames.
All inputs are finite; a program needn't handle non-finite values.
Results may differ from the reference program's by a relative error of at most 0.0003.
Values may be sent and summed in bfloat16 or wider, within the bound.
A program may use at most 128 MiB of HBM per device.

```python
import math
import jax
import jax.numpy as jnp
import numpy as np
from jax import lax

K = 32
L = 64
FR_DEV = 1024
ITERS = 2
NEURONS = 128
FRAMES = 4096
TRIALS = 64


def draw_trial_half(key, part):
    order = jax.random.permutation(key, TRIALS)
    return (order % 2).astype(jnp.int32)


def level_of(key, extent, cuts, low, top_value):
    factor_of, own = 1.0, jax.random.fold_in(key, 6)
    for axis_at, parts in cuts:
        draws = jnp.exp(jax.random.uniform(jax.random.fold_in(own, axis_at), (parts,), jnp.float32, low / len(cuts), top_value / len(cuts)))
        factor_of = factor_of * jnp.repeat(draws, extent[axis_at] // parts).reshape([-1 if axis == axis_at else 1 for axis in range(len(extent))])
    return factor_of


def split_up(count, total, limit, lean):
    weights = [(1 << 20) // math.isqrt(rank ** lean) + 1 for rank in range(2, count + 1)]
    rest, given = total - limit - (count - 1), [1] * (count - 1)
    while rest > 0:
        movable = [i for i in range(count - 1) if given[i] < limit]
        whole, left = sum([weights[i] for i in movable]), rest
        for i in movable:
            extra = min(limit - given[i], max(1, left * weights[i] // whole), rest)
            given[i] = given[i] + extra
            rest = rest - extra
    return np.array([limit] + given)


def uneven(key, count, total, most, slope):
    if count == 2:
        one = jax.random.randint(key, (), max(1, total - most), min(most, total - 1) + 1)
        return jnp.stack([one, total - one])
    sizes = jnp.asarray(split_up(count, total, most, slope), jnp.int32)
    twos = (count - 1) // 2
    giver, sink = sizes[1:1 + 2 * twos:2], sizes[2:2 + 2 * twos:2]
    margin = jnp.minimum(giver - 1, most - sink)
    passed = jax.random.randint(jax.random.fold_in(key, 1), (twos,), 0, 1 << 20) % (margin + 1)
    sizes = sizes.at[1:1 + 2 * twos:2].set(giver - passed).at[2:2 + 2 * twos:2].set(sink + passed)
    return sizes[jax.random.permutation(jax.random.fold_in(key, 2), count)]


def setup_inputs(seed: int = 0) -> dict:
    splits = jax.random.split(jax.random.key(seed), 6)
    calcium = jnp.clip(jnp.exp(math.log(2.0) - 3.6927934 * jax.random.uniform(splits[0], (NEURONS, FRAMES), jnp.float32) ** level_of(splits[0], (NEURONS, FRAMES), ((0, 4), (1, 4)), -0.2, 0.2)), 0.049804688, 2.0).astype(jnp.bfloat16)
    trial_of_frame = jnp.searchsorted(jnp.cumsum(uneven(splits[1], TRIALS, FRAMES, FR_DEV // 8, 1)), jnp.arange(FRAMES), side="right").astype(jnp.int32)
    trial_half = draw_trial_half(jax.random.fold_in(splits[5], 71), 0)
    loadings = jnp.clip(jnp.exp(math.log(0.002) - 2.9957323 * jax.random.uniform(splits[3], (2, NEURONS, K * L), jnp.float32) ** level_of(splits[3], (2, NEURONS, K * L), ((0, 2), (1, 4)), -0.2, 0.2)), 0.0001, 0.002)
    profiles = jnp.clip(jnp.exp(math.log(1.0) - 2.9957323 * jax.random.uniform(splits[4], (2, K, FRAMES), jnp.float32) ** level_of(splits[4], (2, K, FRAMES), ((0, 2), (2, 4)), -0.2, 0.2)), 0.05, 1.0)
    return dict(calcium=calcium, trial_of_frame=trial_of_frame, trial_half=trial_half, loadings=loadings, profiles=profiles)


epsilon = 1e-06

def lagged_profiles(window, span_width, lag_count):
    pieces = [window[:, lag_count - 1 - offset:lag_count - 1 - offset + span_width] for offset in range(lag_count)]
    return jnp.stack(pieces, axis=1).reshape(-1, span_width)

def lagged_data(window, span_width, lag_count):
    pieces = [window[:, offset:offset + span_width] for offset in range(lag_count)]
    return jnp.stack(pieces, axis=1).reshape(-1, span_width)

def reference(calcium, trial_of_frame, trial_half, loadings, profiles):
    neuron_rows, frame_count = calcium.shape
    block_width = min(256, frame_count)
    block_starts = list(range(0, frame_count, block_width))
    loads_final = []
    profs_final = []
    for half_index in range(2):
        frame_mask = (trial_half[trial_of_frame] == half_index).astype(jnp.bfloat16)
        masked = calcium * frame_mask[None, :]
        data_ext = jnp.concatenate([masked, masked[:, :L - 1]], axis=1)
        loading = loadings[half_index]
        profile = profiles[half_index]
        for sweep in range(ITERS):
            load_bf = loading.astype(jnp.bfloat16)
            load_t = load_bf.reshape(neuron_rows, K, L).transpose(1, 0, 2).reshape(K, neuron_rows * L)
            prof_bf = profile.astype(jnp.bfloat16)
            prof_ext = jnp.concatenate([prof_bf[:, frame_count - (L - 1):], prof_bf], axis=1)
            approx_parts = []
            for start in block_starts:
                lagged = lagged_profiles(prof_ext[:, start:start + block_width + L - 1], block_width, L)
                approx_parts.append(jnp.dot(load_bf, lagged, preferred_element_type=jnp.float32))
            approx = jnp.concatenate(approx_parts, axis=1).astype(jnp.bfloat16) * frame_mask[None, :]
            approx_ext = jnp.concatenate([approx, approx[:, :L - 1]], axis=1)
            numer_parts = []
            denom_parts = []
            for start in block_starts:
                data_lag = lagged_data(data_ext[:, start:start + block_width + L - 1], block_width, L)
                approx_lag = lagged_data(approx_ext[:, start:start + block_width + L - 1], block_width, L)
                numer_parts.append(jnp.dot(load_t, data_lag, preferred_element_type=jnp.float32))
                denom_parts.append(jnp.dot(load_t, approx_lag, preferred_element_type=jnp.float32))
            numer = jnp.concatenate(numer_parts, axis=1)
            denom = jnp.concatenate(denom_parts, axis=1)
            profile = profile * numer / jnp.maximum(denom, 1.0)
            prof_bf = profile.astype(jnp.bfloat16)
            prof_ext = jnp.concatenate([prof_bf[:, frame_count - (L - 1):], prof_bf], axis=1)
            numer_w = jnp.zeros((neuron_rows, K * L), jnp.float32)
            denom_w = jnp.zeros((neuron_rows, K * L), jnp.float32)
            for start in block_starts:
                lagged = lagged_profiles(prof_ext[:, start:start + block_width + L - 1], block_width, L)
                approx_block = jnp.dot(load_bf, lagged, preferred_element_type=jnp.float32).astype(jnp.bfloat16)
                approx_block = approx_block * frame_mask[None, start:start + block_width]
                data_block = masked[:, start:start + block_width]
                numer_w = numer_w + lax.dot_general(data_block, lagged, (((1,), (1,)), ((), ())), preferred_element_type=jnp.float32)
                denom_w = denom_w + lax.dot_general(approx_block, lagged, (((1,), (1,)), ((), ())), preferred_element_type=jnp.float32)
            loading = loading * numer_w / denom_w
            scales = jnp.sqrt(lax.optimization_barrier(jnp.sum(profile * profile, axis=1)) + epsilon)
            profile = profile / scales[:, None]
            loading = (loading.reshape(neuron_rows, K, L) * scales[None, :, None]).reshape(neuron_rows, K * L)
        loads_final.append(loading)
        profs_final.append(profile)
    sims = []
    for half_index in range(2):
        own_factors = loads_final[half_index].reshape(neuron_rows, K, L)
        far_factors = loads_final[1 - half_index].reshape(neuron_rows, K, L)
        cross_sum = jnp.einsum('nkl,njl->kj', own_factors, far_factors, precision=lax.Precision.HIGHEST)
        own_squares = lax.optimization_barrier(jnp.sum(own_factors * own_factors, axis=(0, 2)))
        far_squares = lax.optimization_barrier(jnp.sum(far_factors * far_factors, axis=(0, 2)))
        sims.append(cross_sum / jnp.sqrt((own_squares + epsilon)[:, None] * (far_squares + epsilon)[None, :]))
    return (jnp.stack(loads_final), jnp.stack(profs_final), jnp.stack(sims))
```

```python
import functools

import jax
import jax.numpy as jnp
from jax import lax
from jax.experimental import pallas as pl
from jax.experimental.pallas import tpu as pltpu
from jax.sharding import PartitionSpec as P

K = 32
L = 64
ITERS = 2
EPS = 1e-06
RIM = 128
GROUPS = 8
GL = L // GROUPS
GW = GL * K
MESH = pl.DeviceIdType.MESH
F32 = jnp.float32
BF16 = jnp.bfloat16


def dot(a, b):
    return jnp.dot(a, b, preferred_element_type=F32)


def kernel(
    NN, NF, T,
    ca_ref, tof_ref, th_ref, w_ref, prof_ref,
    wout_ref, hout_ref, sim_ref,
    hs, hlag, mext, ms, mlag, alag, acc, accn, accd, hf, wg, wt, wown, stk,
    mrim_s, mrim_r, rim_s, rim_r, ndx, ndr, hall, ssr, wqx, wqr, wqs, wqt, wgb, wfin, pts, ptr, snr, sfr,
    mr_sem, rim_ss, rim_rs, nd_ss, nd_rs, hg_ss, hg_rs, ss_ss, ss_rs,
    ws_ss, ws_rs, wt_ss, wt_rs, wg_ss, wg_rs, pt_sem, sn_ss, sn_rs, sf_ss, sf_rs,
):
    me_n = lax.axis_index("neuron")
    me_f = lax.axis_index("frame")
    me_h = lax.axis_index("half")
    N = ca_ref.shape[0]
    EXT = T + RIM
    gp = GROUPS // NF
    rg = K // 8
    w = T * rg // NN
    pending = []

    def send(src, dst, ssem, rsem, axis, peer):
        c = pltpu.make_async_remote_copy(
            src_ref=src, dst_ref=dst, send_sem=ssem, recv_sem=rsem,
            device_id={axis: peer}, device_id_type=MESH,
        )
        c.start()
        pending.append(c)
        return c

    def npeer(r):
        return lax.rem(me_n + r, NN)

    def fpeer(r):
        return lax.rem(me_f + r, NF)

    barrier = pltpu.get_barrier_semaphore()
    for r in range(1, NN):
        pl.semaphore_signal(barrier, inc=1, device_id={"neuron": npeer(r)}, device_id_type=MESH)
    for r in range(1, NF):
        pl.semaphore_signal(barrier, inc=1, device_id={"frame": fpeer(r)}, device_id_type=MESH)
    pl.semaphore_signal(barrier, inc=1, device_id={"half": 1 - me_h}, device_id_type=MESH)

    trials = th_ref.shape[1]
    rows = lax.broadcasted_iota(jnp.int32, (trials, trials), 0)
    cols = lax.broadcasted_iota(jnp.int32, (trials, trials), 1)
    thf = th_ref[...].astype(F32)
    th_col = jnp.sum(jnp.where(rows == cols, thf, 0.0), axis=1, keepdims=True)
    chosen = jnp.where(th_col == me_h.astype(F32), 1.0, 0.0)
    hit = lax.broadcasted_iota(jnp.int32, (trials, T), 0) == tof_ref[...]
    mask = jnp.sum(jnp.where(hit, chosen, 0.0), axis=0, keepdims=True)
    masked = (ca_ref[...].astype(F32) * mask).astype(BF16)
    mext[:, :T] = masked
    mrim_s[...] = masked[:, :RIM]
    hf[...] = prof_ref[...]
    rim_s[0, 0] = prof_ref[:, :RIM]
    rim_s[0, 1] = prof_ref[:, T - RIM:]

    pl.semaphore_wait(barrier, (NN - 1) + (NF - 1) + 1)

    left = fpeer(NF - 1)
    right = fpeer(1)
    rims = {}

    def send_rims(i):
        rims[i] = (
            send(rim_s.at[i, 0], rim_r.at[i, 0], rim_ss.at[i, 0], rim_rs.at[i, 0], "frame", left),
            send(rim_s.at[i, 1], rim_r.at[i, 1], rim_ss.at[i, 1], rim_rs.at[i, 1], "frame", right),
        )

    send_rims(0)
    mcopy = send(mrim_s, mrim_r, mr_sem.at[0], mr_sem.at[1], "frame", left)

    for g in range(GROUPS):
        wg[g] = w_ref[g].astype(BF16)
    wown[...] = w_ref[pl.ds(me_f * gp, gp)]

    crow = (me_n % rg) * 8
    ccol = (me_n // rg) * w
    if NN == rg:
        hown = prof_ref[pl.ds(pl.multiple_of(crow, 8), 8), :]
    else:
        hown = prof_ref[pl.ds(pl.multiple_of(crow, 8), 8), pl.ds(pl.multiple_of(ccol, 128), w)]

    def own_rows(col):
        out = col[0:8]
        for q in range(1, rg):
            out = jnp.where(me_n % rg == q, col[q * 8:(q + 1) * 8], out)
        return out

    def build_right(width, lo=0, hi=GROUPS, extra=None):
        def body(g, _):
            v = hs[...]
            for b in range(GL):
                hlag[pl.ds(pl.multiple_of(g * GW + b * K, K), K), :width] = (
                    v[:, 2 * RIM - b:2 * RIM - b + width]
                )
            hs[:, RIM:] = v[:, RIM - GL:hs.shape[1] - GL]
            part = dot(wg[g], hlag[pl.ds(pl.multiple_of(g * GW, GW), GW), :width])
            acc[:, :width] = acc[:, :width] + part
            if extra is not None:
                extra(g)
            return 0

        if lo == 0:
            acc[...] = jnp.zeros_like(acc)
        lax.fori_loop(lo, hi, body, 0)

    def fill_hs(left_rim, body, right_rim):
        hs[:, :RIM] = jnp.zeros((K, RIM), BF16)
        hs[:, RIM:2 * RIM] = left_rim.astype(BF16)
        hs[:, 2 * RIM:2 * RIM + T] = body.astype(BF16)
        hs[:, 2 * RIM + T:] = right_rim.astype(BF16)

    def build_left(dst, g):
        v = ms[...]
        for b in range(GL):
            dst[pl.ds(pl.multiple_of(g * GW + b * N, N), N), :] = v[:, b:b + T]
        ms[:, :EXT] = v[:, GL:EXT + GL]

    mcopy.wait_recv()
    mext[:, T:] = mrim_r[...]
    ms[:, :EXT] = mext[...]
    ms[:, EXT:] = jnp.zeros((N, RIM), BF16)

    def mbody(g, _):
        build_left(mlag, g)
        return 0

    lax.fori_loop(0, GROUPS, mbody, 0)
    stk[:N] = mext[:, :T]
    mask_ext = jnp.where(mext[...].astype(F32) > 0.0, 1.0, 0.0)

    def send_sums(it, kind, src):
        for p in range(NN):
            a, b = (p % rg) * 8, (p // rg) * w
            ndx[it, kind, p] = src[a:a + 8, b:b + w]
        at = 2 * it + kind
        return [
            send(ndx.at[it, kind, npeer(r)], ndr.at[it, kind, r - 1], nd_ss.at[at, r], nd_rs.at[at, r],
                 "neuron", npeer(r))
            for r in range(1, NN)
        ]

    RQ = 2 * N // 4
    quad = lax.broadcasted_iota(jnp.int32, (RQ, 128), 1) // K
    wcs = {}

    def contract(rows_bf, g):
        rws = pl.ds(pl.multiple_of(g * GW, GW), GW)
        return lax.dot_general(
            rows_bf, hlag[rws, :T], (((1,), (1,)), ((), ())), preferred_element_type=F32
        )

    scale = None
    for it in range(ITERS):
        last = it == ITERS - 1
        def tbody(g, _):
            x = wg[g].astype(F32)
            for h in range(GW // 128):
                t = x[:, h * 128:(h + 1) * 128].T
                wt[g, :, h * 128:(h + 1) * 128] = jnp.concatenate(
                    [t[q * K:(q + 1) * K] for q in range(4)], axis=1
                ).astype(BF16)
            return 0

        lax.fori_loop(0, GROUPS, tbody, 0)

        accn[...] = jnp.zeros_like(accn)

        def nbody(g, _):
            accn[...] = accn[...] + dot(wt[g], mlag[pl.ds(pl.multiple_of(g * GW, GW), GW), :])
            return 0

        lax.fori_loop(0, GROUPS, nbody, 0)
        ncs = send_sums(it, 0, accn)
        if it == 0:
            for c in rims[it]:
                c.wait_recv()
            fill_hs(rim_r[it, 1], hf[...], rim_r[it, 0])
        else:
            rims[it][0].wait_recv()
            fill_hs(rim_r[it, 1] / scale, hf[...] / scale, rim_r[it, 0] / scale)
        build_right(EXT)
        approx = (acc[...].astype(BF16).astype(F32) * mask_ext).astype(BF16)
        ms[:, :EXT] = approx

        accd[...] = jnp.zeros_like(accd)

        def dbody(g, _):
            build_left(alag, g)
            rws = pl.ds(pl.multiple_of(g * GW, GW), GW)
            accd[...] = accd[...] + dot(wt[g], alag[rws, :])
            return 0

        lax.fori_loop(0, GROUPS, dbody, 0)
        dcs = send_sums(it, 1, accd)
        num = ndx[it, 0, me_n]
        den = ndx[it, 1, me_n]
        for r in range(1, NN):
            ncs[r - 1].wait_recv()
            num = num + ndr[it, 0, r - 1]
        for r in range(1, NN):
            dcs[r - 1].wait_recv()
            den = den + ndr[it, 1, r - 1]
        hown = hown * num / jnp.maximum(den, 1.0)
        hall[it, me_n] = hown
        cs = [
            send(hall.at[it, me_n], hall.at[it, me_n], hg_ss.at[it, r], hg_rs.at[it, r], "neuron", npeer(r))
            for r in range(1, NN)
        ]
        for c in cs:
            c.wait_recv()
        for p in range(NN):
            a, b = (p % rg) * 8, (p // rg) * w
            hf[a:a + 8, b:b + w] = hall[it, p]
        hnew = hf[...]
        rim_s[it + 1, 0] = hnew[:, :RIM]
        rim_s[it + 1, 1] = hnew[:, T - RIM:]
        send_rims(it + 1)
        sq = jnp.sum(hnew * hnew, axis=1, keepdims=True)
        ssr[it, me_f] = jnp.broadcast_to(sq, (K, 128))
        ssc = [
            send(ssr.at[it, me_f], ssr.at[it, me_f], ss_ss.at[it, r], ss_rs.at[it, r], "frame", fpeer(r))
            for r in range(1, NF)
        ]
        rims[it + 1][1].wait_recv()
        fill_hs(rim_r[it + 1, 1], hnew, hnew[:, :RIM])
        build_right(T)
        approx2 = (acc[:, :T].astype(BF16).astype(F32) * mask_ext[:, :T]).astype(BF16)
        stk[N:] = approx2
        for r in list(range(1, NF)) + [0]:
            p = fpeer(r)
            sums = [contract(stk[...], p * gp + q) for q in range(gp)]
            if r:
                top = sums[0][:, :128]
                for x in sums:
                    for h in range(GW // 128):
                        top = jnp.maximum(top, x[:, h * 128:(h + 1) * 128])
                top = jnp.maximum(top, pltpu.roll(top, 64, 1))
                top = jnp.maximum(top, pltpu.roll(top, 32, 1))
                inv = 65534.0 / jnp.maximum(top, 1e-30)
                inv = jnp.concatenate([inv] * (GW // 128), axis=1)
                for q in range(gp):
                    code = jnp.minimum(jnp.round(sums[q] * inv) - 32767.0, 32767.0)
                    wqx[it, r - 1, q] = code.astype(jnp.int32).astype(jnp.int16)
                packed = top[:RQ]
                for j in range(1, 4):
                    packed = jnp.where(quad == j, top[j * RQ:(j + 1) * RQ], packed)
                wqs[it, r - 1] = packed
                wcs[r - 1] = (
                    send(wqs.at[it, r - 1], wqt.at[it, r - 1], wt_ss.at[it, r], wt_rs.at[it, r], "frame", p),
                    send(wqx.at[it, r - 1], wqr.at[it, r - 1], ws_ss.at[it, r], ws_rs.at[it, r], "frame", p),
                )
            else:
                wtot = sums
        for c in ssc:
            c.wait_recv()
        total = ssr[it, 0]
        for p in range(1, NF):
            total = total + ssr[it, p]
        scale_wide = jnp.sqrt(total + EPS)
        scale = scale_wide[:, 0:1]
        ek = lax.broadcasted_iota(jnp.int32, (K, GW), 0)
        ec = lax.broadcasted_iota(jnp.int32, (K, GW), 1) % K
        scale_row = jnp.sum(jnp.where(ek == ec, scale, 0.0), axis=0, keepdims=True)
        hown = hown / own_rows(scale)
        for r in range(1, NF):
            for c in wcs[r - 1]:
                c.wait_recv()
            packed = wqt[it, r - 1]
            tops = []
            for j in range(4):
                t = jnp.where(quad == j, packed, 0.0)
                t = t + pltpu.roll(t, 64, 1)
                tops.append(t + pltpu.roll(t, 32, 1))
            unit = jnp.concatenate(tops, axis=0) * (1.0 / 65534.0)
            unit = jnp.concatenate([unit] * (GW // 128), axis=1)
            wtot = [
                wtot[q] + (wqr[it, r - 1, q].astype(jnp.int32).astype(F32) + 32767.0) * unit
                for q in range(gp)
            ]
        wnew = jnp.stack([wown[q] * wtot[q][:N] / wtot[q][N:] * scale_row for q in range(gp)])
        wown[...] = wnew
        mine = pl.ds(me_f * gp, gp)
        if not last:
            wgb[it, mine] = wnew.astype(BF16)
            cs = [
                send(wgb.at[it, mine], wgb.at[it, mine], wg_ss.at[it, r], wg_rs.at[it, r], "frame", fpeer(r))
                for r in range(1, NF)
            ]
            for c in cs:
                c.wait_recv()
            wg[...] = wgb[it]

    pts[...] = wnew.astype(BF16)
    ptc = send(pts, ptr, pt_sem.at[0], pt_sem.at[1], "half", 1 - me_h)
    wfin[mine] = wnew
    fcs = [
        send(wfin.at[mine], wfin.at[mine], wg_ss.at[ITERS - 1, r], wg_rs.at[ITERS - 1, r], "frame", fpeer(r))
        for r in range(1, NF)
    ]
    hout_ref[...] = hf[...] / scale
    ptc.wait_recv()
    far = ptr[...].astype(F32)
    cross = jnp.zeros((128, 128), F32)
    osq = jnp.zeros((1, 128), F32)
    fsq = jnp.zeros((1, 128), F32)
    for q in range(gp):
        for h in range(GW // 128):
            a = wnew[q, :, h * 128:(h + 1) * 128]
            b = far[q, :, h * 128:(h + 1) * 128]
            cross = cross + lax.dot_general(
                a, b, (((0,), (0,)), ((), ())),
                preferred_element_type=F32, precision=lax.Precision.HIGHEST,
            )
            osq = osq + jnp.sum(a * a, axis=0, keepdims=True)
            fsq = fsq + jnp.sum(b * b, axis=0, keepdims=True)
    ri = lax.broadcasted_iota(jnp.int32, (128, 128), 0)
    ci = lax.broadcasted_iota(jnp.int32, (128, 128), 1)
    cross = jnp.where(ri // K == ci // K, cross, 0.0)
    cross = cross[0:K] + cross[K:2 * K] + cross[2 * K:3 * K] + cross[3 * K:]

    def fold(x):
        x = x + pltpu.roll(x, 64, 1)
        return x + pltpu.roll(x, 32, 1)

    pack = jnp.concatenate(
        [cross, jnp.broadcast_to(osq, (8, 128)), jnp.broadcast_to(fsq, (8, 128))], axis=0
    )
    snr[me_n] = fold(pack)
    cs = [
        send(snr.at[me_n], snr.at[me_n], sn_ss.at[r], sn_rs.at[r], "neuron", npeer(r))
        for r in range(1, NN)
    ]
    for c in cs:
        c.wait_recv()
    tot = snr[0]
    for p in range(1, NN):
        tot = tot + snr[p]
    sfr[me_f] = tot
    cs = [
        send(sfr.at[me_f], sfr.at[me_f], sf_ss.at[r], sf_rs.at[r], "frame", fpeer(r))
        for r in range(1, NF)
    ]
    for c in fcs:
        c.wait_recv()
    wout_ref[...] = wfin[...]
    for c in cs:
        c.wait_recv()
    tot = sfr[0]
    for p in range(1, NF):
        tot = tot + sfr[p]
    own_row = tot[K:K + 1]
    far_row = tot[K + 8:K + 9]
    rk = lax.broadcasted_iota(jnp.int32, (K, 128), 0)
    ck = lax.broadcasted_iota(jnp.int32, (K, 128), 1)
    own_col = jnp.sum(jnp.where(rk == ck, own_row, 0.0), axis=1, keepdims=True)
    sim = tot[:K] / jnp.sqrt((own_col + EPS) * (far_row + EPS))
    sim_ref[...] = sim[:, :K]
    rims[ITERS][0].wait_recv()
    for c in pending:
        c.wait_send()


def roll_right(x, s):
    return pltpu.roll(x, s, 1) if s else x


def roll_left(x, s):
    return pltpu.roll(x, x.shape[1] - s, 1) if s else x


def wide_kernel(
    NN, NF, T,
    ca_ref, tof_ref, th_ref, w_ref, prof_ref,
    wout_ref, hout_ref, sim_ref,
    rim_s, rim_r, mtx, mrx, w32, wt32, hla, mla, ala,
    ndx, ndr, hb, hl, ml, al, dat, md, prx, acc, own, tx, rx, sqx, sqr, scx, scr,
    hg, hgr, wfin, far_s, far_r, snx, snr,
    ssem, rsem,
):
    me_n = lax.axis_index("neuron")
    me_f = lax.axis_index("frame")
    me_h = lax.axis_index("half")
    me_c = lax.rem(me_n, 2)
    me_y = me_n // 2
    N = ca_ref.shape[0]
    F = NF * T
    NB = N // NF
    KC = K // 2
    TC = T // 2
    EXT = T + RIM
    pending = []

    def send(src, dst, peer):
        i = len(pending)
        c = pltpu.make_async_remote_copy(
            src_ref=src, dst_ref=dst, send_sem=ssem.at[i], recv_sem=rsem.at[i],
            device_id=peer, device_id_type=MESH,
        )
        c.start()
        pending.append(c)
        return c

    def npeer(r):
        return lax.rem(me_n + r, NN)

    def fpeer(r):
        return lax.rem(me_f + r, NF)

    core = {"neuron": me_n + 1 - 2 * me_c}
    seven = [(dy, dz) for dz in (3, 2, 1, 0) for dy in (1, 0) if dy or dz]

    def block_of(dy, dz):
        return fpeer(dz) * 2 + lax.rem(me_y + dy, 2)

    def to(dy, dz):
        return {"neuron": npeer(2 * dy), "frame": fpeer(dz)}

    others = [(dn, df) for df in (3, 2, 1, 0) for dn in (3, 2, 1, 0) if dn or df]
    barrier = pltpu.get_barrier_semaphore()
    for dn, df in others:
        pl.semaphore_signal(
            barrier, inc=1, device_id={"neuron": npeer(dn), "frame": fpeer(df)}, device_id_type=MESH
        )
    pl.semaphore_signal(barrier, inc=1, device_id={"half": 1 - me_h}, device_id_type=MESH)

    trials = th_ref.shape[1]
    rows = lax.broadcasted_iota(jnp.int32, (trials, trials), 0)
    cols = lax.broadcasted_iota(jnp.int32, (trials, trials), 1)
    thf = th_ref[...].astype(F32)
    th_col = jnp.sum(jnp.where(rows == cols, thf, 0.0), axis=1, keepdims=True)
    chosen = jnp.where(th_col == me_h.astype(F32), 1.0, 0.0)
    hit = lax.broadcasted_iota(jnp.int32, (trials, T), 0) == tof_ref[...]
    mask = jnp.sum(jnp.where(hit, chosen, 0.0), axis=0, keepdims=True)
    masked = ca_ref[...].astype(F32) * mask
    body = masked.astype(BF16)
    prof = prof_ref[...].astype(BF16)
    rim_s[0, :N] = body[:, :RIM]
    rim_s[0, N:] = prof[:, :RIM]
    rim_s[1, :K] = prof[:, T - RIM:]
    for z in range(NF):
        x = masked[z * NB:(z + 1) * NB]
        mtx[z] = jnp.concatenate([x[:, :TC], x[:, TC:]], axis=0).astype(BF16)

    def turn(x):
        out = []
        for h in range(GW // 128):
            t = x[:, h * 128:(h + 1) * 128].T
            out.append(jnp.concatenate([t[q * K:(q + 1) * K] for q in range(4)], axis=1))
        return jnp.concatenate(out, axis=1).astype(BF16)

    for a in range(GROUPS):
        x = w_ref[a]
        w32[a * N:(a + 1) * N] = x.astype(BF16)
        wt32[a * K:(a + 1) * K] = turn(x)
    mine = pl.ds(pl.multiple_of(me_f * NB, NB), NB)
    w8 = jnp.concatenate([w_ref[a, mine, :] for a in range(GROUPS)], axis=0)

    pl.semaphore_wait(barrier, len(others) + 1)

    to_left = send(rim_s.at[0], rim_r.at[0], {"frame": fpeer(NF - 1)})
    to_right = send(rim_s.at[1, pl.ds(0, K)], rim_r.at[1, pl.ds(0, K)], {"frame": fpeer(1)})
    mcs = [
        send(mtx.at[fpeer(r)], mrx.at[me_f], {"frame": fpeer(r)})
        for r in (3, 2, 1)
    ]
    mrx[me_f] = mtx[me_f]

    to_left.wait_recv()
    mext = jnp.concatenate([body, rim_r[0, :N]], axis=1)
    mask_ext = jnp.where(mext.astype(F32) > 0.0, 1.0, 0.0)

    def lags(dst, x, roll):
        n = x.shape[0]
        for b in range(GL):
            dst[b * n:(b + 1) * n] = roll(x, b)

    def numer_of(m):
        q = dot(wt32[...], m[...])
        s = q[:K]
        for a in range(1, GROUPS):
            s = s + roll_left(q[a * K:(a + 1) * K], a * GL)
        return s[:, :T]

    def scatter(kind, s):
        for p in range(NN):
            a, b = (p % 2) * KC, (p // 2) * TC
            ndx[kind, p] = s[a:a + KC, b:b + TC]
        return [
            send(ndx.at[kind, npeer(r)], ndr.at[kind, r - 1], {"neuron": npeer(r)})
            for r in range(1, NN)
        ]

    lags(mla, mext, roll_left)
    ncs = scatter(0, numer_of(mla))
    to_right.wait_recv()
    lags(hla, jnp.concatenate([rim_r[1, :K], prof, rim_r[0, N:]], axis=1), roll_right)
    p = dot(w32[...], hla[...])
    s = p[:N]
    for a in range(1, GROUPS):
        s = s + roll_right(p[a * N:(a + 1) * N], a * GL)
    approx = (s[:, RIM:].astype(BF16).astype(F32) * mask_ext).astype(BF16)
    lags(ala, approx, roll_left)
    dcs = scatter(1, numer_of(ala))

    own_rows = pl.ds(pl.multiple_of(me_c * KC, KC), KC)
    far_rows = pl.ds(pl.multiple_of((1 - me_c) * KC, KC), KC)
    hown = prof_ref[own_rows, pl.ds(pl.multiple_of(me_y * TC, TC), TC)]
    num = ndx[0, me_n]
    den = ndx[1, me_n]
    for r in range(1, NN):
        ncs[r - 1].wait_recv()
        num = num + ndr[0, r - 1]
    for r in range(1, NN):
        dcs[r - 1].wait_recv()
        den = den + ndr[1, r - 1]
    hown = hown * num / jnp.maximum(den, 1.0)

    def spot(c, blk):
        return pl.ds(pl.multiple_of(c * KC, KC), KC), pl.ds(pl.multiple_of(blk * TC, TC), TC)

    lane = lax.broadcasted_iota(jnp.int32, (8, 128), 1)

    def gather_h(it):
        a, b = spot(me_c, block_of(0, 0))
        hb[it, a, b] = hown.astype(BF16)
        cs = [send(hb.at[it, a, b], hb.at[it, a, b], to(dy, dz)) for dy, dz in seven]
        relays = [send(hb.at[it, a, b], hb.at[it, a, b], core)]
        sq = jnp.sum(hown * hown, axis=1, keepdims=True)
        sqx[it] = jnp.where(lane < 64, sq[:8], sq[8:])
        sqs = [send(sqx.at[it], sqr.at[it, i], to(dy, dz)) for i, (dy, dz) in enumerate(seven)]
        return cs, relays, sqs

    def relay_h(it, cs, relays):
        for i in range(len(seven) - 1, -1, -1):
            cs[i].wait_recv()
            dy, dz = seven[i]
            a, b = spot(me_c, block_of(dy, NF - dz))
            relays.append(send(hb.at[it, a, b], hb.at[it, a, b], core))
        for c in relays:
            c.wait_recv()

    def squares(it, sqs):
        for c in sqs:
            c.wait_recv()
        t = sqx[it]
        for i in range(len(seven)):
            t = t + sqr[it, i]
        return jnp.concatenate(
            [jnp.broadcast_to(t[:, 0:1], (8, 128)), jnp.broadcast_to(t[:, 64:65], (8, 128))], axis=0
        )

    cs, relays, sqs = gather_h(0)

    for c in mcs:
        c.wait_recv()
    for z in range(NF):
        x = mrx[z].astype(F32)
        md[:, z * T:z * T + TC] = x[:NB]
        md[:, z * T + TC:(z + 1) * T] = x[NB:]
    data = md[...]
    mask_all = jnp.where(data[0:1] > 0.0, 1.0, 0.0)
    rolled = [roll_left(data, a * GL) for a in range(GROUPS)]
    for a in range(GROUPS):
        dat[a * 2 * NB:a * 2 * NB + NB] = rolled[a]
    lags(ml, jnp.concatenate(rolled[:4], axis=0).astype(BF16), roll_left)

    def recon(wb):
        p = dot(wb, hl[...])
        s = p[:NB]
        for a in range(1, GROUPS):
            s = s + roll_right(p[a * NB:(a + 1) * NB], a * GL)
        return s.astype(BF16).astype(F32) * mask_all

    def corr(wt, m):
        q = dot(wt, m[...])
        return q[:K] + roll_left(q[K:], 4 * GL)

    def template_ratio():
        approx = recon(w8.astype(BF16))
        for a in range(GROUPS):
            dat[a * 2 * NB + NB:(a + 1) * 2 * NB] = roll_left(approx, a * GL)
        s = lax.dot_general(
            dat[...].astype(BF16), hl[...], (((1,), (1,)), ((), ())), preferred_element_type=F32
        )
        wnum = jnp.concatenate([s[a * 2 * NB:a * 2 * NB + NB] for a in range(GROUPS)], axis=0)
        wden = jnp.concatenate([s[a * 2 * NB + NB:(a + 1) * 2 * NB] for a in range(GROUPS)], axis=0)
        return wnum, wden

    relay_h(0, cs, relays)
    lags(hl, hb[0], roll_right)
    wnum, wden = template_ratio()
    w8 = w8 * wnum / wden

    wt = jnp.concatenate([turn(w8[:4 * NB]), turn(w8[4 * NB:])], axis=0)

    def reduce_start(kind, s):
        acc[kind] = s
        return send(acc.at[kind, far_rows], prx.at[kind], core)

    def reduce_spread(kind, c):
        c.wait_recv()
        s = acc[kind, own_rows, :] + prx[kind]
        own[kind] = s
        top = jnp.max(s, axis=1, keepdims=True)
        e = jnp.ceil(jnp.log2(jnp.maximum(top, 1e-30)) + 0.01)
        code = jnp.minimum(jnp.round(s * jnp.exp2(16.0 - e)) - 32767.0, 32767.0)
        code = code.astype(jnp.int32).astype(jnp.int16)
        ee = jnp.broadcast_to(e, (KC, 128)).astype(jnp.int32).astype(jnp.int16)
        for blk in range(2 * NF):
            tx[kind, blk, :, :TC] = code[:, blk * TC:(blk + 1) * TC]
            tx[kind, blk, :, TC:] = ee
        return [
            send(tx.at[kind, block_of(dy, dz)], rx.at[kind, i], to(dy, dz))
            for i, (dy, dz) in enumerate(seven)
        ]

    def reduce_done(kind, cs):
        t = own[kind, :, pl.ds(pl.multiple_of(block_of(0, 0) * TC, TC), TC)]
        for i in range(len(seven) - 1, -1, -1):
            cs[i].wait_recv()
            e = rx[kind, i, :, TC:].astype(jnp.int32).astype(F32)
            unit = jnp.concatenate([jnp.exp2(e - 16.0)] * (TC // 128), axis=1)
            t = t + (rx[kind, i, :, :TC].astype(jnp.int32).astype(F32) + 32767.0) * unit
        return t

    nc = reduce_start(0, corr(wt, ml))
    approx = recon(w8.astype(BF16))
    lags(al, jnp.concatenate([roll_left(approx, a * GL) for a in range(4)], axis=0).astype(BF16), roll_left)
    ncs = reduce_spread(0, nc)
    dc = reduce_start(1, corr(wt, al))
    scale0 = jnp.sqrt(squares(0, sqs) + EPS)
    dcs = reduce_spread(1, dc)
    num = reduce_done(0, ncs)
    den = reduce_done(1, dcs)
    s0 = scale0[:, 0:1]
    hown = hown * (num * s0) / jnp.maximum(den * s0, 1.0)
    cs, relays, sqs = gather_h(1)
    hg[me_n] = hown
    hcs = [send(hg.at[me_n], hg.at[me_n], {"neuron": npeer(r)}) for r in (3, 2, 1)]
    relay_h(1, cs, relays)
    total = squares(1, sqs)
    scx[...] = jnp.sqrt(total + EPS * scale0 * scale0)
    sc = send(scx, scr, core)
    lags(hl, hb[1], roll_right)
    wnum, wden = template_ratio()
    sc.wait_recv()
    mine_first = me_c == 0
    scale = jnp.concatenate(
        [jnp.where(mine_first, scx[...], scr[...]), jnp.where(mine_first, scr[...], scx[...])], axis=0
    )[:, 0:1]
    ek = lax.broadcasted_iota(jnp.int32, (K, GW), 0)
    ec = lax.broadcasted_iota(jnp.int32, (K, GW), 1) % K
    scale_row = jnp.sum(jnp.where(ek == ec, scale, 0.0), axis=0, keepdims=True)
    w8 = w8 * wnum / wden * scale_row

    far_s[...] = w8.astype(BF16)
    fc = send(far_s, far_r, {"half": 1 - me_h})
    wfin[me_f] = w8
    wcs = [send(wfin.at[me_f], wfin.at[me_f], {"frame": fpeer(r)}) for r in (3, 2, 1)]
    for c in hcs:
        c.wait_recv()
    for p in range(NN):
        a, b = (p % 2) * KC, (p // 2) * TC
        hout_ref[a:a + KC, b:b + TC] = hg[p] / scale[a:a + KC]
    fc.wait_recv()
    far = far_r[...].astype(F32)
    cross = jnp.zeros((128, 128), F32)
    osq = jnp.zeros((1, 128), F32)
    fsq = jnp.zeros((1, 128), F32)
    for h in range(GW // 128):
        a = w8[:, h * 128:(h + 1) * 128]
        b = far[:, h * 128:(h + 1) * 128]
        cross = cross + lax.dot_general(
            a, b, (((0,), (0,)), ((), ())),
            preferred_element_type=F32, precision=lax.Precision.HIGHEST,
        )
        osq = osq + jnp.sum(a * a, axis=0, keepdims=True)
        fsq = fsq + jnp.sum(b * b, axis=0, keepdims=True)
    ri = lax.broadcasted_iota(jnp.int32, (128, 128), 0)
    ci = lax.broadcasted_iota(jnp.int32, (128, 128), 1)
    cross = jnp.where(ri // K == ci // K, cross, 0.0)
    cross = cross[0:K] + cross[K:2 * K] + cross[2 * K:3 * K] + cross[3 * K:]

    def fold(x):
        x = x + pltpu.roll(x, 64, 1)
        return x + pltpu.roll(x, 32, 1)

    cross = fold(cross)
    quad = lane // K
    pack = cross[:8]
    for q in range(1, 4):
        pack = jnp.where(quad == q, cross[q * 8:(q + 1) * 8], pack)
    sub = lax.broadcasted_iota(jnp.int32, (8, 128), 0)
    norms = jnp.where(sub < 4, fold(jnp.broadcast_to(osq, (8, 128))), fold(jnp.broadcast_to(fsq, (8, 128))))
    snx[...] = jnp.concatenate([pack, norms], axis=0)
    scs = [
        send(snx, snr.at[i], {"neuron": npeer(dn), "frame": fpeer(df)})
        for i, (dn, df) in enumerate(others)
    ]
    for c in wcs:
        c.wait_recv()
    for z in range(NF):
        x = wfin[z]
        for a in range(GROUPS):
            wout_ref[a, z * NB:(z + 1) * NB] = x[a * NB:(a + 1) * NB]
    tot = snx[...]
    for i in range(len(others) - 1, -1, -1):
        scs[i].wait_recv()
        tot = tot + snr[i]
    own_row = tot[8:9]
    far_row = tot[12:13]
    rk = lax.broadcasted_iota(jnp.int32, (K, 128), 0)
    ck = lax.broadcasted_iota(jnp.int32, (K, 128), 1)
    own_col = jnp.sum(jnp.where(rk == ck, own_row, 0.0), axis=1, keepdims=True)
    full = jnp.concatenate(
        [tot[:8]] + [pltpu.roll(tot[:8], 128 - q * K, 1) for q in range(1, 4)], axis=0
    )
    sim = full / jnp.sqrt((own_col + EPS) * (far_row + EPS))
    sim_ref[...] = sim[:, :K]
    for c in pending:
        c.wait_send()


def wide_call(NN, NF, T, N):
    F = NF * T
    NB = N // NF
    KC = K // 2
    TC = T // 2
    EXT = T + RIM
    V = pltpu.VMEM
    D = pltpu.SemaphoreType.DMA
    vmem = pl.BlockSpec(memory_space=pltpu.VMEM)
    return pl.pallas_call(
        functools.partial(wide_kernel, NN, NF, T),
        out_shape=(
            jax.ShapeDtypeStruct((GROUPS, N, GW), F32),
            jax.ShapeDtypeStruct((K, T), F32),
            jax.ShapeDtypeStruct((K, K), F32),
        ),
        in_specs=[vmem] * 5,
        out_specs=(vmem,) * 3,
        scratch_shapes=[
            V((2, N + K, RIM), BF16),
            V((2, N + K, RIM), BF16),
            V((NF, 2 * NB, TC), BF16),
            V((NF, 2 * NB, TC), BF16),
            V((GROUPS * N, GW), BF16),
            V((GROUPS * K, GW), BF16),
            V((GW, EXT + RIM), BF16),
            V((GW, EXT), BF16),
            V((GW, EXT), BF16),
            V((2, NN, KC, TC), F32),
            V((2, NN - 1, KC, TC), F32),
            V((ITERS, K, F), BF16),
            V((GW, F), BF16),
            V((GW, F), BF16),
            V((GW, F), BF16),
            V((2 * GROUPS * NB, F), F32),
            V((NB, F), F32),
            V((2, KC, F), F32),
            V((2, K, F), F32),
            V((2, KC, F), F32),
            V((2, 2 * NF, KC, TC + 128), jnp.int16),
            V((2, 7, KC, TC + 128), jnp.int16),
            V((ITERS, 8, 128), F32),
            V((ITERS, 7, 8, 128), F32),
            V((KC, 128), F32),
            V((KC, 128), F32),
            V((NN, KC, TC), F32),
            V((8, 128), F32),
            V((NF, GROUPS * NB, GW), F32),
            V((GROUPS * NB, GW), BF16),
            V((GROUPS * NB, GW), BF16),
            V((16, 128), F32),
            V((NN * NF - 1, 16, 128), F32),
            D((112,)),
            D((112,)),
        ],
        compiler_params=pltpu.CompilerParams(
            collective_id=1, has_side_effects=True, vmem_limit_bytes=56 << 20
        ),
    )


def tall_call(NN, NF, T, N):
    gp = GROUPS // NF
    rg = K // 8
    w = T * rg // NN
    EXT = T + RIM
    V = pltpu.VMEM
    D = pltpu.SemaphoreType.DMA
    vmem = pl.BlockSpec(memory_space=pltpu.VMEM)
    return pl.pallas_call(
        functools.partial(kernel, NN, NF, T),
        out_shape=(
            jax.ShapeDtypeStruct((GROUPS, N, GW), F32),
            jax.ShapeDtypeStruct((K, T), F32),
            jax.ShapeDtypeStruct((K, K), F32),
        ),
        in_specs=[vmem] * 5,
        out_specs=(vmem,) * 3,
        scratch_shapes=[
            V((K, 2 * RIM + T + RIM), BF16),
            V((L * K, EXT), BF16),
            V((N, EXT), BF16),
            V((N, EXT + RIM), BF16),
            V((L * N, T), BF16),
            V((L * N, T), BF16),
            V((N, EXT), F32),
            V((K, T), F32),
            V((K, T), F32),
            V((K, T), F32),
            V((GROUPS, N, GW), BF16),
            V((GROUPS, K, GW), BF16),
            V((gp, N, GW), F32),
            V((2 * N, T), BF16),
            V((N, RIM), BF16),
            V((N, RIM), BF16),
            V((ITERS + 1, 2, K, RIM), F32),
            V((ITERS + 1, 2, K, RIM), F32),
            V((ITERS, 2, NN, 8, w), F32),
            V((ITERS, 2, NN - 1, 8, w), F32),
            V((ITERS, NN, 8, w), F32),
            V((ITERS, NF, K, 128), F32),
            V((ITERS, NF - 1, gp, 2 * N, GW), jnp.int16),
            V((ITERS, NF - 1, gp, 2 * N, GW), jnp.int16),
            V((ITERS, NF - 1, 2 * N // 4, 128), F32),
            V((ITERS, NF - 1, 2 * N // 4, 128), F32),
            V((ITERS - 1, GROUPS, N, GW), BF16),
            V((GROUPS, N, GW), F32),
            V((gp, N, GW), BF16),
            V((gp, N, GW), BF16),
            V((NN, K + 16, 128), F32),
            V((NF, K + 16, 128), F32),
            D((2,)),
            D((ITERS + 1, 2)),
            D((ITERS + 1, 2)),
            D((2 * ITERS, NN)),
            D((2 * ITERS, NN)),
            D((ITERS, NN)),
            D((ITERS, NN)),
            D((ITERS, NF)),
            D((ITERS, NF)),
            D((ITERS, NF)),
            D((ITERS, NF)),
            D((ITERS, NF)),
            D((ITERS, NF)),
            D((ITERS, NF)),
            D((ITERS, NF)),
            D((2,)),
            D((NN,)),
            D((NN,)),
            D((NF,)),
            D((NF,)),
        ],
        compiler_params=pltpu.CompilerParams(
            collective_id=0, has_side_effects=True, vmem_limit_bytes=50 << 20
        ),
    )


def per_device(calcium, trial_of_frame, trial_half, loadings, profiles):
    NN = lax.axis_size("neuron")
    NF = lax.axis_size("frame")
    N, T = calcium.shape
    w_groups = (
        loadings[0].reshape(N, K, GROUPS, GL).transpose(2, 0, 3, 1).reshape(GROUPS, N, GW)
    )
    if NN == 4 and NF == 4 and N == K:
        call = wide_call(NN, NF, T, N)
    else:
        call = tall_call(NN, NF, T, N)
    wout, hout, sim = call(calcium, trial_of_frame.reshape(1, T), trial_half.reshape(1, -1), w_groups, profiles[0])
    loads = wout.reshape(GROUPS, N, GL, K).transpose(1, 3, 0, 2).reshape(1, N, K * L)
    return loads, hout[None], sim[None]


def solution(mesh):
    placed = (
        P("neuron", "frame"),
        P("frame"),
        P(),
        P("half", "neuron", None),
        P("half", None, "frame"),
    )
    return jax.shard_map(
        per_device,
        mesh=mesh,
        in_specs=placed,
        out_specs=(P("half", "neuron", None), P("half", None, "frame"), P("half", None, None)),
        check_vma=False,
    )
```

```python
import functools

import jax
import jax.numpy as jnp
from jax import lax
from jax.experimental import pallas as pl
from jax.experimental.pallas import tpu as pltpu
from jax.sharding import PartitionSpec as P

K = 32
L = 64
ITERS = 2
EPS = 1e-06
RIM = 128
GROUPS = 8
GL = L // GROUPS
GW = GL * K
MESH = pl.DeviceIdType.MESH
F32 = jnp.float32
BF16 = jnp.bfloat16


def dot(a, b):
    return jnp.dot(a, b, preferred_element_type=F32)


def kernel(
    NN, NF, T,
    ca_ref, tof_ref, th_ref, w_ref, prof_ref,
    wout_ref, hout_ref, sim_ref,
    hs, hlag, mext, ms, mlag, alag, acc, accn, accd, hf, wg, wt, wown, stk,
    mrim_s, mrim_r, rim_s, rim_r, ndx, ndr, hall, ssr, wqx, wqr, wqs, wqt, wgb, wfin, pts, ptr, snr, sfr,
    mr_sem, rim_ss, rim_rs, nd_ss, nd_rs, hg_ss, hg_rs, ss_ss, ss_rs,
    ws_ss, ws_rs, wt_ss, wt_rs, wg_ss, wg_rs, pt_sem, sn_ss, sn_rs, sf_ss, sf_rs,
):
    me_n = lax.axis_index("neuron")
    me_f = lax.axis_index("frame")
    me_h = lax.axis_index("half")
    N = ca_ref.shape[0]
    EXT = T + RIM
    gp = GROUPS // NF
    rg = K // 8
    w = T * rg // NN
    pending = []

    def send(src, dst, ssem, rsem, axis, peer):
        c = pltpu.make_async_remote_copy(
            src_ref=src, dst_ref=dst, send_sem=ssem, recv_sem=rsem,
            device_id={axis: peer}, device_id_type=MESH,
        )
        c.start()
        pending.append(c)
        return c

    def npeer(r):
        return lax.rem(me_n + r, NN)

    def fpeer(r):
        return lax.rem(me_f + r, NF)

    barrier = pltpu.get_barrier_semaphore()
    for r in range(1, NN):
        pl.semaphore_signal(barrier, inc=1, device_id={"neuron": npeer(r)}, device_id_type=MESH)
    for r in range(1, NF):
        pl.semaphore_signal(barrier, inc=1, device_id={"frame": fpeer(r)}, device_id_type=MESH)
    pl.semaphore_signal(barrier, inc=1, device_id={"half": 1 - me_h}, device_id_type=MESH)

    trials = th_ref.shape[1]
    rows = lax.broadcasted_iota(jnp.int32, (trials, trials), 0)
    cols = lax.broadcasted_iota(jnp.int32, (trials, trials), 1)
    thf = th_ref[...].astype(F32)
    th_col = jnp.sum(jnp.where(rows == cols, thf, 0.0), axis=1, keepdims=True)
    chosen = jnp.where(th_col == me_h.astype(F32), 1.0, 0.0)
    hit = lax.broadcasted_iota(jnp.int32, (trials, T), 0) == tof_ref[...]
    mask = jnp.sum(jnp.where(hit, chosen, 0.0), axis=0, keepdims=True)
    masked = (ca_ref[...].astype(F32) * mask).astype(BF16)
    mext[:, :T] = masked
    mrim_s[...] = masked[:, :RIM]
    hf[...] = prof_ref[...]
    rim_s[0, 0] = prof_ref[:, :RIM]
    rim_s[0, 1] = prof_ref[:, T - RIM:]

    pl.semaphore_wait(barrier, (NN - 1) + (NF - 1) + 1)

    left = fpeer(NF - 1)
    right = fpeer(1)
    rims = {}

    def send_rims(i):
        rims[i] = (
            send(rim_s.at[i, 0], rim_r.at[i, 0], rim_ss.at[i, 0], rim_rs.at[i, 0], "frame", left),
            send(rim_s.at[i, 1], rim_r.at[i, 1], rim_ss.at[i, 1], rim_rs.at[i, 1], "frame", right),
        )

    send_rims(0)
    mcopy = send(mrim_s, mrim_r, mr_sem.at[0], mr_sem.at[1], "frame", left)

    for g in range(GROUPS):
        wg[g] = w_ref[g].astype(BF16)
    wown[...] = w_ref[pl.ds(me_f * gp, gp)]

    crow = (me_n % rg) * 8
    ccol = (me_n // rg) * w
    if NN == rg:
        hown = prof_ref[pl.ds(pl.multiple_of(crow, 8), 8), :]
    else:
        hown = prof_ref[pl.ds(pl.multiple_of(crow, 8), 8), pl.ds(pl.multiple_of(ccol, 128), w)]

    def own_rows(col):
        out = col[0:8]
        for q in range(1, rg):
            out = jnp.where(me_n % rg == q, col[q * 8:(q + 1) * 8], out)
        return out

    def build_right(width, lo=0, hi=GROUPS, extra=None):
        def body(g, _):
            v = hs[...]
            for b in range(GL):
                hlag[pl.ds(pl.multiple_of(g * GW + b * K, K), K), :width] = (
                    v[:, 2 * RIM - b:2 * RIM - b + width]
                )
            hs[:, RIM:] = v[:, RIM - GL:hs.shape[1] - GL]
            part = dot(wg[g], hlag[pl.ds(pl.multiple_of(g * GW, GW), GW), :width])
            acc[:, :width] = acc[:, :width] + part
            if extra is not None:
                extra(g)
            return 0

        if lo == 0:
            acc[...] = jnp.zeros_like(acc)
        lax.fori_loop(lo, hi, body, 0)

    def fill_hs(left_rim, body, right_rim):
        hs[:, :RIM] = jnp.zeros((K, RIM), BF16)
        hs[:, RIM:2 * RIM] = left_rim.astype(BF16)
        hs[:, 2 * RIM:2 * RIM + T] = body.astype(BF16)
        hs[:, 2 * RIM + T:] = right_rim.astype(BF16)

    def build_left(dst, g):
        v = ms[...]
        for b in range(GL):
            dst[pl.ds(pl.multiple_of(g * GW + b * N, N), N), :] = v[:, b:b + T]
        ms[:, :EXT] = v[:, GL:EXT + GL]

    mcopy.wait_recv()
    mext[:, T:] = mrim_r[...]
    ms[:, :EXT] = mext[...]
    ms[:, EXT:] = jnp.zeros((N, RIM), BF16)

    def mbody(g, _):
        build_left(mlag, g)
        return 0

    lax.fori_loop(0, GROUPS, mbody, 0)
    stk[:N] = mext[:, :T]
    mask_ext = jnp.where(mext[...].astype(F32) > 0.0, 1.0, 0.0)

    def send_sums(it, kind, src):
        for p in range(NN):
            a, b = (p % rg) * 8, (p // rg) * w
            ndx[it, kind, p] = src[a:a + 8, b:b + w]
        at = 2 * it + kind
        return [
            send(ndx.at[it, kind, npeer(r)], ndr.at[it, kind, r - 1], nd_ss.at[at, r], nd_rs.at[at, r],
                 "neuron", npeer(r))
            for r in range(1, NN)
        ]

    RQ = 2 * N // 4
    quad = lax.broadcasted_iota(jnp.int32, (RQ, 128), 1) // K
    wcs = {}

    def contract(rows_bf, g):
        rws = pl.ds(pl.multiple_of(g * GW, GW), GW)
        return lax.dot_general(
            rows_bf, hlag[rws, :T], (((1,), (1,)), ((), ())), preferred_element_type=F32
        )

    scale = None
    for it in range(ITERS):
        last = it == ITERS - 1
        def tbody(g, _):
            x = wg[g].astype(F32)
            for h in range(GW // 128):
                t = x[:, h * 128:(h + 1) * 128].T
                wt[g, :, h * 128:(h + 1) * 128] = jnp.concatenate(
                    [t[q * K:(q + 1) * K] for q in range(4)], axis=1
                ).astype(BF16)
            return 0

        lax.fori_loop(0, GROUPS, tbody, 0)

        accn[...] = jnp.zeros_like(accn)

        def nbody(g, _):
            accn[...] = accn[...] + dot(wt[g], mlag[pl.ds(pl.multiple_of(g * GW, GW), GW), :])
            return 0

        lax.fori_loop(0, GROUPS, nbody, 0)
        ncs = send_sums(it, 0, accn)
        if it == 0:
            for c in rims[it]:
                c.wait_recv()
            fill_hs(rim_r[it, 1], hf[...], rim_r[it, 0])
        else:
            rims[it][0].wait_recv()
            fill_hs(rim_r[it, 1] / scale, hf[...] / scale, rim_r[it, 0] / scale)
        build_right(EXT)
        approx = (acc[...].astype(BF16).astype(F32) * mask_ext).astype(BF16)
        ms[:, :EXT] = approx

        accd[...] = jnp.zeros_like(accd)

        def dbody(g, _):
            build_left(alag, g)
            rws = pl.ds(pl.multiple_of(g * GW, GW), GW)
            accd[...] = accd[...] + dot(wt[g], alag[rws, :])
            return 0

        lax.fori_loop(0, GROUPS, dbody, 0)
        dcs = send_sums(it, 1, accd)
        num = ndx[it, 0, me_n]
        den = ndx[it, 1, me_n]
        for r in range(1, NN):
            ncs[r - 1].wait_recv()
            num = num + ndr[it, 0, r - 1]
        for r in range(1, NN):
            dcs[r - 1].wait_recv()
            den = den + ndr[it, 1, r - 1]
        hown = hown * num / jnp.maximum(den, 1.0)
        hall[it, me_n] = hown
        cs = [
            send(hall.at[it, me_n], hall.at[it, me_n], hg_ss.at[it, r], hg_rs.at[it, r], "neuron", npeer(r))
            for r in range(1, NN)
        ]
        for c in cs:
            c.wait_recv()
        for p in range(NN):
            a, b = (p % rg) * 8, (p // rg) * w
            hf[a:a + 8, b:b + w] = hall[it, p]
        hnew = hf[...]
        rim_s[it + 1, 0] = hnew[:, :RIM]
        rim_s[it + 1, 1] = hnew[:, T - RIM:]
        send_rims(it + 1)
        sq = jnp.sum(hnew * hnew, axis=1, keepdims=True)
        ssr[it, me_f] = jnp.broadcast_to(sq, (K, 128))
        ssc = [
            send(ssr.at[it, me_f], ssr.at[it, me_f], ss_ss.at[it, r], ss_rs.at[it, r], "frame", fpeer(r))
            for r in range(1, NF)
        ]
        rims[it + 1][1].wait_recv()
        fill_hs(rim_r[it + 1, 1], hnew, hnew[:, :RIM])
        build_right(T)
        approx2 = (acc[:, :T].astype(BF16).astype(F32) * mask_ext[:, :T]).astype(BF16)
        stk[N:] = approx2
        for r in list(range(1, NF)) + [0]:
            p = fpeer(r)
            sums = [contract(stk[...], p * gp + q) for q in range(gp)]
            if r:
                top = sums[0][:, :128]
                for x in sums:
                    for h in range(GW // 128):
                        top = jnp.maximum(top, x[:, h * 128:(h + 1) * 128])
                top = jnp.maximum(top, pltpu.roll(top, 64, 1))
                top = jnp.maximum(top, pltpu.roll(top, 32, 1))
                inv = 65534.0 / jnp.maximum(top, 1e-30)
                inv = jnp.concatenate([inv] * (GW // 128), axis=1)
                for q in range(gp):
                    code = jnp.minimum(jnp.round(sums[q] * inv) - 32767.0, 32767.0)
                    wqx[it, r - 1, q] = code.astype(jnp.int32).astype(jnp.int16)
                packed = top[:RQ]
                for j in range(1, 4):
                    packed = jnp.where(quad == j, top[j * RQ:(j + 1) * RQ], packed)
                wqs[it, r - 1] = packed
                wcs[r - 1] = (
                    send(wqs.at[it, r - 1], wqt.at[it, r - 1], wt_ss.at[it, r], wt_rs.at[it, r], "frame", p),
                    send(wqx.at[it, r - 1], wqr.at[it, r - 1], ws_ss.at[it, r], ws_rs.at[it, r], "frame", p),
                )
            else:
                wtot = sums
        for c in ssc:
            c.wait_recv()
        total = ssr[it, 0]
        for p in range(1, NF):
            total = total + ssr[it, p]
        scale_wide = jnp.sqrt(total + EPS)
        scale = scale_wide[:, 0:1]
        ek = lax.broadcasted_iota(jnp.int32, (K, GW), 0)
        ec = lax.broadcasted_iota(jnp.int32, (K, GW), 1) % K
        scale_row = jnp.sum(jnp.where(ek == ec, scale, 0.0), axis=0, keepdims=True)
        hown = hown / own_rows(scale)
        for r in range(1, NF):
            for c in wcs[r - 1]:
                c.wait_recv()
            packed = wqt[it, r - 1]
            tops = []
            for j in range(4):
                t = jnp.where(quad == j, packed, 0.0)
                t = t + pltpu.roll(t, 64, 1)
                tops.append(t + pltpu.roll(t, 32, 1))
            unit = jnp.concatenate(tops, axis=0) * (1.0 / 65534.0)
            unit = jnp.concatenate([unit] * (GW // 128), axis=1)
            wtot = [
                wtot[q] + (wqr[it, r - 1, q].astype(jnp.int32).astype(F32) + 32767.0) * unit
                for q in range(gp)
            ]
        wnew = jnp.stack([wown[q] * wtot[q][:N] / wtot[q][N:] * scale_row for q in range(gp)])
        wown[...] = wnew
        mine = pl.ds(me_f * gp, gp)
        if not last:
            wgb[it, mine] = wnew.astype(BF16)
            cs = [
                send(wgb.at[it, mine], wgb.at[it, mine], wg_ss.at[it, r], wg_rs.at[it, r], "frame", fpeer(r))
                for r in range(1, NF)
            ]
            for c in cs:
                c.wait_recv()
            wg[...] = wgb[it]

    pts[...] = wnew.astype(BF16)
    ptc = send(pts, ptr, pt_sem.at[0], pt_sem.at[1], "half", 1 - me_h)
    wfin[mine] = wnew
    fcs = [
        send(wfin.at[mine], wfin.at[mine], wg_ss.at[ITERS - 1, r], wg_rs.at[ITERS - 1, r], "frame", fpeer(r))
        for r in range(1, NF)
    ]
    hout_ref[...] = hf[...] / scale
    ptc.wait_recv()
    far = ptr[...].astype(F32)
    cross = jnp.zeros((128, 128), F32)
    osq = jnp.zeros((1, 128), F32)
    fsq = jnp.zeros((1, 128), F32)
    for q in range(gp):
        for h in range(GW // 128):
            a = wnew[q, :, h * 128:(h + 1) * 128]
            b = far[q, :, h * 128:(h + 1) * 128]
            cross = cross + lax.dot_general(
                a, b, (((0,), (0,)), ((), ())),
                preferred_element_type=F32, precision=lax.Precision.HIGHEST,
            )
            osq = osq + jnp.sum(a * a, axis=0, keepdims=True)
            fsq = fsq + jnp.sum(b * b, axis=0, keepdims=True)
    ri = lax.broadcasted_iota(jnp.int32, (128, 128), 0)
    ci = lax.broadcasted_iota(jnp.int32, (128, 128), 1)
    cross = jnp.where(ri // K == ci // K, cross, 0.0)
    cross = cross[0:K] + cross[K:2 * K] + cross[2 * K:3 * K] + cross[3 * K:]

    def fold(x):
        x = x + pltpu.roll(x, 64, 1)
        return x + pltpu.roll(x, 32, 1)

    pack = jnp.concatenate(
        [cross, jnp.broadcast_to(osq, (8, 128)), jnp.broadcast_to(fsq, (8, 128))], axis=0
    )
    snr[me_n] = fold(pack)
    cs = [
        send(snr.at[me_n], snr.at[me_n], sn_ss.at[r], sn_rs.at[r], "neuron", npeer(r))
        for r in range(1, NN)
    ]
    for c in cs:
        c.wait_recv()
    tot = snr[0]
    for p in range(1, NN):
        tot = tot + snr[p]
    sfr[me_f] = tot
    cs = [
        send(sfr.at[me_f], sfr.at[me_f], sf_ss.at[r], sf_rs.at[r], "frame", fpeer(r))
        for r in range(1, NF)
    ]
    for c in fcs:
        c.wait_recv()
    wout_ref[...] = wfin[...]
    for c in cs:
        c.wait_recv()
    tot = sfr[0]
    for p in range(1, NF):
        tot = tot + sfr[p]
    own_row = tot[K:K + 1]
    far_row = tot[K + 8:K + 9]
    rk = lax.broadcasted_iota(jnp.int32, (K, 128), 0)
    ck = lax.broadcasted_iota(jnp.int32, (K, 128), 1)
    own_col = jnp.sum(jnp.where(rk == ck, own_row, 0.0), axis=1, keepdims=True)
    sim = tot[:K] / jnp.sqrt((own_col + EPS) * (far_row + EPS))
    sim_ref[...] = sim[:, :K]
    rims[ITERS][0].wait_recv()
    for c in pending:
        c.wait_send()


def roll_right(x, s):
    return pltpu.roll(x, s, 1) if s else x


def roll_left(x, s):
    return pltpu.roll(x, x.shape[1] - s, 1) if s else x


def wide_kernel(
    NN, NF, T,
    ca_hbm, tof_hbm, th_hbm, w_hbm, prof_hbm,
    wout_ref, hout_ref, sim_ref,
    ca_ref, tof_ref, th_ref, w_ref, prof_ref, by_lag, wf,
    rim_s, rim_r, mtx, mrx, w32, wt32, hla, mla, ala,
    ndx, ndr, hb, hl, ml, al, dat, md, prx, acc, own, tx, rx,
    hg, wfin, far_s, far_r, snx, snr,
    isem, ssem, rsem,
):
    me_n = lax.axis_index("neuron")
    me_f = lax.axis_index("frame")
    me_h = lax.axis_index("half")
    me_c = lax.rem(me_n, 2)
    me_y = me_n // 2
    N = ca_ref.shape[0]
    F = NF * T
    NB = N // NF
    KC = K // 2
    TC = T // 2
    EXT = T + RIM
    pending = []

    def send(src, dst, peer):
        i = len(pending)
        c = pltpu.make_async_remote_copy(
            src_ref=src, dst_ref=dst, send_sem=ssem.at[i], recv_sem=rsem.at[i],
            device_id=peer, device_id_type=MESH,
        )
        c.start()
        pending.append(c)
        return c

    def npeer(r):
        return lax.rem(me_n + r, NN)

    def fpeer(r):
        return lax.rem(me_f + r, NF)

    core = {"neuron": me_n + 1 - 2 * me_c}
    seven = [(dy, dz) for dz in (3, 2, 1, 0) for dy in (1, 0) if dy or dz]

    def block_of(dy, dz):
        return fpeer(dz) * 2 + lax.rem(me_y + dy, 2)

    def to(dy, dz):
        return {"neuron": npeer(2 * dy), "frame": fpeer(dz)}

    others = [(dn, df) for df in (3, 2, 1, 0) for dn in (3, 2, 1, 0) if dn or df]
    barrier = pltpu.get_barrier_semaphore()
    for dn, df in others:
        pl.semaphore_signal(
            barrier, inc=1, device_id={"neuron": npeer(dn), "frame": fpeer(df)}, device_id_type=MESH
        )
    pl.semaphore_signal(barrier, inc=1, device_id={"half": 1 - me_h}, device_id_type=MESH)

    loads = [
        pltpu.make_async_copy(a, b, isem.at[i])
        for i, (a, b) in enumerate([
            (w_hbm, w_ref), (th_hbm, th_ref), (tof_hbm, tof_ref), (ca_hbm, ca_ref), (prof_hbm, prof_ref),
        ])
    ]
    for c in loads:
        c.start()

    def turn(x):
        out = []
        for h in range(GW // 128):
            t = x[:, h * 128:(h + 1) * 128].T
            out.append(jnp.concatenate([t[q * K:(q + 1) * K] for q in range(4)], axis=1))
        return jnp.concatenate(out, axis=1)

    loads[0].wait()
    for j in range(K * L // 128):
        by_lag[j * 128:(j + 1) * 128, :N] = w_ref[:, j * 128:(j + 1) * 128].T
    for a in range(GROUPS):
        x = jnp.concatenate(
            [by_lag[pl.ds(a * GL + b, K, stride=L), :][:, :N] for b in range(GL)], axis=1
        )
        wt32[a * K:(a + 1) * K] = x.astype(BF16)
        x = turn(x)
        wf[a] = x
        w32[a * N:(a + 1) * N] = x.astype(BF16)
    mine = pl.ds(pl.multiple_of(me_f * NB, NB), NB)
    w8 = jnp.concatenate([wf[a, mine, :] for a in range(GROUPS)], axis=0)
    for c in loads[1:]:
        c.wait()

    trials = th_ref.shape[1]
    rows = lax.broadcasted_iota(jnp.int32, (trials, trials), 0)
    cols = lax.broadcasted_iota(jnp.int32, (trials, trials), 1)
    thf = th_ref[...].astype(F32)
    th_col = jnp.sum(jnp.where(rows == cols, thf, 0.0), axis=1, keepdims=True)
    chosen = jnp.where(th_col == me_h.astype(F32), 1.0, 0.0)
    hit = lax.broadcasted_iota(jnp.int32, (trials, T), 0) == tof_ref[...]
    mask = jnp.sum(jnp.where(hit, chosen, 0.0), axis=0, keepdims=True)
    masked = ca_ref[...].astype(F32) * mask
    body = masked.astype(BF16)
    prof = prof_ref[...].astype(BF16)
    rim_s[0, :N] = body[:, :RIM]
    rim_s[0, N:] = prof[:, :RIM]
    rim_s[1, :K] = prof[:, T - RIM:]
    for z in range(NF):
        x = masked[z * NB:(z + 1) * NB]
        mtx[z] = jnp.concatenate([x[:, :TC], x[:, TC:]], axis=0).astype(BF16)

    pl.semaphore_wait(barrier, len(others) + 1)

    to_left = send(rim_s.at[0], rim_r.at[0], {"frame": fpeer(NF - 1)})
    to_right = send(rim_s.at[1, pl.ds(0, K)], rim_r.at[1, pl.ds(0, K)], {"frame": fpeer(1)})
    mcs = [
        send(mtx.at[fpeer(r)], mrx.at[me_f], {"frame": fpeer(r)})
        for r in (3, 2, 1)
    ]
    mrx[me_f] = mtx[me_f]

    to_left.wait_recv()
    mext = jnp.concatenate([body, rim_r[0, :N]], axis=1)
    mask_ext = jnp.where(mext.astype(F32) > 0.0, 1.0, 0.0)

    def lags(dst, x, roll):
        n = x.shape[0]
        for b in range(GL):
            dst[b * n:(b + 1) * n] = roll(x, b)

    def numer_of(m):
        q = dot(wt32[...], m[...])
        s = q[:K]
        for a in range(1, GROUPS):
            s = s + roll_left(q[a * K:(a + 1) * K], a * GL)
        return s[:, :T]

    def scatter(kind, s):
        for p in range(NN):
            a, b = (p % 2) * KC, (p // 2) * TC
            ndx[kind, p] = s[a:a + KC, b:b + TC]
        return [
            send(ndx.at[kind, npeer(r)], ndr.at[kind, r - 1], {"neuron": npeer(r)})
            for r in range(1, NN)
        ]

    lags(mla, mext, roll_left)
    ncs = scatter(0, numer_of(mla))
    to_right.wait_recv()
    lags(hla, jnp.concatenate([rim_r[1, :K], prof, rim_r[0, N:]], axis=1), roll_right)
    p = dot(w32[...], hla[...])
    s = p[:N]
    for a in range(1, GROUPS):
        s = s + roll_right(p[a * N:(a + 1) * N], a * GL)
    approx = (s[:, RIM:].astype(BF16).astype(F32) * mask_ext).astype(BF16)
    lags(ala, approx, roll_left)
    dcs = scatter(1, numer_of(ala))

    own_rows = pl.ds(pl.multiple_of(me_c * KC, KC), KC)
    far_rows = pl.ds(pl.multiple_of((1 - me_c) * KC, KC), KC)
    hown = prof_ref[own_rows, pl.ds(pl.multiple_of(me_y * TC, TC), TC)]
    num = ndx[0, me_n]
    den = ndx[1, me_n]
    for r in range(1, NN):
        ncs[r - 1].wait_recv()
        num = num + ndr[0, r - 1]
    for r in range(1, NN):
        dcs[r - 1].wait_recv()
        den = den + ndr[1, r - 1]
    hown = hown * num / jnp.maximum(den, 1.0)

    def spot(c, blk):
        return pl.ds(pl.multiple_of(c * KC, KC), KC), pl.ds(pl.multiple_of(blk * TC, TC), TC)

    lane = lax.broadcasted_iota(jnp.int32, (8, 128), 1)

    def gather_h(it):
        a, b = spot(me_c, block_of(0, 0))
        hb[it, a, b] = hown.astype(BF16)
        cs = [send(hb.at[it, a, b], hb.at[it, a, b], to(dy, dz)) for dy, dz in seven]
        relays = [send(hb.at[it, a, b], hb.at[it, a, b], core)]
        return cs, relays

    def relay_h(it, cs, relays):
        for i in range(len(seven) - 1, -1, -1):
            cs[i].wait_recv()
            dy, dz = seven[i]
            a, b = spot(me_c, block_of(dy, NF - dz))
            relays.append(send(hb.at[it, a, b], hb.at[it, a, b], core))
        for c in relays:
            c.wait_recv()

    def squares(it):
        x = hb[it].astype(F32)
        return jnp.sum(x * x, axis=1, keepdims=True)

    cs, relays = gather_h(0)

    for c in mcs:
        c.wait_recv()
    for z in range(NF):
        x = mrx[z].astype(F32)
        md[:, z * T:z * T + TC] = x[:NB]
        md[:, z * T + TC:(z + 1) * T] = x[NB:]
    data = md[...]
    mask_all = jnp.where(data[0:1] > 0.0, 1.0, 0.0)
    rolled = [roll_left(data, a * GL) for a in range(GROUPS)]
    for a in range(GROUPS):
        dat[a * 2 * NB:a * 2 * NB + NB] = rolled[a]
    lags(ml, jnp.concatenate(rolled[:4], axis=0).astype(BF16), roll_left)

    def recon(wb):
        p = dot(wb, hl[...])
        s = p[:NB]
        for a in range(1, GROUPS):
            s = s + roll_right(p[a * NB:(a + 1) * NB], a * GL)
        return s.astype(BF16).astype(F32) * mask_all

    def corr(wt, m):
        q = dot(wt, m[...])
        return q[:K] + roll_left(q[K:], 4 * GL)

    def template_ratio():
        approx = recon(w8.astype(BF16))
        for a in range(GROUPS):
            dat[a * 2 * NB + NB:(a + 1) * 2 * NB] = roll_left(approx, a * GL)
        s = lax.dot_general(
            dat[...].astype(BF16), hl[...], (((1,), (1,)), ((), ())), preferred_element_type=F32
        )
        wnum = jnp.concatenate([s[a * 2 * NB:a * 2 * NB + NB] for a in range(GROUPS)], axis=0)
        wden = jnp.concatenate([s[a * 2 * NB + NB:(a + 1) * 2 * NB] for a in range(GROUPS)], axis=0)
        return wnum, wden

    relay_h(0, cs, relays)
    lags(hl, hb[0], roll_right)
    wnum, wden = template_ratio()
    w8 = w8 * wnum / wden

    wt = jnp.concatenate([turn(w8[:4 * NB]), turn(w8[4 * NB:])], axis=0).astype(BF16)

    def reduce_start(kind, s):
        acc[kind] = s
        return send(acc.at[kind, far_rows], prx.at[kind], core)

    def reduce_spread(kind, c):
        c.wait_recv()
        s = acc[kind, own_rows, :] + prx[kind]
        own[kind] = s
        top = jnp.max(s, axis=1, keepdims=True)
        e = jnp.ceil(jnp.log2(jnp.maximum(top, 1e-30)) + 0.01)
        code = jnp.minimum(jnp.round(s * jnp.exp2(16.0 - e)) - 32767.0, 32767.0)
        code = code.astype(jnp.int32).astype(jnp.int16)
        ee = jnp.broadcast_to(e, (KC, 128)).astype(jnp.int32).astype(jnp.int16)
        for blk in range(2 * NF):
            tx[kind, blk, :, :TC] = code[:, blk * TC:(blk + 1) * TC]
            tx[kind, blk, :, TC:] = ee
        return [
            send(tx.at[kind, block_of(dy, dz)], rx.at[kind, i], to(dy, dz))
            for i, (dy, dz) in enumerate(seven)
        ]

    def reduce_done(kind, cs):
        t = own[kind, :, pl.ds(pl.multiple_of(block_of(0, 0) * TC, TC), TC)]
        for i in range(len(seven) - 1, -1, -1):
            cs[i].wait_recv()
            e = rx[kind, i, :, TC:].astype(jnp.int32).astype(F32)
            unit = jnp.concatenate([jnp.exp2(e - 16.0)] * (TC // 128), axis=1)
            t = t + (rx[kind, i, :, :TC].astype(jnp.int32).astype(F32) + 32767.0) * unit
        return t

    nc = reduce_start(0, corr(wt, ml))
    approx = recon(w8.astype(BF16))
    ncs = reduce_spread(0, nc)
    lags(al, jnp.concatenate([roll_left(approx, a * GL) for a in range(4)], axis=0).astype(BF16), roll_left)
    dc = reduce_start(1, corr(wt, al))
    scale0 = jnp.sqrt(squares(0) + EPS)
    dcs = reduce_spread(1, dc)
    num = reduce_done(0, ncs)
    den = reduce_done(1, dcs)
    s0 = jnp.where(me_c == 0, scale0[:KC], scale0[KC:])
    hown = hown * (num * s0) / jnp.maximum(den * s0, 1.0)
    cs, relays = gather_h(1)
    hg[me_n] = hown
    hcs = [send(hg.at[me_n], hg.at[me_n], {"neuron": npeer(r)}) for r in (3, 2, 1)]
    relay_h(1, cs, relays)
    lags(hl, hb[1], roll_right)
    wnum, wden = template_ratio()
    scale = jnp.sqrt(squares(1) + EPS * scale0 * scale0)
    ek = lax.broadcasted_iota(jnp.int32, (K, GW), 0)
    ec = lax.broadcasted_iota(jnp.int32, (K, GW), 1) % K
    scale_row = jnp.sum(jnp.where(ek == ec, scale, 0.0), axis=0, keepdims=True)
    w8 = w8 * wnum / wden * scale_row

    far_s[...] = w8.astype(BF16)
    fc = send(far_s, far_r, {"half": 1 - me_h})
    wfin[me_f] = w8
    wcs = [send(wfin.at[me_f], wfin.at[me_f], {"frame": fpeer(r)}) for r in (3, 2, 1)]
    for c in hcs:
        c.wait_recv()
    for p in range(NN):
        a, b = (p % 2) * KC, (p // 2) * TC
        hout_ref[a:a + KC, b:b + TC] = hg[p] / scale[a:a + KC]
    fc.wait_recv()
    far = far_r[...].astype(F32)
    cross = jnp.zeros((128, 128), F32)
    osq = jnp.zeros((1, 128), F32)
    fsq = jnp.zeros((1, 128), F32)
    for h in range(GW // 128):
        a = w8[:, h * 128:(h + 1) * 128]
        b = far[:, h * 128:(h + 1) * 128]
        cross = cross + lax.dot_general(
            a, b, (((0,), (0,)), ((), ())),
            preferred_element_type=F32, precision=lax.Precision.HIGHEST,
        )
        osq = osq + jnp.sum(a * a, axis=0, keepdims=True)
        fsq = fsq + jnp.sum(b * b, axis=0, keepdims=True)
    ri = lax.broadcasted_iota(jnp.int32, (128, 128), 0)
    ci = lax.broadcasted_iota(jnp.int32, (128, 128), 1)
    cross = jnp.where(ri // K == ci // K, cross, 0.0)
    cross = cross[0:K] + cross[K:2 * K] + cross[2 * K:3 * K] + cross[3 * K:]

    def fold(x):
        x = x + pltpu.roll(x, 64, 1)
        return x + pltpu.roll(x, 32, 1)

    cross = fold(cross)
    quad = lane // K
    pack = cross[:8]
    for q in range(1, 4):
        pack = jnp.where(quad == q, cross[q * 8:(q + 1) * 8], pack)
    sub = lax.broadcasted_iota(jnp.int32, (8, 128), 0)
    norms = jnp.where(sub < 4, fold(jnp.broadcast_to(osq, (8, 128))), fold(jnp.broadcast_to(fsq, (8, 128))))
    snx[...] = jnp.concatenate([pack, norms], axis=0)
    scs = [
        send(snx, snr.at[i], {"neuron": npeer(dn), "frame": fpeer(df)})
        for i, (dn, df) in enumerate(others)
    ]
    for c in wcs:
        c.wait_recv()
    for z in range(NF):
        x = wfin[z]
        for a in range(GROUPS):
            wout_ref[a, z * NB:(z + 1) * NB] = x[a * NB:(a + 1) * NB]
    tot = snx[...]
    for i in range(len(others) - 1, -1, -1):
        scs[i].wait_recv()
        tot = tot + snr[i]
    own_row = tot[8:9]
    far_row = tot[12:13]
    rk = lax.broadcasted_iota(jnp.int32, (K, 128), 0)
    ck = lax.broadcasted_iota(jnp.int32, (K, 128), 1)
    own_col = jnp.sum(jnp.where(rk == ck, own_row, 0.0), axis=1, keepdims=True)
    full = jnp.concatenate(
        [tot[:8]] + [pltpu.roll(tot[:8], 128 - q * K, 1) for q in range(1, 4)], axis=0
    )
    sim = full / jnp.sqrt((own_col + EPS) * (far_row + EPS))
    sim_ref[...] = sim[:, :K]
    for c in pending:
        c.wait_send()


def wide_call(NN, NF, T, N, trials):
    F = NF * T
    NB = N // NF
    KC = K // 2
    TC = T // 2
    EXT = T + RIM
    V = pltpu.VMEM
    D = pltpu.SemaphoreType.DMA
    vmem = pl.BlockSpec(memory_space=pltpu.VMEM)
    return pl.pallas_call(
        functools.partial(wide_kernel, NN, NF, T),
        out_shape=(
            jax.ShapeDtypeStruct((GROUPS, N, GW), F32),
            jax.ShapeDtypeStruct((K, T), F32),
            jax.ShapeDtypeStruct((K, K), F32),
        ),
        in_specs=[pl.BlockSpec(memory_space=pl.ANY)] * 5,
        out_specs=(vmem,) * 3,
        scratch_shapes=[
            V((N, T), BF16),
            V((1, T), jnp.int32),
            V((1, trials), jnp.int32),
            V((N, K * L), F32),
            V((K, T), F32),
            V((K * L, 128), F32),
            V((GROUPS, N, GW), F32),
            V((2, N + K, RIM), BF16),
            V((2, N + K, RIM), BF16),
            V((NF, 2 * NB, TC), BF16),
            V((NF, 2 * NB, TC), BF16),
            V((GROUPS * N, GW), BF16),
            V((GROUPS * K, GW), BF16),
            V((GW, EXT + RIM), BF16),
            V((GW, EXT), BF16),
            V((GW, EXT), BF16),
            V((2, NN, KC, TC), F32),
            V((2, NN - 1, KC, TC), F32),
            V((ITERS, K, F), BF16),
            V((GW, F), BF16),
            V((GW, F), BF16),
            V((GW, F), BF16),
            V((2 * GROUPS * NB, F), F32),
            V((NB, F), F32),
            V((2, KC, F), F32),
            V((2, K, F), F32),
            V((2, KC, F), F32),
            V((2, 2 * NF, KC, TC + 128), jnp.int16),
            V((2, 7, KC, TC + 128), jnp.int16),
            V((NN, KC, TC), F32),
            V((NF, GROUPS * NB, GW), F32),
            V((GROUPS * NB, GW), BF16),
            V((GROUPS * NB, GW), BF16),
            V((16, 128), F32),
            V((NN * NF - 1, 16, 128), F32),
            D((5,)),
            D((80,)),
            D((80,)),
        ],
        compiler_params=pltpu.CompilerParams(
            collective_id=1, has_side_effects=True, vmem_limit_bytes=56 << 20
        ),
    )


def tall_call(NN, NF, T, N):
    gp = GROUPS // NF
    rg = K // 8
    w = T * rg // NN
    EXT = T + RIM
    V = pltpu.VMEM
    D = pltpu.SemaphoreType.DMA
    vmem = pl.BlockSpec(memory_space=pltpu.VMEM)
    return pl.pallas_call(
        functools.partial(kernel, NN, NF, T),
        out_shape=(
            jax.ShapeDtypeStruct((GROUPS, N, GW), F32),
            jax.ShapeDtypeStruct((K, T), F32),
            jax.ShapeDtypeStruct((K, K), F32),
        ),
        in_specs=[vmem] * 5,
        out_specs=(vmem,) * 3,
        scratch_shapes=[
            V((K, 2 * RIM + T + RIM), BF16),
            V((L * K, EXT), BF16),
            V((N, EXT), BF16),
            V((N, EXT + RIM), BF16),
            V((L * N, T), BF16),
            V((L * N, T), BF16),
            V((N, EXT), F32),
            V((K, T), F32),
            V((K, T), F32),
            V((K, T), F32),
            V((GROUPS, N, GW), BF16),
            V((GROUPS, K, GW), BF16),
            V((gp, N, GW), F32),
            V((2 * N, T), BF16),
            V((N, RIM), BF16),
            V((N, RIM), BF16),
            V((ITERS + 1, 2, K, RIM), F32),
            V((ITERS + 1, 2, K, RIM), F32),
            V((ITERS, 2, NN, 8, w), F32),
            V((ITERS, 2, NN - 1, 8, w), F32),
            V((ITERS, NN, 8, w), F32),
            V((ITERS, NF, K, 128), F32),
            V((ITERS, NF - 1, gp, 2 * N, GW), jnp.int16),
            V((ITERS, NF - 1, gp, 2 * N, GW), jnp.int16),
            V((ITERS, NF - 1, 2 * N // 4, 128), F32),
            V((ITERS, NF - 1, 2 * N // 4, 128), F32),
            V((ITERS - 1, GROUPS, N, GW), BF16),
            V((GROUPS, N, GW), F32),
            V((gp, N, GW), BF16),
            V((gp, N, GW), BF16),
            V((NN, K + 16, 128), F32),
            V((NF, K + 16, 128), F32),
            D((2,)),
            D((ITERS + 1, 2)),
            D((ITERS + 1, 2)),
            D((2 * ITERS, NN)),
            D((2 * ITERS, NN)),
            D((ITERS, NN)),
            D((ITERS, NN)),
            D((ITERS, NF)),
            D((ITERS, NF)),
            D((ITERS, NF)),
            D((ITERS, NF)),
            D((ITERS, NF)),
            D((ITERS, NF)),
            D((ITERS, NF)),
            D((ITERS, NF)),
            D((2,)),
            D((NN,)),
            D((NN,)),
            D((NF,)),
            D((NF,)),
        ],
        compiler_params=pltpu.CompilerParams(
            collective_id=0, has_side_effects=True, vmem_limit_bytes=50 << 20
        ),
    )


def per_device(calcium, trial_of_frame, trial_half, loadings, profiles):
    NN = lax.axis_size("neuron")
    NF = lax.axis_size("frame")
    N, T = calcium.shape
    small = (calcium, trial_of_frame.reshape(1, T), trial_half.reshape(1, -1))
    if NN == 4 and NF == 4 and N == K:
        call = wide_call(NN, NF, T, N, trial_half.shape[0])
        wout, hout, sim = call(*small, loadings[0], profiles[0])
    else:
        w_groups = loadings[0].reshape(N, K, GROUPS, GL).transpose(2, 0, 3, 1).reshape(GROUPS, N, GW)
        wout, hout, sim = tall_call(NN, NF, T, N)(*small, w_groups, profiles[0])
    loads = wout.reshape(GROUPS, N, GL, K).transpose(1, 3, 0, 2).reshape(1, N, K * L)
    return loads, hout[None], sim[None]


def solution(mesh):
    placed = (
        P("neuron", "frame"),
        P("frame"),
        P(),
        P("half", "neuron", None),
        P("half", None, "frame"),
    )
    return jax.shard_map(
        per_device,
        mesh=mesh,
        in_specs=placed,
        out_specs=(P("half", "neuron", None), P("half", None, "frame"), P("half", None, None)),
        check_vma=False,
    )
```

```python
import functools

import jax
import jax.numpy as jnp
from jax import lax
from jax.experimental import pallas as pl
from jax.experimental.pallas import tpu as pltpu
from jax.sharding import PartitionSpec as P

K = 32
L = 64
ITERS = 2
EPS = 1e-06
RIM = 128
GROUPS = 8
GL = L // GROUPS
GW = GL * K
MESH = pl.DeviceIdType.MESH
F32 = jnp.float32
BF16 = jnp.bfloat16


def dot(a, b):
    return jnp.dot(a, b, preferred_element_type=F32)


def kernel(
    NN, NF, T,
    ca_ref, tof_ref, th_ref, w_ref, prof_ref,
    wout_ref, hout_ref, sim_ref,
    hs, hlag, mext, ms, mlag, alag, acc, accn, accd, hf, wg, wt, wown, stk,
    mrim_s, mrim_r, rim_s, rim_r, ndx, ndr, hall, ssr, wqx, wqr, wqs, wqt, wgb, wfin, pts, ptr, snr, sfr,
    mr_sem, rim_ss, rim_rs, nd_ss, nd_rs, hg_ss, hg_rs, ss_ss, ss_rs,
    ws_ss, ws_rs, wt_ss, wt_rs, wg_ss, wg_rs, pt_sem, sn_ss, sn_rs, sf_ss, sf_rs,
):
    me_n = lax.axis_index("neuron")
    me_f = lax.axis_index("frame")
    me_h = lax.axis_index("half")
    N = ca_ref.shape[0]
    EXT = T + RIM
    gp = GROUPS // NF
    rg = K // 8
    w = T * rg // NN
    pending = []

    def send(src, dst, ssem, rsem, axis, peer):
        c = pltpu.make_async_remote_copy(
            src_ref=src, dst_ref=dst, send_sem=ssem, recv_sem=rsem,
            device_id={axis: peer}, device_id_type=MESH,
        )
        c.start()
        pending.append(c)
        return c

    def npeer(r):
        return lax.rem(me_n + r, NN)

    def fpeer(r):
        return lax.rem(me_f + r, NF)

    barrier = pltpu.get_barrier_semaphore()
    for r in range(1, NN):
        pl.semaphore_signal(barrier, inc=1, device_id={"neuron": npeer(r)}, device_id_type=MESH)
    for r in range(1, NF):
        pl.semaphore_signal(barrier, inc=1, device_id={"frame": fpeer(r)}, device_id_type=MESH)
    pl.semaphore_signal(barrier, inc=1, device_id={"half": 1 - me_h}, device_id_type=MESH)

    trials = th_ref.shape[1]
    rows = lax.broadcasted_iota(jnp.int32, (trials, trials), 0)
    cols = lax.broadcasted_iota(jnp.int32, (trials, trials), 1)
    thf = th_ref[...].astype(F32)
    th_col = jnp.sum(jnp.where(rows == cols, thf, 0.0), axis=1, keepdims=True)
    chosen = jnp.where(th_col == me_h.astype(F32), 1.0, 0.0)
    hit = lax.broadcasted_iota(jnp.int32, (trials, T), 0) == tof_ref[...]
    mask = jnp.sum(jnp.where(hit, chosen, 0.0), axis=0, keepdims=True)
    masked = (ca_ref[...].astype(F32) * mask).astype(BF16)
    mext[:, :T] = masked
    mrim_s[...] = masked[:, :RIM]
    hf[...] = prof_ref[...]
    rim_s[0, 0] = prof_ref[:, :RIM]
    rim_s[0, 1] = prof_ref[:, T - RIM:]

    pl.semaphore_wait(barrier, (NN - 1) + (NF - 1) + 1)

    left = fpeer(NF - 1)
    right = fpeer(1)
    rims = {}

    def send_rims(i):
        rims[i] = (
            send(rim_s.at[i, 0], rim_r.at[i, 0], rim_ss.at[i, 0], rim_rs.at[i, 0], "frame", left),
            send(rim_s.at[i, 1], rim_r.at[i, 1], rim_ss.at[i, 1], rim_rs.at[i, 1], "frame", right),
        )

    send_rims(0)
    mcopy = send(mrim_s, mrim_r, mr_sem.at[0], mr_sem.at[1], "frame", left)

    for g in range(GROUPS):
        wg[g] = w_ref[g].astype(BF16)
    wown[...] = w_ref[pl.ds(me_f * gp, gp)]

    crow = (me_n % rg) * 8
    ccol = (me_n // rg) * w
    if NN == rg:
        hown = prof_ref[pl.ds(pl.multiple_of(crow, 8), 8), :]
    else:
        hown = prof_ref[pl.ds(pl.multiple_of(crow, 8), 8), pl.ds(pl.multiple_of(ccol, 128), w)]

    def own_rows(col):
        out = col[0:8]
        for q in range(1, rg):
            out = jnp.where(me_n % rg == q, col[q * 8:(q + 1) * 8], out)
        return out

    def build_right(width, lo=0, hi=GROUPS, extra=None):
        def body(g, _):
            v = hs[...]
            for b in range(GL):
                hlag[pl.ds(pl.multiple_of(g * GW + b * K, K), K), :width] = (
                    v[:, 2 * RIM - b:2 * RIM - b + width]
                )
            hs[:, RIM:] = v[:, RIM - GL:hs.shape[1] - GL]
            part = dot(wg[g], hlag[pl.ds(pl.multiple_of(g * GW, GW), GW), :width])
            acc[:, :width] = acc[:, :width] + part
            if extra is not None:
                extra(g)
            return 0

        if lo == 0:
            acc[...] = jnp.zeros_like(acc)
        lax.fori_loop(lo, hi, body, 0)

    def fill_hs(left_rim, body, right_rim):
        hs[:, :RIM] = jnp.zeros((K, RIM), BF16)
        hs[:, RIM:2 * RIM] = left_rim.astype(BF16)
        hs[:, 2 * RIM:2 * RIM + T] = body.astype(BF16)
        hs[:, 2 * RIM + T:] = right_rim.astype(BF16)

    def build_left(dst, g):
        v = ms[...]
        for b in range(GL):
            dst[pl.ds(pl.multiple_of(g * GW + b * N, N), N), :] = v[:, b:b + T]
        ms[:, :EXT] = v[:, GL:EXT + GL]

    mcopy.wait_recv()
    mext[:, T:] = mrim_r[...]
    ms[:, :EXT] = mext[...]
    ms[:, EXT:] = jnp.zeros((N, RIM), BF16)

    def mbody(g, _):
        build_left(mlag, g)
        return 0

    lax.fori_loop(0, GROUPS, mbody, 0)
    stk[:N] = mext[:, :T]
    mask_ext = jnp.where(mext[...].astype(F32) > 0.0, 1.0, 0.0)

    def send_sums(it, kind, src):
        for p in range(NN):
            a, b = (p % rg) * 8, (p // rg) * w
            ndx[it, kind, p] = src[a:a + 8, b:b + w]
        at = 2 * it + kind
        return [
            send(ndx.at[it, kind, npeer(r)], ndr.at[it, kind, r - 1], nd_ss.at[at, r], nd_rs.at[at, r],
                 "neuron", npeer(r))
            for r in range(1, NN)
        ]

    RQ = 2 * N // 4
    quad = lax.broadcasted_iota(jnp.int32, (RQ, 128), 1) // K
    wcs = {}

    def contract(rows_bf, g):
        rws = pl.ds(pl.multiple_of(g * GW, GW), GW)
        return lax.dot_general(
            rows_bf, hlag[rws, :T], (((1,), (1,)), ((), ())), preferred_element_type=F32
        )

    scale = None
    for it in range(ITERS):
        last = it == ITERS - 1
        def tbody(g, _):
            x = wg[g].astype(F32)
            for h in range(GW // 128):
                t = x[:, h * 128:(h + 1) * 128].T
                wt[g, :, h * 128:(h + 1) * 128] = jnp.concatenate(
                    [t[q * K:(q + 1) * K] for q in range(4)], axis=1
                ).astype(BF16)
            return 0

        lax.fori_loop(0, GROUPS, tbody, 0)

        accn[...] = jnp.zeros_like(accn)

        def nbody(g, _):
            accn[...] = accn[...] + dot(wt[g], mlag[pl.ds(pl.multiple_of(g * GW, GW), GW), :])
            return 0

        lax.fori_loop(0, GROUPS, nbody, 0)
        ncs = send_sums(it, 0, accn)
        if it == 0:
            for c in rims[it]:
                c.wait_recv()
            fill_hs(rim_r[it, 1], hf[...], rim_r[it, 0])
        else:
            rims[it][0].wait_recv()
            fill_hs(rim_r[it, 1] / scale, hf[...] / scale, rim_r[it, 0] / scale)
        build_right(EXT)
        approx = (acc[...].astype(BF16).astype(F32) * mask_ext).astype(BF16)
        ms[:, :EXT] = approx

        accd[...] = jnp.zeros_like(accd)

        def dbody(g, _):
            build_left(alag, g)
            rws = pl.ds(pl.multiple_of(g * GW, GW), GW)
            accd[...] = accd[...] + dot(wt[g], alag[rws, :])
            return 0

        lax.fori_loop(0, GROUPS, dbody, 0)
        dcs = send_sums(it, 1, accd)
        num = ndx[it, 0, me_n]
        den = ndx[it, 1, me_n]
        for r in range(1, NN):
            ncs[r - 1].wait_recv()
            num = num + ndr[it, 0, r - 1]
        for r in range(1, NN):
            dcs[r - 1].wait_recv()
            den = den + ndr[it, 1, r - 1]
        hown = hown * num / jnp.maximum(den, 1.0)
        hall[it, me_n] = hown
        cs = [
            send(hall.at[it, me_n], hall.at[it, me_n], hg_ss.at[it, r], hg_rs.at[it, r], "neuron", npeer(r))
            for r in range(1, NN)
        ]
        for c in cs:
            c.wait_recv()
        for p in range(NN):
            a, b = (p % rg) * 8, (p // rg) * w
            hf[a:a + 8, b:b + w] = hall[it, p]
        hnew = hf[...]
        rim_s[it + 1, 0] = hnew[:, :RIM]
        rim_s[it + 1, 1] = hnew[:, T - RIM:]
        send_rims(it + 1)
        sq = jnp.sum(hnew * hnew, axis=1, keepdims=True)
        ssr[it, me_f] = jnp.broadcast_to(sq, (K, 128))
        ssc = [
            send(ssr.at[it, me_f], ssr.at[it, me_f], ss_ss.at[it, r], ss_rs.at[it, r], "frame", fpeer(r))
            for r in range(1, NF)
        ]
        rims[it + 1][1].wait_recv()
        fill_hs(rim_r[it + 1, 1], hnew, hnew[:, :RIM])
        build_right(T)
        approx2 = (acc[:, :T].astype(BF16).astype(F32) * mask_ext[:, :T]).astype(BF16)
        stk[N:] = approx2
        for r in list(range(1, NF)) + [0]:
            p = fpeer(r)
            sums = [contract(stk[...], p * gp + q) for q in range(gp)]
            if r:
                top = sums[0][:, :128]
                for x in sums:
                    for h in range(GW // 128):
                        top = jnp.maximum(top, x[:, h * 128:(h + 1) * 128])
                top = jnp.maximum(top, pltpu.roll(top, 64, 1))
                top = jnp.maximum(top, pltpu.roll(top, 32, 1))
                inv = 65534.0 / jnp.maximum(top, 1e-30)
                inv = jnp.concatenate([inv] * (GW // 128), axis=1)
                for q in range(gp):
                    code = jnp.minimum(jnp.round(sums[q] * inv) - 32767.0, 32767.0)
                    wqx[it, r - 1, q] = code.astype(jnp.int32).astype(jnp.int16)
                packed = top[:RQ]
                for j in range(1, 4):
                    packed = jnp.where(quad == j, top[j * RQ:(j + 1) * RQ], packed)
                wqs[it, r - 1] = packed
                wcs[r - 1] = (
                    send(wqs.at[it, r - 1], wqt.at[it, r - 1], wt_ss.at[it, r], wt_rs.at[it, r], "frame", p),
                    send(wqx.at[it, r - 1], wqr.at[it, r - 1], ws_ss.at[it, r], ws_rs.at[it, r], "frame", p),
                )
            else:
                wtot = sums
        for c in ssc:
            c.wait_recv()
        total = ssr[it, 0]
        for p in range(1, NF):
            total = total + ssr[it, p]
        scale_wide = jnp.sqrt(total + EPS)
        scale = scale_wide[:, 0:1]
        ek = lax.broadcasted_iota(jnp.int32, (K, GW), 0)
        ec = lax.broadcasted_iota(jnp.int32, (K, GW), 1) % K
        scale_row = jnp.sum(jnp.where(ek == ec, scale, 0.0), axis=0, keepdims=True)
        hown = hown / own_rows(scale)
        for r in range(1, NF):
            for c in wcs[r - 1]:
                c.wait_recv()
            packed = wqt[it, r - 1]
            tops = []
            for j in range(4):
                t = jnp.where(quad == j, packed, 0.0)
                t = t + pltpu.roll(t, 64, 1)
                tops.append(t + pltpu.roll(t, 32, 1))
            unit = jnp.concatenate(tops, axis=0) * (1.0 / 65534.0)
            unit = jnp.concatenate([unit] * (GW // 128), axis=1)
            wtot = [
                wtot[q] + (wqr[it, r - 1, q].astype(jnp.int32).astype(F32) + 32767.0) * unit
                for q in range(gp)
            ]
        wnew = jnp.stack([wown[q] * wtot[q][:N] / wtot[q][N:] * scale_row for q in range(gp)])
        wown[...] = wnew
        mine = pl.ds(me_f * gp, gp)
        if not last:
            wgb[it, mine] = wnew.astype(BF16)
            cs = [
                send(wgb.at[it, mine], wgb.at[it, mine], wg_ss.at[it, r], wg_rs.at[it, r], "frame", fpeer(r))
                for r in range(1, NF)
            ]
            for c in cs:
                c.wait_recv()
            wg[...] = wgb[it]

    pts[...] = wnew.astype(BF16)
    ptc = send(pts, ptr, pt_sem.at[0], pt_sem.at[1], "half", 1 - me_h)
    wfin[mine] = wnew
    fcs = [
        send(wfin.at[mine], wfin.at[mine], wg_ss.at[ITERS - 1, r], wg_rs.at[ITERS - 1, r], "frame", fpeer(r))
        for r in range(1, NF)
    ]
    hout_ref[...] = hf[...] / scale
    ptc.wait_recv()
    far = ptr[...].astype(F32)
    cross = jnp.zeros((128, 128), F32)
    osq = jnp.zeros((1, 128), F32)
    fsq = jnp.zeros((1, 128), F32)
    for q in range(gp):
        for h in range(GW // 128):
            a = wnew[q, :, h * 128:(h + 1) * 128]
            b = far[q, :, h * 128:(h + 1) * 128]
            cross = cross + lax.dot_general(
                a, b, (((0,), (0,)), ((), ())),
                preferred_element_type=F32, precision=lax.Precision.HIGHEST,
            )
            osq = osq + jnp.sum(a * a, axis=0, keepdims=True)
            fsq = fsq + jnp.sum(b * b, axis=0, keepdims=True)
    ri = lax.broadcasted_iota(jnp.int32, (128, 128), 0)
    ci = lax.broadcasted_iota(jnp.int32, (128, 128), 1)
    cross = jnp.where(ri // K == ci // K, cross, 0.0)
    cross = cross[0:K] + cross[K:2 * K] + cross[2 * K:3 * K] + cross[3 * K:]

    def fold(x):
        x = x + pltpu.roll(x, 64, 1)
        return x + pltpu.roll(x, 32, 1)

    pack = jnp.concatenate(
        [cross, jnp.broadcast_to(osq, (8, 128)), jnp.broadcast_to(fsq, (8, 128))], axis=0
    )
    snr[me_n] = fold(pack)
    cs = [
        send(snr.at[me_n], snr.at[me_n], sn_ss.at[r], sn_rs.at[r], "neuron", npeer(r))
        for r in range(1, NN)
    ]
    for c in cs:
        c.wait_recv()
    tot = snr[0]
    for p in range(1, NN):
        tot = tot + snr[p]
    sfr[me_f] = tot
    cs = [
        send(sfr.at[me_f], sfr.at[me_f], sf_ss.at[r], sf_rs.at[r], "frame", fpeer(r))
        for r in range(1, NF)
    ]
    for c in fcs:
        c.wait_recv()
    wout_ref[...] = wfin[...]
    for c in cs:
        c.wait_recv()
    tot = sfr[0]
    for p in range(1, NF):
        tot = tot + sfr[p]
    own_row = tot[K:K + 1]
    far_row = tot[K + 8:K + 9]
    rk = lax.broadcasted_iota(jnp.int32, (K, 128), 0)
    ck = lax.broadcasted_iota(jnp.int32, (K, 128), 1)
    own_col = jnp.sum(jnp.where(rk == ck, own_row, 0.0), axis=1, keepdims=True)
    sim = tot[:K] / jnp.sqrt((own_col + EPS) * (far_row + EPS))
    sim_ref[...] = sim[:, :K]
    rims[ITERS][0].wait_recv()
    for c in pending:
        c.wait_send()


def roll_right(x, s):
    return pltpu.roll(x, s, 1) if s else x


def roll_left(x, s):
    return pltpu.roll(x, x.shape[1] - s, 1) if s else x


def wide_kernel(
    NN, NF, T,
    ca_hbm, tof_hbm, th_hbm, w_hbm, prof_hbm,
    wout_ref, hout_ref, sim_ref,
    ca_ref, tof_ref, th_ref, w_ref, prof_ref, by_lag, wf,
    rim_s, rim_r, mtx, mrx, w32, wt32, hla, mla, ala,
    ndx, ndr, hb, hl, ml, al, dat, md, prx, acc, own, tx, rx, topx, topr,
    hg, far_s, far_r, snx, snr,
    isem, ssem, rsem,
):
    me_n = lax.axis_index("neuron")
    me_f = lax.axis_index("frame")
    me_h = lax.axis_index("half")
    me_c = lax.rem(me_n, 2)
    me_y = me_n // 2
    N = ca_ref.shape[0]
    F = NF * T
    NB = N // NF
    KC = K // 2
    TC = T // 2
    EXT = T + RIM
    pending = []

    def send(src, dst, peer):
        i = len(pending)
        c = pltpu.make_async_remote_copy(
            src_ref=src, dst_ref=dst, send_sem=ssem.at[i], recv_sem=rsem.at[i],
            device_id=peer, device_id_type=MESH,
        )
        c.start()
        pending.append(c)
        return c

    def npeer(r):
        return lax.rem(me_n + r, NN)

    def fpeer(r):
        return lax.rem(me_f + r, NF)

    core = {"neuron": me_n + 1 - 2 * me_c}
    seven = [(dy, dz) for dz in (3, 2, 1, 0) for dy in (1, 0) if dy or dz]

    def block_of(dy, dz):
        return fpeer(dz) * 2 + lax.rem(me_y + dy, 2)

    def to(dy, dz):
        return {"neuron": npeer(2 * dy), "frame": fpeer(dz)}

    others = [(dn, df) for df in (3, 2, 1, 0) for dn in (3, 2, 1, 0) if dn or df]
    barrier = pltpu.get_barrier_semaphore()
    for dn, df in others:
        pl.semaphore_signal(
            barrier, inc=1, device_id={"neuron": npeer(dn), "frame": fpeer(df)}, device_id_type=MESH
        )
    pl.semaphore_signal(barrier, inc=1, device_id={"half": 1 - me_h}, device_id_type=MESH)

    loads = [
        pltpu.make_async_copy(a, b, isem.at[i])
        for i, (a, b) in enumerate([
            (th_hbm, th_ref), (tof_hbm, tof_ref), (ca_hbm, ca_ref), (prof_hbm, prof_ref), (w_hbm, w_ref),
        ])
    ]
    for c in loads:
        c.start()

    def turn(x):
        out = []
        for h in range(GW // 128):
            t = x[:, h * 128:(h + 1) * 128].T
            out.append(jnp.concatenate([t[q * K:(q + 1) * K] for q in range(4)], axis=1))
        return jnp.concatenate(out, axis=1)

    for c in loads[:-1]:
        c.wait()

    trials = th_ref.shape[1]
    rows = lax.broadcasted_iota(jnp.int32, (trials, trials), 0)
    cols = lax.broadcasted_iota(jnp.int32, (trials, trials), 1)
    thf = th_ref[...].astype(F32)
    th_col = jnp.sum(jnp.where(rows == cols, thf, 0.0), axis=1, keepdims=True)
    chosen = jnp.where(th_col == me_h.astype(F32), 1.0, 0.0)
    hit = lax.broadcasted_iota(jnp.int32, (trials, T), 0) == tof_ref[...]
    mask = jnp.sum(jnp.where(hit, chosen, 0.0), axis=0, keepdims=True)
    masked = ca_ref[...].astype(F32) * mask
    body = masked.astype(BF16)
    prof = prof_ref[...].astype(BF16)
    rim_s[0, :N] = body[:, :RIM]
    rim_s[0, N:] = prof[:, :RIM]
    rim_s[1, :K] = prof[:, T - RIM:]
    for z in range(NF):
        x = masked[z * NB:(z + 1) * NB]
        mtx[z] = jnp.concatenate([x[:, :TC], x[:, TC:]], axis=0).astype(BF16)

    pl.semaphore_wait(barrier, len(others) + 1)

    to_left = send(rim_s.at[0], rim_r.at[0], {"frame": fpeer(NF - 1)})
    to_right = send(rim_s.at[1, pl.ds(0, K)], rim_r.at[1, pl.ds(0, K)], {"frame": fpeer(1)})
    mcs = [
        send(mtx.at[fpeer(r)], mrx.at[me_f], {"frame": fpeer(r)})
        for r in (3, 2, 1)
    ]
    mrx[me_f] = mtx[me_f]

    loads[-1].wait()
    for j in range(K * L // 128):
        by_lag[j * 128:(j + 1) * 128, :N] = w_ref[:, j * 128:(j + 1) * 128].T
    for a in range(GROUPS):
        x = jnp.concatenate(
            [by_lag[pl.ds(a * GL + b, K, stride=L), :][:, :N] for b in range(GL)], axis=1
        )
        wt32[a * K:(a + 1) * K] = x.astype(BF16)
        x = turn(x)
        wf[a] = x
        w32[a * N:(a + 1) * N] = x.astype(BF16)
    mine = pl.ds(pl.multiple_of(me_f * NB, NB), NB)
    w8 = jnp.concatenate([wf[a, mine, :] for a in range(GROUPS)], axis=0)

    to_left.wait_recv()
    mext = jnp.concatenate([body, rim_r[0, :N]], axis=1)
    mask_ext = jnp.where(mext.astype(F32) > 0.0, 1.0, 0.0)

    def lags(dst, x, roll):
        n = x.shape[0]
        for b in range(GL):
            dst[b * n:(b + 1) * n] = roll(x, b)

    def numer_of(m):
        q = dot(wt32[...], m[...])
        s = q[:K]
        for a in range(1, GROUPS):
            s = s + roll_left(q[a * K:(a + 1) * K], a * GL)
        return s[:, :T]

    def scatter(kind, s):
        for p in range(NN):
            a, b = (p % 2) * KC, (p // 2) * TC
            ndx[kind, p] = s[a:a + KC, b:b + TC]
        return [
            send(ndx.at[kind, npeer(r)], ndr.at[kind, r - 1], {"neuron": npeer(r)})
            for r in range(1, NN)
        ]

    lags(mla, mext, roll_left)
    ncs = scatter(0, numer_of(mla))
    to_right.wait_recv()
    lags(hla, jnp.concatenate([rim_r[1, :K], prof, rim_r[0, N:]], axis=1), roll_right)
    p = dot(w32[...], hla[...])
    s = p[:N]
    for a in range(1, GROUPS):
        s = s + roll_right(p[a * N:(a + 1) * N], a * GL)
    approx = (s[:, RIM:].astype(BF16).astype(F32) * mask_ext).astype(BF16)
    lags(ala, approx, roll_left)
    dcs = scatter(1, numer_of(ala))

    own_rows = pl.ds(pl.multiple_of(me_c * KC, KC), KC)
    far_rows = pl.ds(pl.multiple_of((1 - me_c) * KC, KC), KC)
    hown = prof_ref[own_rows, pl.ds(pl.multiple_of(me_y * TC, TC), TC)]
    num = ndx[0, me_n]
    den = ndx[1, me_n]
    for r in range(1, NN):
        ncs[r - 1].wait_recv()
        num = num + ndr[0, r - 1]
    for r in range(1, NN):
        dcs[r - 1].wait_recv()
        den = den + ndr[1, r - 1]
    hown = hown * num / jnp.maximum(den, 1.0)

    def spot(c, blk):
        return pl.ds(pl.multiple_of(c * KC, KC), KC), pl.ds(pl.multiple_of(blk * TC, TC), TC)

    lane = lax.broadcasted_iota(jnp.int32, (8, 128), 1)

    def gather_h(it):
        a, b = spot(me_c, block_of(0, 0))
        hb[it, a, b] = hown.astype(BF16)
        cs = [send(hb.at[it, a, b], hb.at[it, a, b], to(dy, dz)) for dy, dz in seven]
        relays = [send(hb.at[it, a, b], hb.at[it, a, b], core)]
        return cs, relays

    def half_lags(it, rows_of, c):
        x = hb[it, rows_of, :]
        for b in range(GL):
            hl[pl.ds(pl.multiple_of(b * K + c * KC, KC), KC), :] = roll_right(x, b)

    def relay_h(it, cs, relays):
        for i in range(len(seven) - 1, -1, -1):
            cs[i].wait_recv()
            dy, dz = seven[i]
            a, b = spot(me_c, block_of(dy, NF - dz))
            relays.append(send(hb.at[it, a, b], hb.at[it, a, b], core))
        half_lags(it, own_rows, me_c)
        for c in relays:
            c.wait_recv()
        half_lags(it, far_rows, 1 - me_c)

    def squares(it):
        x = hb[it].astype(F32)
        return jnp.sum(x * x, axis=1, keepdims=True)

    cs, relays = gather_h(0)

    for c in mcs:
        c.wait_recv()
    for z in range(NF):
        x = mrx[z].astype(F32)
        md[:, z * T:z * T + TC] = x[:NB]
        md[:, z * T + TC:(z + 1) * T] = x[NB:]
    data = md[...]
    mask_all = jnp.where(data[0:1] > 0.0, 1.0, 0.0)
    rolled = [roll_left(data, a * GL) for a in range(GROUPS)]
    for a in range(GROUPS):
        dat[a * 2 * NB:a * 2 * NB + NB] = rolled[a]
    lags(ml, jnp.concatenate(rolled[:4], axis=0).astype(BF16), roll_left)

    def recon(wb):
        p = dot(wb, hl[...])
        s = p[:NB]
        for a in range(1, GROUPS):
            s = s + roll_right(p[a * NB:(a + 1) * NB], a * GL)
        return s.astype(BF16).astype(F32) * mask_all

    def corr(wt, m):
        q = dot(wt, m[...])
        return q[:K] + roll_left(q[K:], 4 * GL)

    def template_ratio():
        approx = recon(w8.astype(BF16))
        for a in range(GROUPS):
            dat[a * 2 * NB + NB:(a + 1) * 2 * NB] = roll_left(approx, a * GL)
        s = lax.dot_general(
            dat[...].astype(BF16), hl[...], (((1,), (1,)), ((), ())), preferred_element_type=F32
        )
        wnum = jnp.concatenate([s[a * 2 * NB:a * 2 * NB + NB] for a in range(GROUPS)], axis=0)
        wden = jnp.concatenate([s[a * 2 * NB + NB:(a + 1) * 2 * NB] for a in range(GROUPS)], axis=0)
        return wnum, wden

    relay_h(0, cs, relays)
    wnum, wden = template_ratio()
    w8 = w8 * wnum / wden

    wt = jnp.concatenate([turn(w8[:4 * NB]), turn(w8[4 * NB:])], axis=0).astype(BF16)

    def reduce_start(kind, s):
        acc[kind] = s
        return send(acc.at[kind, far_rows], prx.at[kind], core)

    def reduce_spread(kind, c):
        c.wait_recv()
        s = acc[kind, own_rows, :] + prx[kind]
        own[kind] = s
        top = jnp.maximum(jnp.max(s, axis=1, keepdims=True), 1e-30)
        topx[kind] = jnp.sum(jnp.where(eye, top, 0.0), axis=0, keepdims=True)
        ts = [send(topx.at[kind], topr.at[kind * 7 + i], to(dy, dz)) for i, (dy, dz) in enumerate(seven)]
        code = jnp.round(s * (65534.0 / top)) - 32767.0
        tx[kind] = jnp.minimum(code, 32767.0).astype(jnp.int32).astype(jnp.int16)
        return ts, [
            send(
                tx.at[kind, :, pl.ds(pl.multiple_of(block_of(dy, dz) * TC, TC), TC)],
                rx.at[kind, i], to(dy, dz),
            )
            for i, (dy, dz) in enumerate(seven)
        ]

    def reduce_done(kind, sent):
        ts, cs = sent
        t = own[kind, :, pl.ds(pl.multiple_of(block_of(0, 0) * TC, TC), TC)]
        for i in range(len(seven) - 1, -1, -1):
            ts[i].wait_recv()
            unit = jnp.sum(jnp.where(eye, topr[kind * 7 + i], 0.0), axis=1, keepdims=True) * (1.0 / 65534.0)
            cs[i].wait_recv()
            t = t + (rx[kind, i].astype(jnp.int32).astype(F32) + 32767.0) * unit
        return t

    eye = lax.broadcasted_iota(jnp.int32, (KC, 128), 0) == lax.broadcasted_iota(jnp.int32, (KC, 128), 1)
    nc = reduce_start(0, corr(wt, ml))
    approx = recon(w8.astype(BF16))
    ncs = reduce_spread(0, nc)
    lags(al, jnp.concatenate([roll_left(approx, a * GL) for a in range(4)], axis=0).astype(BF16), roll_left)
    dc = reduce_start(1, corr(wt, al))
    scale0 = jnp.sqrt(squares(0) + EPS)
    dcs = reduce_spread(1, dc)
    num = reduce_done(0, ncs)
    den = reduce_done(1, dcs)
    s0 = jnp.where(me_c == 0, scale0[:KC], scale0[KC:])
    hown = hown * (num * s0) / jnp.maximum(den * s0, 1.0)
    cs, relays = gather_h(1)
    hg[me_n] = hown
    hcs = [send(hg.at[me_n], hg.at[me_n], {"neuron": npeer(r)}) for r in (3, 2, 1)]
    relay_h(1, cs, relays)
    wnum, wden = template_ratio()
    scale = jnp.sqrt(squares(1) + EPS * scale0 * scale0)
    ek = lax.broadcasted_iota(jnp.int32, (K, GW), 0)
    ec = lax.broadcasted_iota(jnp.int32, (K, GW), 1) % K
    scale_row = jnp.sum(jnp.where(ek == ec, scale, 0.0), axis=0, keepdims=True)
    w8 = w8 * wnum / wden * scale_row

    far_s[...] = w8.astype(BF16)
    fc = send(far_s, far_r, {"half": 1 - me_h})
    for q in range(2):
        t = turn(w8[q * 4 * NB:(q + 1) * 4 * NB])
        for b in range(GL):
            for a in range(4):
                at = b * K + a * NB
                by_lag[pl.ds(q * 4 * GL + a * GL + b, K, stride=L), :NB] = t[:, at:at + NB]
    for j in range(K * L // 128):
        wout_ref[mine, j * 128:(j + 1) * 128] = by_lag[j * 128:(j + 1) * 128, :NB].T
    wcs = [send(wout_ref.at[mine], wout_ref.at[mine], {"frame": fpeer(r)}) for r in (3, 2, 1)]
    for c in hcs:
        c.wait_recv()
    for p in range(NN):
        a, b = (p % 2) * KC, (p // 2) * TC
        hout_ref[a:a + KC, b:b + TC] = hg[p] / scale[a:a + KC]
    fc.wait_recv()
    far = far_r[...].astype(F32)
    cross = jnp.zeros((128, 128), F32)
    osq = jnp.zeros((1, 128), F32)
    fsq = jnp.zeros((1, 128), F32)
    for h in range(GW // 128):
        a = w8[:, h * 128:(h + 1) * 128]
        b = far[:, h * 128:(h + 1) * 128]
        cross = cross + lax.dot_general(
            a, b, (((0,), (0,)), ((), ())),
            preferred_element_type=F32, precision=lax.Precision.HIGHEST,
        )
        osq = osq + jnp.sum(a * a, axis=0, keepdims=True)
        fsq = fsq + jnp.sum(b * b, axis=0, keepdims=True)
    ri = lax.broadcasted_iota(jnp.int32, (128, 128), 0)
    ci = lax.broadcasted_iota(jnp.int32, (128, 128), 1)
    cross = jnp.where(ri // K == ci // K, cross, 0.0)
    cross = cross[0:K] + cross[K:2 * K] + cross[2 * K:3 * K] + cross[3 * K:]

    def fold(x):
        x = x + pltpu.roll(x, 64, 1)
        return x + pltpu.roll(x, 32, 1)

    cross = fold(cross)
    quad = lane // K
    pack = cross[:8]
    for q in range(1, 4):
        pack = jnp.where(quad == q, cross[q * 8:(q + 1) * 8], pack)
    for q in range(8):
        snx[:, q * 128:(q + 1) * 128] = pack[q:q + 1]
    snx[:, 8 * 128:] = jnp.where(quad[:1] < 2, fold(osq), fold(fsq))
    scs = [
        send(snx, snr.at[i], {"neuron": npeer(dn), "frame": fpeer(df)})
        for i, (dn, df) in enumerate(others)
    ]
    tot = snx[...]
    for i in range(len(others) - 1, -1, -1):
        scs[i].wait_recv()
        tot = tot + snr[i]
    own_row = tot[:, 8 * 128:]
    far_row = pltpu.roll(own_row, 64, 1)
    tot = jnp.concatenate([tot[:, q * 128:(q + 1) * 128] for q in range(8)], axis=0)
    rk = lax.broadcasted_iota(jnp.int32, (K, 128), 0)
    ck = lax.broadcasted_iota(jnp.int32, (K, 128), 1)
    own_col = jnp.sum(jnp.where(rk == ck, own_row, 0.0), axis=1, keepdims=True)
    full = jnp.concatenate(
        [tot] + [pltpu.roll(tot, 128 - q * K, 1) for q in range(1, 4)], axis=0
    )
    sim = full / jnp.sqrt((own_col + EPS) * (far_row + EPS))
    sim_ref[...] = sim[:, :K]
    for c in wcs:
        c.wait_recv()
    for c in pending:
        c.wait_send()


def wide_call(NN, NF, T, N, trials):
    F = NF * T
    NB = N // NF
    KC = K // 2
    TC = T // 2
    EXT = T + RIM
    V = pltpu.VMEM
    D = pltpu.SemaphoreType.DMA
    vmem = pl.BlockSpec(memory_space=pltpu.VMEM)
    return pl.pallas_call(
        functools.partial(wide_kernel, NN, NF, T),
        out_shape=(
            jax.ShapeDtypeStruct((N, K * L), F32),
            jax.ShapeDtypeStruct((K, T), F32),
            jax.ShapeDtypeStruct((K, K), F32),
        ),
        in_specs=[pl.BlockSpec(memory_space=pl.ANY)] * 5,
        out_specs=(vmem,) * 3,
        scratch_shapes=[
            V((N, T), BF16),
            V((1, T), jnp.int32),
            V((1, trials), jnp.int32),
            V((N, K * L), F32),
            V((K, T), F32),
            V((K * L, 128), F32),
            V((GROUPS, N, GW), F32),
            V((2, N + K, RIM), BF16),
            V((2, N + K, RIM), BF16),
            V((NF, 2 * NB, TC), BF16),
            V((NF, 2 * NB, TC), BF16),
            V((GROUPS * N, GW), BF16),
            V((GROUPS * K, GW), BF16),
            V((GW, EXT + RIM), BF16),
            V((GW, EXT), BF16),
            V((GW, EXT), BF16),
            V((2, NN, KC, TC), F32),
            V((2, NN - 1, KC, TC), F32),
            V((ITERS, K, F), BF16),
            V((GW, F), BF16),
            V((GW, F), BF16),
            V((GW, F), BF16),
            V((2 * GROUPS * NB, F), F32),
            V((NB, F), F32),
            V((2, KC, F), F32),
            V((2, K, F), F32),
            V((2, KC, F), F32),
            V((2, KC, F), jnp.int16),
            V((2, 7, KC, TC), jnp.int16),
            V((2, 1, 128), F32),
            V((14, 1, 128), F32),
            V((NN, KC, TC), F32),
            V((GROUPS * NB, GW), BF16),
            V((GROUPS * NB, GW), BF16),
            V((1, 9 * 128), F32),
            V((NN * NF - 1, 1, 9 * 128), F32),
            D((5,)),
            D((96,)),
            D((96,)),
        ],
        compiler_params=pltpu.CompilerParams(
            collective_id=1, has_side_effects=True, vmem_limit_bytes=56 << 20
        ),
    )


def emit_kernel(w_ref, h_ref, s_ref, w_out, h_out, s_out, sem):
    pairs = [(h_ref, h_out.at[0]), (s_ref, s_out.at[0])]
    step = w_ref.shape[1] // 2
    for r in range(w_ref.shape[0] // 8):
        for q in range(2):
            part = (pl.ds(r * 8, 8), pl.ds(q * step, step))
            pairs.append((w_ref.at[part], w_out.at[0].at[part]))
    cs = [pltpu.make_async_copy(a, b, sem.at[i]) for i, (a, b) in enumerate(pairs)]
    for c in cs:
        c.start()
    for c in cs:
        c.wait()


def emit(*arrays):
    return pl.pallas_call(
        emit_kernel,
        out_shape=tuple(jax.ShapeDtypeStruct((1, *x.shape), F32) for x in arrays),
        in_specs=[pl.BlockSpec(memory_space=pltpu.VMEM)] * 3,
        out_specs=(pl.BlockSpec(memory_space=pl.ANY),) * 3,
        scratch_shapes=[pltpu.SemaphoreType.DMA((2 + arrays[0].shape[0] // 4,))],
    )(*arrays)


def tall_call(NN, NF, T, N):
    gp = GROUPS // NF
    rg = K // 8
    w = T * rg // NN
    EXT = T + RIM
    V = pltpu.VMEM
    D = pltpu.SemaphoreType.DMA
    vmem = pl.BlockSpec(memory_space=pltpu.VMEM)
    return pl.pallas_call(
        functools.partial(kernel, NN, NF, T),
        out_shape=(
            jax.ShapeDtypeStruct((GROUPS, N, GW), F32),
            jax.ShapeDtypeStruct((K, T), F32),
            jax.ShapeDtypeStruct((K, K), F32),
        ),
        in_specs=[vmem] * 5,
        out_specs=(vmem,) * 3,
        scratch_shapes=[
            V((K, 2 * RIM + T + RIM), BF16),
            V((L * K, EXT), BF16),
            V((N, EXT), BF16),
            V((N, EXT + RIM), BF16),
            V((L * N, T), BF16),
            V((L * N, T), BF16),
            V((N, EXT), F32),
            V((K, T), F32),
            V((K, T), F32),
            V((K, T), F32),
            V((GROUPS, N, GW), BF16),
            V((GROUPS, K, GW), BF16),
            V((gp, N, GW), F32),
            V((2 * N, T), BF16),
            V((N, RIM), BF16),
            V((N, RIM), BF16),
            V((ITERS + 1, 2, K, RIM), F32),
            V((ITERS + 1, 2, K, RIM), F32),
            V((ITERS, 2, NN, 8, w), F32),
            V((ITERS, 2, NN - 1, 8, w), F32),
            V((ITERS, NN, 8, w), F32),
            V((ITERS, NF, K, 128), F32),
            V((ITERS, NF - 1, gp, 2 * N, GW), jnp.int16),
            V((ITERS, NF - 1, gp, 2 * N, GW), jnp.int16),
            V((ITERS, NF - 1, 2 * N // 4, 128), F32),
            V((ITERS, NF - 1, 2 * N // 4, 128), F32),
            V((ITERS - 1, GROUPS, N, GW), BF16),
            V((GROUPS, N, GW), F32),
            V((gp, N, GW), BF16),
            V((gp, N, GW), BF16),
            V((NN, K + 16, 128), F32),
            V((NF, K + 16, 128), F32),
            D((2,)),
            D((ITERS + 1, 2)),
            D((ITERS + 1, 2)),
            D((2 * ITERS, NN)),
            D((2 * ITERS, NN)),
            D((ITERS, NN)),
            D((ITERS, NN)),
            D((ITERS, NF)),
            D((ITERS, NF)),
            D((ITERS, NF)),
            D((ITERS, NF)),
            D((ITERS, NF)),
            D((ITERS, NF)),
            D((ITERS, NF)),
            D((ITERS, NF)),
            D((2,)),
            D((NN,)),
            D((NN,)),
            D((NF,)),
            D((NF,)),
        ],
        compiler_params=pltpu.CompilerParams(
            collective_id=0, has_side_effects=True, vmem_limit_bytes=50 << 20
        ),
    )


def per_device(calcium, trial_of_frame, trial_half, loadings, profiles):
    NN = lax.axis_size("neuron")
    NF = lax.axis_size("frame")
    N, T = calcium.shape
    small = (calcium, trial_of_frame.reshape(1, T), trial_half.reshape(1, -1))
    if NN == 4 and NF == 4 and N == K:
        call = wide_call(NN, NF, T, N, trial_half.shape[0])
        return emit(*call(*small, loadings[0], profiles[0]))
    w_groups = loadings[0].reshape(N, K, GROUPS, GL).transpose(2, 0, 3, 1).reshape(GROUPS, N, GW)
    wout, hout, sim = tall_call(NN, NF, T, N)(*small, w_groups, profiles[0])
    loads = wout.reshape(GROUPS, N, GL, K).transpose(1, 3, 0, 2).reshape(1, N, K * L)
    return loads, hout[None], sim[None]


def solution(mesh):
    placed = (
        P("neuron", "frame"),
        P("frame"),
        P(),
        P("half", "neuron", None),
        P("half", None, "frame"),
    )
    return jax.shard_map(
        per_device,
        mesh=mesh,
        in_specs=placed,
        out_specs=(P("half", "neuron", None), P("half", None, "frame"), P("half", None, None)),
        check_vma=False,
    )
```

```python
import functools

import jax
import jax.numpy as jnp
from jax import lax
from jax.experimental import pallas as pl
from jax.experimental.pallas import tpu as pltpu
from jax.sharding import PartitionSpec as P

K = 32
L = 64
ITERS = 2
EPS = 1e-06
RIM = 128
GROUPS = 8
GL = L // GROUPS
GW = GL * K
MESH = pl.DeviceIdType.MESH
F32 = jnp.float32
BF16 = jnp.bfloat16


def dot(a, b):
    return jnp.dot(a, b, preferred_element_type=F32)


def kernel(
    NN, NF, T,
    ca_ref, tof_ref, th_ref, w_ref, prof_ref,
    wout_ref, hout_ref, sim_ref,
    hs, hlag, mext, ms, mlag, alag, acc, accn, accd, hf, wg, wt, wown, stk,
    mrim_s, mrim_r, rim_s, rim_r, ndx, ndr, hall, ssr, wqx, wqr, wqs, wqt, wgb, wfin, pts, ptr, snr, sfr,
    mr_sem, rim_ss, rim_rs, nd_ss, nd_rs, hg_ss, hg_rs, ss_ss, ss_rs,
    ws_ss, ws_rs, wt_ss, wt_rs, wg_ss, wg_rs, pt_sem, sn_ss, sn_rs, sf_ss, sf_rs,
):
    me_n = lax.axis_index("neuron")
    me_f = lax.axis_index("frame")
    me_h = lax.axis_index("half")
    N = ca_ref.shape[0]
    EXT = T + RIM
    gp = GROUPS // NF
    rg = K // 8
    w = T * rg // NN
    pending = []

    def send(src, dst, ssem, rsem, axis, peer):
        c = pltpu.make_async_remote_copy(
            src_ref=src, dst_ref=dst, send_sem=ssem, recv_sem=rsem,
            device_id={axis: peer}, device_id_type=MESH,
        )
        c.start()
        pending.append(c)
        return c

    def npeer(r):
        return lax.rem(me_n + r, NN)

    def fpeer(r):
        return lax.rem(me_f + r, NF)

    barrier = pltpu.get_barrier_semaphore()
    for r in range(1, NN):
        pl.semaphore_signal(barrier, inc=1, device_id={"neuron": npeer(r)}, device_id_type=MESH)
    for r in range(1, NF):
        pl.semaphore_signal(barrier, inc=1, device_id={"frame": fpeer(r)}, device_id_type=MESH)
    pl.semaphore_signal(barrier, inc=1, device_id={"half": 1 - me_h}, device_id_type=MESH)

    trials = th_ref.shape[1]
    rows = lax.broadcasted_iota(jnp.int32, (trials, trials), 0)
    cols = lax.broadcasted_iota(jnp.int32, (trials, trials), 1)
    thf = th_ref[...].astype(F32)
    th_col = jnp.sum(jnp.where(rows == cols, thf, 0.0), axis=1, keepdims=True)
    chosen = jnp.where(th_col == me_h.astype(F32), 1.0, 0.0)
    hit = lax.broadcasted_iota(jnp.int32, (trials, T), 0) == tof_ref[...]
    mask = jnp.sum(jnp.where(hit, chosen, 0.0), axis=0, keepdims=True)
    masked = (ca_ref[...].astype(F32) * mask).astype(BF16)
    mext[:, :T] = masked
    mrim_s[...] = masked[:, :RIM]
    hf[...] = prof_ref[...]
    rim_s[0, 0] = prof_ref[:, :RIM]
    rim_s[0, 1] = prof_ref[:, T - RIM:]

    pl.semaphore_wait(barrier, (NN - 1) + (NF - 1) + 1)

    left = fpeer(NF - 1)
    right = fpeer(1)
    rims = {}

    def send_rims(i):
        rims[i] = (
            send(rim_s.at[i, 0], rim_r.at[i, 0], rim_ss.at[i, 0], rim_rs.at[i, 0], "frame", left),
            send(rim_s.at[i, 1], rim_r.at[i, 1], rim_ss.at[i, 1], rim_rs.at[i, 1], "frame", right),
        )

    send_rims(0)
    mcopy = send(mrim_s, mrim_r, mr_sem.at[0], mr_sem.at[1], "frame", left)

    for g in range(GROUPS):
        wg[g] = w_ref[g].astype(BF16)
    wown[...] = w_ref[pl.ds(me_f * gp, gp)]

    crow = (me_n % rg) * 8
    ccol = (me_n // rg) * w
    if NN == rg:
        hown = prof_ref[pl.ds(pl.multiple_of(crow, 8), 8), :]
    else:
        hown = prof_ref[pl.ds(pl.multiple_of(crow, 8), 8), pl.ds(pl.multiple_of(ccol, 128), w)]

    def own_rows(col):
        out = col[0:8]
        for q in range(1, rg):
            out = jnp.where(me_n % rg == q, col[q * 8:(q + 1) * 8], out)
        return out

    def build_right(width, lo=0, hi=GROUPS, extra=None):
        def body(g, _):
            v = hs[...]
            for b in range(GL):
                hlag[pl.ds(pl.multiple_of(g * GW + b * K, K), K), :width] = (
                    v[:, 2 * RIM - b:2 * RIM - b + width]
                )
            hs[:, RIM:] = v[:, RIM - GL:hs.shape[1] - GL]
            part = dot(wg[g], hlag[pl.ds(pl.multiple_of(g * GW, GW), GW), :width])
            acc[:, :width] = acc[:, :width] + part
            if extra is not None:
                extra(g)
            return 0

        if lo == 0:
            acc[...] = jnp.zeros_like(acc)
        lax.fori_loop(lo, hi, body, 0)

    def fill_hs(left_rim, body, right_rim):
        hs[:, :RIM] = jnp.zeros((K, RIM), BF16)
        hs[:, RIM:2 * RIM] = left_rim.astype(BF16)
        hs[:, 2 * RIM:2 * RIM + T] = body.astype(BF16)
        hs[:, 2 * RIM + T:] = right_rim.astype(BF16)

    def build_left(dst, g):
        v = ms[...]
        for b in range(GL):
            dst[pl.ds(pl.multiple_of(g * GW + b * N, N), N), :] = v[:, b:b + T]
        ms[:, :EXT] = v[:, GL:EXT + GL]

    mcopy.wait_recv()
    mext[:, T:] = mrim_r[...]
    ms[:, :EXT] = mext[...]
    ms[:, EXT:] = jnp.zeros((N, RIM), BF16)

    def mbody(g, _):
        build_left(mlag, g)
        return 0

    lax.fori_loop(0, GROUPS, mbody, 0)
    stk[:N] = mext[:, :T]
    mask_ext = jnp.where(mext[...].astype(F32) > 0.0, 1.0, 0.0)

    def send_sums(it, kind, src):
        for p in range(NN):
            a, b = (p % rg) * 8, (p // rg) * w
            ndx[it, kind, p] = src[a:a + 8, b:b + w]
        at = 2 * it + kind
        return [
            send(ndx.at[it, kind, npeer(r)], ndr.at[it, kind, r - 1], nd_ss.at[at, r], nd_rs.at[at, r],
                 "neuron", npeer(r))
            for r in range(1, NN)
        ]

    RQ = 2 * N // 4
    quad = lax.broadcasted_iota(jnp.int32, (RQ, 128), 1) // K
    wcs = {}

    def contract(rows_bf, g):
        rws = pl.ds(pl.multiple_of(g * GW, GW), GW)
        return lax.dot_general(
            rows_bf, hlag[rws, :T], (((1,), (1,)), ((), ())), preferred_element_type=F32
        )

    scale = None
    for it in range(ITERS):
        last = it == ITERS - 1
        def tbody(g, _):
            x = wg[g].astype(F32)
            for h in range(GW // 128):
                t = x[:, h * 128:(h + 1) * 128].T
                wt[g, :, h * 128:(h + 1) * 128] = jnp.concatenate(
                    [t[q * K:(q + 1) * K] for q in range(4)], axis=1
                ).astype(BF16)
            return 0

        lax.fori_loop(0, GROUPS, tbody, 0)

        accn[...] = jnp.zeros_like(accn)

        def nbody(g, _):
            accn[...] = accn[...] + dot(wt[g], mlag[pl.ds(pl.multiple_of(g * GW, GW), GW), :])
            return 0

        lax.fori_loop(0, GROUPS, nbody, 0)
        ncs = send_sums(it, 0, accn)
        if it == 0:
            for c in rims[it]:
                c.wait_recv()
            fill_hs(rim_r[it, 1], hf[...], rim_r[it, 0])
        else:
            rims[it][0].wait_recv()
            fill_hs(rim_r[it, 1] / scale, hf[...] / scale, rim_r[it, 0] / scale)
        build_right(EXT)
        approx = (acc[...].astype(BF16).astype(F32) * mask_ext).astype(BF16)
        ms[:, :EXT] = approx

        accd[...] = jnp.zeros_like(accd)

        def dbody(g, _):
            build_left(alag, g)
            rws = pl.ds(pl.multiple_of(g * GW, GW), GW)
            accd[...] = accd[...] + dot(wt[g], alag[rws, :])
            return 0

        lax.fori_loop(0, GROUPS, dbody, 0)
        dcs = send_sums(it, 1, accd)
        num = ndx[it, 0, me_n]
        den = ndx[it, 1, me_n]
        for r in range(1, NN):
            ncs[r - 1].wait_recv()
            num = num + ndr[it, 0, r - 1]
        for r in range(1, NN):
            dcs[r - 1].wait_recv()
            den = den + ndr[it, 1, r - 1]
        hown = hown * num / jnp.maximum(den, 1.0)
        hall[it, me_n] = hown
        cs = [
            send(hall.at[it, me_n], hall.at[it, me_n], hg_ss.at[it, r], hg_rs.at[it, r], "neuron", npeer(r))
            for r in range(1, NN)
        ]
        for c in cs:
            c.wait_recv()
        for p in range(NN):
            a, b = (p % rg) * 8, (p // rg) * w
            hf[a:a + 8, b:b + w] = hall[it, p]
        hnew = hf[...]
        rim_s[it + 1, 0] = hnew[:, :RIM]
        rim_s[it + 1, 1] = hnew[:, T - RIM:]
        send_rims(it + 1)
        sq = jnp.sum(hnew * hnew, axis=1, keepdims=True)
        ssr[it, me_f] = jnp.broadcast_to(sq, (K, 128))
        ssc = [
            send(ssr.at[it, me_f], ssr.at[it, me_f], ss_ss.at[it, r], ss_rs.at[it, r], "frame", fpeer(r))
            for r in range(1, NF)
        ]
        rims[it + 1][1].wait_recv()
        fill_hs(rim_r[it + 1, 1], hnew, hnew[:, :RIM])
        build_right(T)
        approx2 = (acc[:, :T].astype(BF16).astype(F32) * mask_ext[:, :T]).astype(BF16)
        stk[N:] = approx2
        for r in list(range(1, NF)) + [0]:
            p = fpeer(r)
            sums = [contract(stk[...], p * gp + q) for q in range(gp)]
            if r:
                top = sums[0][:, :128]
                for x in sums:
                    for h in range(GW // 128):
                        top = jnp.maximum(top, x[:, h * 128:(h + 1) * 128])
                top = jnp.maximum(top, pltpu.roll(top, 64, 1))
                top = jnp.maximum(top, pltpu.roll(top, 32, 1))
                inv = 65534.0 / jnp.maximum(top, 1e-30)
                inv = jnp.concatenate([inv] * (GW // 128), axis=1)
                for q in range(gp):
                    code = jnp.minimum(jnp.round(sums[q] * inv) - 32767.0, 32767.0)
                    wqx[it, r - 1, q] = code.astype(jnp.int32).astype(jnp.int16)
                packed = top[:RQ]
                for j in range(1, 4):
                    packed = jnp.where(quad == j, top[j * RQ:(j + 1) * RQ], packed)
                wqs[it, r - 1] = packed
                wcs[r - 1] = (
                    send(wqs.at[it, r - 1], wqt.at[it, r - 1], wt_ss.at[it, r], wt_rs.at[it, r], "frame", p),
                    send(wqx.at[it, r - 1], wqr.at[it, r - 1], ws_ss.at[it, r], ws_rs.at[it, r], "frame", p),
                )
            else:
                wtot = sums
        for c in ssc:
            c.wait_recv()
        total = ssr[it, 0]
        for p in range(1, NF):
            total = total + ssr[it, p]
        scale_wide = jnp.sqrt(total + EPS)
        scale = scale_wide[:, 0:1]
        ek = lax.broadcasted_iota(jnp.int32, (K, GW), 0)
        ec = lax.broadcasted_iota(jnp.int32, (K, GW), 1) % K
        scale_row = jnp.sum(jnp.where(ek == ec, scale, 0.0), axis=0, keepdims=True)
        hown = hown / own_rows(scale)
        for r in range(1, NF):
            for c in wcs[r - 1]:
                c.wait_recv()
            packed = wqt[it, r - 1]
            tops = []
            for j in range(4):
                t = jnp.where(quad == j, packed, 0.0)
                t = t + pltpu.roll(t, 64, 1)
                tops.append(t + pltpu.roll(t, 32, 1))
            unit = jnp.concatenate(tops, axis=0) * (1.0 / 65534.0)
            unit = jnp.concatenate([unit] * (GW // 128), axis=1)
            wtot = [
                wtot[q] + (wqr[it, r - 1, q].astype(jnp.int32).astype(F32) + 32767.0) * unit
                for q in range(gp)
            ]
        wnew = jnp.stack([wown[q] * wtot[q][:N] / wtot[q][N:] * scale_row for q in range(gp)])
        wown[...] = wnew
        mine = pl.ds(me_f * gp, gp)
        if not last:
            wgb[it, mine] = wnew.astype(BF16)
            cs = [
                send(wgb.at[it, mine], wgb.at[it, mine], wg_ss.at[it, r], wg_rs.at[it, r], "frame", fpeer(r))
                for r in range(1, NF)
            ]
            for c in cs:
                c.wait_recv()
            wg[...] = wgb[it]

    pts[...] = wnew.astype(BF16)
    ptc = send(pts, ptr, pt_sem.at[0], pt_sem.at[1], "half", 1 - me_h)
    wfin[mine] = wnew
    fcs = [
        send(wfin.at[mine], wfin.at[mine], wg_ss.at[ITERS - 1, r], wg_rs.at[ITERS - 1, r], "frame", fpeer(r))
        for r in range(1, NF)
    ]
    hout_ref[...] = hf[...] / scale
    ptc.wait_recv()
    far = ptr[...].astype(F32)
    cross = jnp.zeros((128, 128), F32)
    osq = jnp.zeros((1, 128), F32)
    fsq = jnp.zeros((1, 128), F32)
    for q in range(gp):
        for h in range(GW // 128):
            a = wnew[q, :, h * 128:(h + 1) * 128]
            b = far[q, :, h * 128:(h + 1) * 128]
            cross = cross + lax.dot_general(
                a, b, (((0,), (0,)), ((), ())),
                preferred_element_type=F32, precision=lax.Precision.HIGHEST,
            )
            osq = osq + jnp.sum(a * a, axis=0, keepdims=True)
            fsq = fsq + jnp.sum(b * b, axis=0, keepdims=True)
    ri = lax.broadcasted_iota(jnp.int32, (128, 128), 0)
    ci = lax.broadcasted_iota(jnp.int32, (128, 128), 1)
    cross = jnp.where(ri // K == ci // K, cross, 0.0)
    cross = cross[0:K] + cross[K:2 * K] + cross[2 * K:3 * K] + cross[3 * K:]

    def fold(x):
        x = x + pltpu.roll(x, 64, 1)
        return x + pltpu.roll(x, 32, 1)

    pack = jnp.concatenate(
        [cross, jnp.broadcast_to(osq, (8, 128)), jnp.broadcast_to(fsq, (8, 128))], axis=0
    )
    snr[me_n] = fold(pack)
    cs = [
        send(snr.at[me_n], snr.at[me_n], sn_ss.at[r], sn_rs.at[r], "neuron", npeer(r))
        for r in range(1, NN)
    ]
    for c in cs:
        c.wait_recv()
    tot = snr[0]
    for p in range(1, NN):
        tot = tot + snr[p]
    sfr[me_f] = tot
    cs = [
        send(sfr.at[me_f], sfr.at[me_f], sf_ss.at[r], sf_rs.at[r], "frame", fpeer(r))
        for r in range(1, NF)
    ]
    for c in fcs:
        c.wait_recv()
    wout_ref[...] = wfin[...]
    for c in cs:
        c.wait_recv()
    tot = sfr[0]
    for p in range(1, NF):
        tot = tot + sfr[p]
    own_row = tot[K:K + 1]
    far_row = tot[K + 8:K + 9]
    rk = lax.broadcasted_iota(jnp.int32, (K, 128), 0)
    ck = lax.broadcasted_iota(jnp.int32, (K, 128), 1)
    own_col = jnp.sum(jnp.where(rk == ck, own_row, 0.0), axis=1, keepdims=True)
    sim = tot[:K] / jnp.sqrt((own_col + EPS) * (far_row + EPS))
    sim_ref[...] = sim[:, :K]
    rims[ITERS][0].wait_recv()
    for c in pending:
        c.wait_send()


def roll_right(x, s):
    return pltpu.roll(x, s, 1) if s else x


def roll_left(x, s):
    return pltpu.roll(x, x.shape[1] - s, 1) if s else x


def wide_kernel(
    NN, NF, T,
    ca_hbm, tof_hbm, th_hbm, w_hbm, prof_hbm,
    wout_ref, hout_ref, sim_ref,
    ca_ref, tof_ref, th_ref, w_ref, prof_ref, by_lag, wf,
    rim_s, rim_r, mtx, mrx, w32, wt32, hla, mla, ala, qs, ps,
    ndx, ndr, hb, hl, ml, al, dat, md, prx, acc, own, tx, rx, topx, topr,
    hg, wtx, wtr, wcx, wcr, far_s, far_r, snx, snr,
    isem, ssem, rsem,
):
    me_n = lax.axis_index("neuron")
    me_f = lax.axis_index("frame")
    me_h = lax.axis_index("half")
    me_c = lax.rem(me_n, 2)
    me_y = me_n // 2
    N = ca_ref.shape[0]
    F = NF * T
    NB = N // NF
    KC = K // 2
    TC = T // 2
    EXT = T + RIM
    pending = []

    def send(src, dst, peer):
        i = len(pending)
        c = pltpu.make_async_remote_copy(
            src_ref=src, dst_ref=dst, send_sem=ssem.at[i], recv_sem=rsem.at[i],
            device_id=peer, device_id_type=MESH,
        )
        c.start()
        pending.append(c)
        return c

    def npeer(r):
        return lax.rem(me_n + r, NN)

    def fpeer(r):
        return lax.rem(me_f + r, NF)

    core = {"neuron": me_n + 1 - 2 * me_c}
    seven = [(dy, dz) for dz in (3, 2, 1, 0) for dy in (1, 0) if dy or dz]

    def block_of(dy, dz):
        return fpeer(dz) * 2 + lax.rem(me_y + dy, 2)

    def to(dy, dz):
        return {"neuron": npeer(2 * dy), "frame": fpeer(dz)}

    others = [(dn, df) for df in (3, 2, 1, 0) for dn in (3, 2, 1, 0) if dn or df]
    barrier = pltpu.get_barrier_semaphore()
    for dn, df in others:
        pl.semaphore_signal(
            barrier, inc=1, device_id={"neuron": npeer(dn), "frame": fpeer(df)}, device_id_type=MESH
        )
    pl.semaphore_signal(barrier, inc=1, device_id={"half": 1 - me_h}, device_id_type=MESH)

    loads = [
        pltpu.make_async_copy(a, b, isem.at[i])
        for i, (a, b) in enumerate([
            (th_hbm, th_ref), (tof_hbm, tof_ref), (ca_hbm, ca_ref), (prof_hbm, prof_ref), (w_hbm, w_ref),
        ])
    ]
    for c in loads:
        c.start()

    def turn(x):
        out = []
        for h in range(GW // 128):
            t = x[:, h * 128:(h + 1) * 128].T
            out.append(jnp.concatenate([t[q * K:(q + 1) * K] for q in range(4)], axis=1))
        return jnp.concatenate(out, axis=1)

    for c in loads[:-1]:
        c.wait()

    trials = th_ref.shape[1]
    rows = lax.broadcasted_iota(jnp.int32, (trials, trials), 0)
    cols = lax.broadcasted_iota(jnp.int32, (trials, trials), 1)
    thf = th_ref[...].astype(F32)
    th_col = jnp.sum(jnp.where(rows == cols, thf, 0.0), axis=1, keepdims=True)
    chosen = jnp.where(th_col == me_h.astype(F32), 1.0, 0.0)
    hit = lax.broadcasted_iota(jnp.int32, (trials, T), 0) == tof_ref[...]
    mask = jnp.sum(jnp.where(hit, chosen, 0.0), axis=0, keepdims=True)
    masked = ca_ref[...].astype(F32) * mask
    body = masked.astype(BF16)
    prof = prof_ref[...].astype(BF16)
    rim_s[0, :N] = body[:, :RIM]
    rim_s[0, N:] = prof[:, :RIM]
    rim_s[1, :K] = prof[:, T - RIM:]
    for z in range(NF):
        x = masked[z * NB:(z + 1) * NB]
        mtx[z] = jnp.concatenate([x[:, :TC], x[:, TC:]], axis=0).astype(BF16)

    loads[-1].wait()
    for j in range(K * L // 128):
        by_lag[j * 128:(j + 1) * 128, :N] = w_ref[:, j * 128:(j + 1) * 128].T

    def lay_out(lo, hi):
        for a in range(lo, hi):
            x = jnp.concatenate(
                [by_lag[pl.ds(a * GL + b, K, stride=L), :][:, :N] for b in range(GL)], axis=1
            )
            wt32[a * K:(a + 1) * K] = x.astype(BF16)
            x = turn(x)
            wf[a] = x
            w32[a * N:(a + 1) * N] = x.astype(BF16)

    lay_out(0, 4)
    pl.semaphore_wait(barrier, len(others) + 1)

    to_left = send(rim_s.at[0], rim_r.at[0], {"frame": fpeer(NF - 1)})
    to_right = send(rim_s.at[1, pl.ds(0, K)], rim_r.at[1, pl.ds(0, K)], {"frame": fpeer(1)})
    mcs = [
        send(mtx.at[fpeer(r)], mrx.at[me_f], {"frame": fpeer(r)})
        for r in (3, 2, 1)
    ]
    mrx[me_f] = mtx[me_f]

    lay_out(4, GROUPS)
    mine = pl.ds(pl.multiple_of(me_f * NB, NB), NB)
    w8 = jnp.concatenate([wf[a, mine, :] for a in range(GROUPS)], axis=0)

    def lags(dst, x, roll, lo=0, hi=None, at=0):
        n = x.shape[0]
        hi = x.shape[1] if hi is None else hi
        for b in range(GL):
            dst[b * n:(b + 1) * n, at:at + hi - lo] = roll(x, b)[:, lo:hi]

    IN = T - RIM
    lags(mla, body, roll_left, 0, IN)
    qs[:, :IN] = dot(wt32[...], mla[:, :IN])
    lags(hla, prof, roll_right, RIM, T, 2 * RIM)
    ps[:, 2 * RIM:EXT] = dot(w32[...], hla[:, 2 * RIM:EXT])

    to_left.wait_recv()
    mext = jnp.concatenate([body, rim_r[0, :N]], axis=1)
    mask_ext = jnp.where(mext.astype(F32) > 0.0, 1.0, 0.0)

    def shifted_sum(q):
        s = q[:K]
        for a in range(1, GROUPS):
            s = s + roll_left(q[a * K:(a + 1) * K], a * GL)
        return s[:, :T]

    def scatter(kind, s):
        for p in range(NN):
            a, b = (p % 2) * KC, (p // 2) * TC
            ndx[kind, p] = s[a:a + KC, b:b + TC]
        return [
            send(ndx.at[kind, npeer(r)], ndr.at[kind, r - 1], {"neuron": npeer(r)})
            for r in range(1, NN)
        ]

    lags(mla, mext[:, IN:], roll_left, at=IN)
    qs[:, IN:] = dot(wt32[...], mla[:, IN:])
    lags(hla, jnp.concatenate([prof[:, IN:], rim_r[0, N:]], axis=1), roll_right, RIM, 2 * RIM, EXT)
    ps[:, EXT:] = dot(w32[...], hla[:, EXT:])
    ncs = scatter(0, shifted_sum(qs[...]))
    to_right.wait_recv()
    lags(hla, jnp.concatenate([rim_r[1, :K], prof[:, :RIM]], axis=1), roll_right)
    ps[:, :2 * RIM] = dot(w32[...], hla[:, :2 * RIM])
    p = ps[...]
    s = p[:N]
    for a in range(1, GROUPS):
        s = s + roll_right(p[a * N:(a + 1) * N], a * GL)
    approx = (s[:, RIM:].astype(BF16).astype(F32) * mask_ext).astype(BF16)
    lags(ala, approx, roll_left)
    dcs = scatter(1, shifted_sum(dot(wt32[...], ala[...])))

    own_rows = pl.ds(pl.multiple_of(me_c * KC, KC), KC)
    far_rows = pl.ds(pl.multiple_of((1 - me_c) * KC, KC), KC)
    hown = prof_ref[own_rows, pl.ds(pl.multiple_of(me_y * TC, TC), TC)]
    num = ndx[0, me_n]
    den = ndx[1, me_n]
    for r in range(1, NN):
        ncs[r - 1].wait_recv()
        num = num + ndr[0, r - 1]
    for r in range(1, NN):
        dcs[r - 1].wait_recv()
        den = den + ndr[1, r - 1]
    hown = hown * num / jnp.maximum(den, 1.0)

    def spot(c, blk):
        return pl.ds(pl.multiple_of(c * KC, KC), KC), pl.ds(pl.multiple_of(blk * TC, TC), TC)

    lane = lax.broadcasted_iota(jnp.int32, (8, 128), 1)

    def gather_h(it):
        a, b = spot(me_c, block_of(0, 0))
        hb[it, a, b] = hown.astype(BF16)
        cs = [send(hb.at[it, a, b], hb.at[it, a, b], to(dy, dz)) for dy, dz in seven]
        relays = [send(hb.at[it, a, b], hb.at[it, a, b], core)]
        return cs, relays

    def half_lags(it, rows_of, c):
        x = hb[it, rows_of, :]
        for b in range(GL):
            hl[pl.ds(pl.multiple_of(b * K + c * KC, KC), KC), :] = roll_right(x, b)

    def relay_h(it, cs, relays):
        for i in range(len(seven) - 1, -1, -1):
            cs[i].wait_recv()
            dy, dz = seven[i]
            a, b = spot(me_c, block_of(dy, NF - dz))
            relays.append(send(hb.at[it, a, b], hb.at[it, a, b], core))
        half_lags(it, own_rows, me_c)
        for c in relays:
            c.wait_recv()
        half_lags(it, far_rows, 1 - me_c)

    def squares(it):
        x = hb[it].astype(F32)
        return jnp.sum(x * x, axis=1, keepdims=True)

    cs, relays = gather_h(0)

    for c in mcs:
        c.wait_recv()
    for z in range(NF):
        x = mrx[z].astype(F32)
        md[:, z * T:z * T + TC] = x[:NB]
        md[:, z * T + TC:(z + 1) * T] = x[NB:]
    data = md[...]
    mask_all = jnp.where(data[0:1] > 0.0, 1.0, 0.0)
    rolled = [roll_left(data, a * GL) for a in range(GROUPS)]
    for a in range(GROUPS):
        dat[a * 2 * NB:a * 2 * NB + NB] = rolled[a]
    lags(ml, jnp.concatenate(rolled[:4], axis=0).astype(BF16), roll_left)

    def recon(wb):
        p = dot(wb, hl[...])
        s = p[:NB]
        for a in range(1, GROUPS):
            s = s + roll_right(p[a * NB:(a + 1) * NB], a * GL)
        return s.astype(BF16).astype(F32) * mask_all

    def corr(wt, m):
        q = dot(wt, m[...])
        return q[:K] + roll_left(q[K:], 4 * GL)

    def template_ratio():
        approx = recon(w8.astype(BF16))
        for a in range(GROUPS):
            dat[a * 2 * NB + NB:(a + 1) * 2 * NB] = roll_left(approx, a * GL)
        s = lax.dot_general(
            dat[...].astype(BF16), hl[...], (((1,), (1,)), ((), ())), preferred_element_type=F32
        )
        wnum = jnp.concatenate([s[a * 2 * NB:a * 2 * NB + NB] for a in range(GROUPS)], axis=0)
        wden = jnp.concatenate([s[a * 2 * NB + NB:(a + 1) * 2 * NB] for a in range(GROUPS)], axis=0)
        return wnum, wden

    relay_h(0, cs, relays)
    wnum, wden = template_ratio()
    w8 = w8 * wnum / wden

    wt = jnp.concatenate([turn(w8[:4 * NB]), turn(w8[4 * NB:])], axis=0).astype(BF16)

    def reduce_start(kind, s):
        acc[kind] = s
        return send(acc.at[kind, far_rows], prx.at[kind], core)

    def reduce_spread(kind, c):
        c.wait_recv()
        s = acc[kind, own_rows, :] + prx[kind]
        own[kind] = s
        top = jnp.maximum(jnp.max(s, axis=1, keepdims=True), 1e-30)
        topx[kind] = jnp.sum(jnp.where(eye, top, 0.0), axis=0, keepdims=True)
        ts = [send(topx.at[kind], topr.at[kind * 7 + i], to(dy, dz)) for i, (dy, dz) in enumerate(seven)]
        code = jnp.round(s * (65534.0 / top)) - 32767.0
        tx[kind] = jnp.minimum(code, 32767.0).astype(jnp.int32).astype(jnp.int16)
        return ts, [
            send(
                tx.at[kind, :, pl.ds(pl.multiple_of(block_of(dy, dz) * TC, TC), TC)],
                rx.at[kind, i], to(dy, dz),
            )
            for i, (dy, dz) in enumerate(seven)
        ]

    def reduce_done(kind, sent):
        ts, cs = sent
        t = own[kind, :, pl.ds(pl.multiple_of(block_of(0, 0) * TC, TC), TC)]
        for i in range(len(seven) - 1, -1, -1):
            ts[i].wait_recv()
            unit = jnp.sum(jnp.where(eye, topr[kind * 7 + i], 0.0), axis=1, keepdims=True) * (1.0 / 65534.0)
            cs[i].wait_recv()
            t = t + (rx[kind, i].astype(jnp.int32).astype(F32) + 32767.0) * unit
        return t

    eye = lax.broadcasted_iota(jnp.int32, (KC, 128), 0) == lax.broadcasted_iota(jnp.int32, (KC, 128), 1)
    nc = reduce_start(0, corr(wt, ml))
    approx = recon(w8.astype(BF16))
    ncs = reduce_spread(0, nc)
    lags(al, jnp.concatenate([roll_left(approx, a * GL) for a in range(4)], axis=0).astype(BF16), roll_left)
    dc = reduce_start(1, corr(wt, al))
    scale0 = jnp.sqrt(squares(0) + EPS)
    dcs = reduce_spread(1, dc)
    num = reduce_done(0, ncs)
    den = reduce_done(1, dcs)
    s0 = jnp.where(me_c == 0, scale0[:KC], scale0[KC:])
    hown = hown * (num * s0) / jnp.maximum(den * s0, 1.0)
    cs, relays = gather_h(1)
    hg[me_n] = hown
    hcs = [send(hg.at[me_n], hg.at[me_n], {"neuron": npeer(r)}) for r in (3, 2, 1)]
    relay_h(1, cs, relays)
    wnum, wden = template_ratio()
    scale = jnp.sqrt(squares(1) + EPS * scale0 * scale0)
    ek = lax.broadcasted_iota(jnp.int32, (K, GW), 0)
    ec = lax.broadcasted_iota(jnp.int32, (K, GW), 1) % K
    scale_row = jnp.sum(jnp.where(ek == ec, scale, 0.0), axis=0, keepdims=True)
    w8 = w8 * wnum / wden * scale_row

    far_s[...] = w8.astype(BF16)
    fc = send(far_s, far_r, {"half": 1 - me_h})
    for q in range(2):
        t = turn(w8[q * 4 * NB:(q + 1) * 4 * NB])
        for b in range(GL):
            for a in range(4):
                at = b * K + a * NB
                by_lag[pl.ds(q * 4 * GL + a * GL + b, K, stride=L), :NB] = t[:, at:at + NB]
    x = jnp.concatenate(
        [by_lag[j * 128:(j + 1) * 128, :NB].T for j in range(K * L // 128)], axis=1
    )
    top = jnp.maximum(jnp.max(x, axis=1, keepdims=True), 1e-30)
    wtx[...] = jnp.sum(jnp.where(eye[:NB], top, 0.0), axis=0, keepdims=True)
    x = jnp.minimum(jnp.round(x * (65534.0 / top)) - 32767.0, 32767.0)
    half = K * L // 2
    wcx[...] = jnp.concatenate([x[:, :half], x[:, half:]], axis=0).astype(jnp.int32).astype(jnp.int16)
    wcs = [
        (
            send(wtx, wtr.at[r - 1], {"frame": fpeer(r)}),
            send(wcx, wcr.at[r - 1], {"frame": fpeer(r)}),
        )
        for r in (3, 2, 1)
    ]

    def place(z, code, top_row):
        unit = jnp.sum(jnp.where(eye[:NB], top_row, 0.0), axis=1, keepdims=True) * (1.0 / 65534.0)
        y = (code.astype(jnp.int32).astype(F32) + 32767.0)
        at = pl.ds(pl.multiple_of(z * NB, NB), NB)
        wout_ref[at, :half] = y[:NB] * unit
        wout_ref[at, half:] = y[NB:] * unit

    place(me_f, wcx[...], wtx[...])
    for c in hcs:
        c.wait_recv()
    for p in range(NN):
        a, b = (p % 2) * KC, (p // 2) * TC
        hout_ref[a:a + KC, b:b + TC] = hg[p] / scale[a:a + KC]
    fc.wait_recv()
    far = far_r[...].astype(F32)
    cross = jnp.zeros((128, 128), F32)
    osq = jnp.zeros((1, 128), F32)
    fsq = jnp.zeros((1, 128), F32)
    for h in range(GW // 128):
        a = w8[:, h * 128:(h + 1) * 128]
        b = far[:, h * 128:(h + 1) * 128]
        cross = cross + lax.dot_general(
            a, b, (((0,), (0,)), ((), ())),
            preferred_element_type=F32, precision=lax.Precision.HIGHEST,
        )
        osq = osq + jnp.sum(a * a, axis=0, keepdims=True)
        fsq = fsq + jnp.sum(b * b, axis=0, keepdims=True)
    ri = lax.broadcasted_iota(jnp.int32, (128, 128), 0)
    ci = lax.broadcasted_iota(jnp.int32, (128, 128), 1)
    cross = jnp.where(ri // K == ci // K, cross, 0.0)
    cross = cross[0:K] + cross[K:2 * K] + cross[2 * K:3 * K] + cross[3 * K:]

    def fold(x):
        x = x + pltpu.roll(x, 64, 1)
        return x + pltpu.roll(x, 32, 1)

    cross = fold(cross)
    quad = lane // K
    pack = cross[:8]
    for q in range(1, 4):
        pack = jnp.where(quad == q, cross[q * 8:(q + 1) * 8], pack)
    for q in range(8):
        snx[:, q * 128:(q + 1) * 128] = pack[q:q + 1]
    snx[:, 8 * 128:] = jnp.where(quad[:1] < 2, fold(osq), fold(fsq))
    scs = [
        send(snx, snr.at[i], {"neuron": npeer(dn), "frame": fpeer(df)})
        for i, (dn, df) in enumerate(others)
    ]
    for i, r in enumerate((3, 2, 1)):
        for c in wcs[i]:
            c.wait_recv()
        place(fpeer(NF - r), wcr[r - 1], wtr[r - 1])
    tot = snx[...]
    for i in range(len(others) - 1, -1, -1):
        scs[i].wait_recv()
        tot = tot + snr[i]
    own_row = tot[:, 8 * 128:]
    far_row = pltpu.roll(own_row, 64, 1)
    tot = jnp.concatenate([tot[:, q * 128:(q + 1) * 128] for q in range(8)], axis=0)
    rk = lax.broadcasted_iota(jnp.int32, (K, 128), 0)
    ck = lax.broadcasted_iota(jnp.int32, (K, 128), 1)
    own_col = jnp.sum(jnp.where(rk == ck, own_row, 0.0), axis=1, keepdims=True)
    full = jnp.concatenate(
        [tot] + [pltpu.roll(tot, 128 - q * K, 1) for q in range(1, 4)], axis=0
    )
    sim = full / jnp.sqrt((own_col + EPS) * (far_row + EPS))
    sim_ref[...] = sim[:, :K]
    for c in pending:
        c.wait_send()


def wide_call(NN, NF, T, N, trials):
    F = NF * T
    NB = N // NF
    KC = K // 2
    TC = T // 2
    EXT = T + RIM
    V = pltpu.VMEM
    D = pltpu.SemaphoreType.DMA
    vmem = pl.BlockSpec(memory_space=pltpu.VMEM)
    return pl.pallas_call(
        functools.partial(wide_kernel, NN, NF, T),
        out_shape=(
            jax.ShapeDtypeStruct((N, K * L), F32),
            jax.ShapeDtypeStruct((K, T), F32),
            jax.ShapeDtypeStruct((K, K), F32),
        ),
        in_specs=[pl.BlockSpec(memory_space=pl.ANY)] * 5,
        out_specs=(vmem,) * 3,
        scratch_shapes=[
            V((N, T), BF16),
            V((1, T), jnp.int32),
            V((1, trials), jnp.int32),
            V((N, K * L), F32),
            V((K, T), F32),
            V((K * L, 128), F32),
            V((GROUPS, N, GW), F32),
            V((2, N + K, RIM), BF16),
            V((2, N + K, RIM), BF16),
            V((NF, 2 * NB, TC), BF16),
            V((NF, 2 * NB, TC), BF16),
            V((GROUPS * N, GW), BF16),
            V((GROUPS * K, GW), BF16),
            V((GW, EXT + RIM), BF16),
            V((GW, EXT), BF16),
            V((GW, EXT), BF16),
            V((GROUPS * K, EXT), F32),
            V((GROUPS * N, EXT + RIM), F32),
            V((2, NN, KC, TC), F32),
            V((2, NN - 1, KC, TC), F32),
            V((ITERS, K, F), BF16),
            V((GW, F), BF16),
            V((GW, F), BF16),
            V((GW, F), BF16),
            V((2 * GROUPS * NB, F), F32),
            V((NB, F), F32),
            V((2, KC, F), F32),
            V((2, K, F), F32),
            V((2, KC, F), F32),
            V((2, KC, F), jnp.int16),
            V((2, 7, KC, TC), jnp.int16),
            V((2, 1, 128), F32),
            V((14, 1, 128), F32),
            V((NN, KC, TC), F32),
            V((1, 128), F32),
            V((NF - 1, 1, 128), F32),
            V((2 * NB, K * L // 2), jnp.int16),
            V((NF - 1, 2 * NB, K * L // 2), jnp.int16),
            V((GROUPS * NB, GW), BF16),
            V((GROUPS * NB, GW), BF16),
            V((1, 9 * 128), F32),
            V((NN * NF - 1, 1, 9 * 128), F32),
            D((5,)),
            D((104,)),
            D((104,)),
        ],
        compiler_params=pltpu.CompilerParams(
            collective_id=1, has_side_effects=True, vmem_limit_bytes=56 << 20
        ),
    )


def emit_kernel(w_ref, h_ref, s_ref, w_out, h_out, s_out, sem):
    pairs = [(h_ref, h_out.at[0]), (s_ref, s_out.at[0])]
    step = w_ref.shape[1] // 2
    for r in range(w_ref.shape[0] // 8):
        for q in range(2):
            part = (pl.ds(r * 8, 8), pl.ds(q * step, step))
            pairs.append((w_ref.at[part], w_out.at[0].at[part]))
    cs = [pltpu.make_async_copy(a, b, sem.at[i]) for i, (a, b) in enumerate(pairs)]
    for c in cs:
        c.start()
    for c in cs:
        c.wait()


def emit(*arrays):
    return pl.pallas_call(
        emit_kernel,
        out_shape=tuple(jax.ShapeDtypeStruct((1, *x.shape), F32) for x in arrays),
        in_specs=[pl.BlockSpec(memory_space=pltpu.VMEM)] * 3,
        out_specs=(pl.BlockSpec(memory_space=pl.ANY),) * 3,
        scratch_shapes=[pltpu.SemaphoreType.DMA((2 + arrays[0].shape[0] // 4,))],
    )(*arrays)


def tall_call(NN, NF, T, N):
    gp = GROUPS // NF
    rg = K // 8
    w = T * rg // NN
    EXT = T + RIM
    V = pltpu.VMEM
    D = pltpu.SemaphoreType.DMA
    vmem = pl.BlockSpec(memory_space=pltpu.VMEM)
    return pl.pallas_call(
        functools.partial(kernel, NN, NF, T),
        out_shape=(
            jax.ShapeDtypeStruct((GROUPS, N, GW), F32),
            jax.ShapeDtypeStruct((K, T), F32),
            jax.ShapeDtypeStruct((K, K), F32),
        ),
        in_specs=[vmem] * 5,
        out_specs=(vmem,) * 3,
        scratch_shapes=[
            V((K, 2 * RIM + T + RIM), BF16),
            V((L * K, EXT), BF16),
            V((N, EXT), BF16),
            V((N, EXT + RIM), BF16),
            V((L * N, T), BF16),
            V((L * N, T), BF16),
            V((N, EXT), F32),
            V((K, T), F32),
            V((K, T), F32),
            V((K, T), F32),
            V((GROUPS, N, GW), BF16),
            V((GROUPS, K, GW), BF16),
            V((gp, N, GW), F32),
            V((2 * N, T), BF16),
            V((N, RIM), BF16),
            V((N, RIM), BF16),
            V((ITERS + 1, 2, K, RIM), F32),
            V((ITERS + 1, 2, K, RIM), F32),
            V((ITERS, 2, NN, 8, w), F32),
            V((ITERS, 2, NN - 1, 8, w), F32),
            V((ITERS, NN, 8, w), F32),
            V((ITERS, NF, K, 128), F32),
            V((ITERS, NF - 1, gp, 2 * N, GW), jnp.int16),
            V((ITERS, NF - 1, gp, 2 * N, GW), jnp.int16),
            V((ITERS, NF - 1, 2 * N // 4, 128), F32),
            V((ITERS, NF - 1, 2 * N // 4, 128), F32),
            V((ITERS - 1, GROUPS, N, GW), BF16),
            V((GROUPS, N, GW), F32),
            V((gp, N, GW), BF16),
            V((gp, N, GW), BF16),
            V((NN, K + 16, 128), F32),
            V((NF, K + 16, 128), F32),
            D((2,)),
            D((ITERS + 1, 2)),
            D((ITERS + 1, 2)),
            D((2 * ITERS, NN)),
            D((2 * ITERS, NN)),
            D((ITERS, NN)),
            D((ITERS, NN)),
            D((ITERS, NF)),
            D((ITERS, NF)),
            D((ITERS, NF)),
            D((ITERS, NF)),
            D((ITERS, NF)),
            D((ITERS, NF)),
            D((ITERS, NF)),
            D((ITERS, NF)),
            D((2,)),
            D((NN,)),
            D((NN,)),
            D((NF,)),
            D((NF,)),
        ],
        compiler_params=pltpu.CompilerParams(
            collective_id=0, has_side_effects=True, vmem_limit_bytes=50 << 20
        ),
    )


def per_device(calcium, trial_of_frame, trial_half, loadings, profiles):
    NN = lax.axis_size("neuron")
    NF = lax.axis_size("frame")
    N, T = calcium.shape
    small = (calcium, trial_of_frame.reshape(1, T), trial_half.reshape(1, -1))
    if NN == 4 and NF == 4 and N == K:
        call = wide_call(NN, NF, T, N, trial_half.shape[0])
        return emit(*call(*small, loadings[0], profiles[0]))
    w_groups = loadings[0].reshape(N, K, GROUPS, GL).transpose(2, 0, 3, 1).reshape(GROUPS, N, GW)
    wout, hout, sim = tall_call(NN, NF, T, N)(*small, w_groups, profiles[0])
    loads = wout.reshape(GROUPS, N, GL, K).transpose(1, 3, 0, 2).reshape(1, N, K * L)
    return loads, hout[None], sim[None]


def solution(mesh):
    placed = (
        P("neuron", "frame"),
        P("frame"),
        P(),
        P("half", "neuron", None),
        P("half", None, "frame"),
    )
    return jax.shard_map(
        per_device,
        mesh=mesh,
        in_specs=placed,
        out_specs=(P("half", "neuron", None), P("half", None, "frame"), P("half", None, None)),
        check_vma=False,
    )
```

```python
import functools

import jax
import jax.numpy as jnp
from jax import lax
from jax.experimental import pallas as pl
from jax.experimental.pallas import tpu as pltpu
from jax.sharding import PartitionSpec as P

K = 32
L = 64
ITERS = 2
EPS = 1e-06
RIM = 128
GROUPS = 8
GL = L // GROUPS
GW = GL * K
MESH = pl.DeviceIdType.MESH
F32 = jnp.float32
BF16 = jnp.bfloat16


def dot(a, b):
    return jnp.dot(a, b, preferred_element_type=F32)


def kernel(
    NN, NF, T,
    ca_ref, tof_ref, th_ref, w_ref, prof_ref,
    wout_ref, hout_ref, sim_ref,
    hs, hlag, mext, ms, mlag, alag, acc, accn, accd, hf, wg, wt, wown, stk,
    mrim_s, mrim_r, rim_s, rim_r, ndx, ndr, hall, ssr, wqx, wqr, wqs, wqt, wgb, wfin, pts, ptr, snr, sfr,
    mr_sem, rim_ss, rim_rs, nd_ss, nd_rs, hg_ss, hg_rs, ss_ss, ss_rs,
    ws_ss, ws_rs, wt_ss, wt_rs, wg_ss, wg_rs, pt_sem, sn_ss, sn_rs, sf_ss, sf_rs,
):
    me_n = lax.axis_index("neuron")
    me_f = lax.axis_index("frame")
    me_h = lax.axis_index("half")
    N = ca_ref.shape[0]
    EXT = T + RIM
    gp = GROUPS // NF
    rg = K // 8
    w = T * rg // NN
    pending = []

    def send(src, dst, ssem, rsem, axis, peer):
        c = pltpu.make_async_remote_copy(
            src_ref=src, dst_ref=dst, send_sem=ssem, recv_sem=rsem,
            device_id={axis: peer}, device_id_type=MESH,
        )
        c.start()
        pending.append(c)
        return c

    def npeer(r):
        return lax.rem(me_n + r, NN)

    def fpeer(r):
        return lax.rem(me_f + r, NF)

    barrier = pltpu.get_barrier_semaphore()
    for r in range(1, NN):
        pl.semaphore_signal(barrier, inc=1, device_id={"neuron": npeer(r)}, device_id_type=MESH)
    for r in range(1, NF):
        pl.semaphore_signal(barrier, inc=1, device_id={"frame": fpeer(r)}, device_id_type=MESH)
    pl.semaphore_signal(barrier, inc=1, device_id={"half": 1 - me_h}, device_id_type=MESH)

    trials = th_ref.shape[1]
    rows = lax.broadcasted_iota(jnp.int32, (trials, trials), 0)
    cols = lax.broadcasted_iota(jnp.int32, (trials, trials), 1)
    thf = th_ref[...].astype(F32)
    th_col = jnp.sum(jnp.where(rows == cols, thf, 0.0), axis=1, keepdims=True)
    chosen = jnp.where(th_col == me_h.astype(F32), 1.0, 0.0)
    hit = lax.broadcasted_iota(jnp.int32, (trials, T), 0) == tof_ref[...]
    mask = jnp.sum(jnp.where(hit, chosen, 0.0), axis=0, keepdims=True)
    masked = (ca_ref[...].astype(F32) * mask).astype(BF16)
    mext[:, :T] = masked
    mrim_s[...] = masked[:, :RIM]
    hf[...] = prof_ref[...]
    rim_s[0, 0] = prof_ref[:, :RIM]
    rim_s[0, 1] = prof_ref[:, T - RIM:]

    pl.semaphore_wait(barrier, (NN - 1) + (NF - 1) + 1)

    left = fpeer(NF - 1)
    right = fpeer(1)
    rims = {}

    def send_rims(i):
        rims[i] = (
            send(rim_s.at[i, 0], rim_r.at[i, 0], rim_ss.at[i, 0], rim_rs.at[i, 0], "frame", left),
            send(rim_s.at[i, 1], rim_r.at[i, 1], rim_ss.at[i, 1], rim_rs.at[i, 1], "frame", right),
        )

    send_rims(0)
    mcopy = send(mrim_s, mrim_r, mr_sem.at[0], mr_sem.at[1], "frame", left)

    for g in range(GROUPS):
        wg[g] = w_ref[g].astype(BF16)
    wown[...] = w_ref[pl.ds(me_f * gp, gp)]

    crow = (me_n % rg) * 8
    ccol = (me_n // rg) * w
    if NN == rg:
        hown = prof_ref[pl.ds(pl.multiple_of(crow, 8), 8), :]
    else:
        hown = prof_ref[pl.ds(pl.multiple_of(crow, 8), 8), pl.ds(pl.multiple_of(ccol, 128), w)]

    def own_rows(col):
        out = col[0:8]
        for q in range(1, rg):
            out = jnp.where(me_n % rg == q, col[q * 8:(q + 1) * 8], out)
        return out

    def build_right(width, lo=0, hi=GROUPS, extra=None):
        def body(g, _):
            v = hs[...]
            for b in range(GL):
                hlag[pl.ds(pl.multiple_of(g * GW + b * K, K), K), :width] = (
                    v[:, 2 * RIM - b:2 * RIM - b + width]
                )
            hs[:, RIM:] = v[:, RIM - GL:hs.shape[1] - GL]
            part = dot(wg[g], hlag[pl.ds(pl.multiple_of(g * GW, GW), GW), :width])
            acc[:, :width] = acc[:, :width] + part
            if extra is not None:
                extra(g)
            return 0

        if lo == 0:
            acc[...] = jnp.zeros_like(acc)
        lax.fori_loop(lo, hi, body, 0)

    def fill_hs(left_rim, body, right_rim):
        hs[:, :RIM] = jnp.zeros((K, RIM), BF16)
        hs[:, RIM:2 * RIM] = left_rim.astype(BF16)
        hs[:, 2 * RIM:2 * RIM + T] = body.astype(BF16)
        hs[:, 2 * RIM + T:] = right_rim.astype(BF16)

    def build_left(dst, g):
        v = ms[...]
        for b in range(GL):
            dst[pl.ds(pl.multiple_of(g * GW + b * N, N), N), :] = v[:, b:b + T]
        ms[:, :EXT] = v[:, GL:EXT + GL]

    mcopy.wait_recv()
    mext[:, T:] = mrim_r[...]
    ms[:, :EXT] = mext[...]
    ms[:, EXT:] = jnp.zeros((N, RIM), BF16)

    def mbody(g, _):
        build_left(mlag, g)
        return 0

    lax.fori_loop(0, GROUPS, mbody, 0)
    stk[:N] = mext[:, :T]
    mask_ext = jnp.where(mext[...].astype(F32) > 0.0, 1.0, 0.0)

    def send_sums(it, kind, src):
        for p in range(NN):
            a, b = (p % rg) * 8, (p // rg) * w
            ndx[it, kind, p] = src[a:a + 8, b:b + w]
        at = 2 * it + kind
        return [
            send(ndx.at[it, kind, npeer(r)], ndr.at[it, kind, r - 1], nd_ss.at[at, r], nd_rs.at[at, r],
                 "neuron", npeer(r))
            for r in range(1, NN)
        ]

    RQ = 2 * N // 4
    quad = lax.broadcasted_iota(jnp.int32, (RQ, 128), 1) // K
    wcs = {}

    def contract(rows_bf, g):
        rws = pl.ds(pl.multiple_of(g * GW, GW), GW)
        return lax.dot_general(
            rows_bf, hlag[rws, :T], (((1,), (1,)), ((), ())), preferred_element_type=F32
        )

    scale = None
    for it in range(ITERS):
        last = it == ITERS - 1
        def tbody(g, _):
            x = wg[g].astype(F32)
            for h in range(GW // 128):
                t = x[:, h * 128:(h + 1) * 128].T
                wt[g, :, h * 128:(h + 1) * 128] = jnp.concatenate(
                    [t[q * K:(q + 1) * K] for q in range(4)], axis=1
                ).astype(BF16)
            return 0

        lax.fori_loop(0, GROUPS, tbody, 0)

        accn[...] = jnp.zeros_like(accn)

        def nbody(g, _):
            accn[...] = accn[...] + dot(wt[g], mlag[pl.ds(pl.multiple_of(g * GW, GW), GW), :])
            return 0

        lax.fori_loop(0, GROUPS, nbody, 0)
        ncs = send_sums(it, 0, accn)
        if it == 0:
            for c in rims[it]:
                c.wait_recv()
            fill_hs(rim_r[it, 1], hf[...], rim_r[it, 0])
        else:
            rims[it][0].wait_recv()
            fill_hs(rim_r[it, 1] / scale, hf[...] / scale, rim_r[it, 0] / scale)
        build_right(EXT)
        approx = (acc[...].astype(BF16).astype(F32) * mask_ext).astype(BF16)
        ms[:, :EXT] = approx

        accd[...] = jnp.zeros_like(accd)

        def dbody(g, _):
            build_left(alag, g)
            rws = pl.ds(pl.multiple_of(g * GW, GW), GW)
            accd[...] = accd[...] + dot(wt[g], alag[rws, :])
            return 0

        lax.fori_loop(0, GROUPS, dbody, 0)
        dcs = send_sums(it, 1, accd)
        num = ndx[it, 0, me_n]
        den = ndx[it, 1, me_n]
        for r in range(1, NN):
            ncs[r - 1].wait_recv()
            num = num + ndr[it, 0, r - 1]
        for r in range(1, NN):
            dcs[r - 1].wait_recv()
            den = den + ndr[it, 1, r - 1]
        hown = hown * num / jnp.maximum(den, 1.0)
        hall[it, me_n] = hown
        cs = [
            send(hall.at[it, me_n], hall.at[it, me_n], hg_ss.at[it, r], hg_rs.at[it, r], "neuron", npeer(r))
            for r in range(1, NN)
        ]
        for c in cs:
            c.wait_recv()
        for p in range(NN):
            a, b = (p % rg) * 8, (p // rg) * w
            hf[a:a + 8, b:b + w] = hall[it, p]
        hnew = hf[...]
        rim_s[it + 1, 0] = hnew[:, :RIM]
        rim_s[it + 1, 1] = hnew[:, T - RIM:]
        send_rims(it + 1)
        sq = jnp.sum(hnew * hnew, axis=1, keepdims=True)
        ssr[it, me_f] = jnp.broadcast_to(sq, (K, 128))
        ssc = [
            send(ssr.at[it, me_f], ssr.at[it, me_f], ss_ss.at[it, r], ss_rs.at[it, r], "frame", fpeer(r))
            for r in range(1, NF)
        ]
        rims[it + 1][1].wait_recv()
        fill_hs(rim_r[it + 1, 1], hnew, hnew[:, :RIM])
        build_right(T)
        approx2 = (acc[:, :T].astype(BF16).astype(F32) * mask_ext[:, :T]).astype(BF16)
        stk[N:] = approx2
        for r in list(range(1, NF)) + [0]:
            p = fpeer(r)
            sums = [contract(stk[...], p * gp + q) for q in range(gp)]
            if r:
                top = sums[0][:, :128]
                for x in sums:
                    for h in range(GW // 128):
                        top = jnp.maximum(top, x[:, h * 128:(h + 1) * 128])
                top = jnp.maximum(top, pltpu.roll(top, 64, 1))
                top = jnp.maximum(top, pltpu.roll(top, 32, 1))
                inv = 65534.0 / jnp.maximum(top, 1e-30)
                inv = jnp.concatenate([inv] * (GW // 128), axis=1)
                for q in range(gp):
                    code = jnp.minimum(jnp.round(sums[q] * inv) - 32767.0, 32767.0)
                    wqx[it, r - 1, q] = code.astype(jnp.int32).astype(jnp.int16)
                packed = top[:RQ]
                for j in range(1, 4):
                    packed = jnp.where(quad == j, top[j * RQ:(j + 1) * RQ], packed)
                wqs[it, r - 1] = packed
                wcs[r - 1] = (
                    send(wqs.at[it, r - 1], wqt.at[it, r - 1], wt_ss.at[it, r], wt_rs.at[it, r], "frame", p),
                    send(wqx.at[it, r - 1], wqr.at[it, r - 1], ws_ss.at[it, r], ws_rs.at[it, r], "frame", p),
                )
            else:
                wtot = sums
        for c in ssc:
            c.wait_recv()
        total = ssr[it, 0]
        for p in range(1, NF):
            total = total + ssr[it, p]
        scale_wide = jnp.sqrt(total + EPS)
        scale = scale_wide[:, 0:1]
        ek = lax.broadcasted_iota(jnp.int32, (K, GW), 0)
        ec = lax.broadcasted_iota(jnp.int32, (K, GW), 1) % K
        scale_row = jnp.sum(jnp.where(ek == ec, scale, 0.0), axis=0, keepdims=True)
        hown = hown / own_rows(scale)
        for r in range(1, NF):
            for c in wcs[r - 1]:
                c.wait_recv()
            packed = wqt[it, r - 1]
            tops = []
            for j in range(4):
                t = jnp.where(quad == j, packed, 0.0)
                t = t + pltpu.roll(t, 64, 1)
                tops.append(t + pltpu.roll(t, 32, 1))
            unit = jnp.concatenate(tops, axis=0) * (1.0 / 65534.0)
            unit = jnp.concatenate([unit] * (GW // 128), axis=1)
            wtot = [
                wtot[q] + (wqr[it, r - 1, q].astype(jnp.int32).astype(F32) + 32767.0) * unit
                for q in range(gp)
            ]
        wnew = jnp.stack([wown[q] * wtot[q][:N] / wtot[q][N:] * scale_row for q in range(gp)])
        wown[...] = wnew
        mine = pl.ds(me_f * gp, gp)
        if not last:
            wgb[it, mine] = wnew.astype(BF16)
            cs = [
                send(wgb.at[it, mine], wgb.at[it, mine], wg_ss.at[it, r], wg_rs.at[it, r], "frame", fpeer(r))
                for r in range(1, NF)
            ]
            for c in cs:
                c.wait_recv()
            wg[...] = wgb[it]

    pts[...] = wnew.astype(BF16)
    ptc = send(pts, ptr, pt_sem.at[0], pt_sem.at[1], "half", 1 - me_h)
    wfin[mine] = wnew
    fcs = [
        send(wfin.at[mine], wfin.at[mine], wg_ss.at[ITERS - 1, r], wg_rs.at[ITERS - 1, r], "frame", fpeer(r))
        for r in range(1, NF)
    ]
    hout_ref[...] = hf[...] / scale
    ptc.wait_recv()
    far = ptr[...].astype(F32)
    cross = jnp.zeros((128, 128), F32)
    osq = jnp.zeros((1, 128), F32)
    fsq = jnp.zeros((1, 128), F32)
    for q in range(gp):
        for h in range(GW // 128):
            a = wnew[q, :, h * 128:(h + 1) * 128]
            b = far[q, :, h * 128:(h + 1) * 128]
            cross = cross + lax.dot_general(
                a, b, (((0,), (0,)), ((), ())),
                preferred_element_type=F32, precision=lax.Precision.HIGHEST,
            )
            osq = osq + jnp.sum(a * a, axis=0, keepdims=True)
            fsq = fsq + jnp.sum(b * b, axis=0, keepdims=True)
    ri = lax.broadcasted_iota(jnp.int32, (128, 128), 0)
    ci = lax.broadcasted_iota(jnp.int32, (128, 128), 1)
    cross = jnp.where(ri // K == ci // K, cross, 0.0)
    cross = cross[0:K] + cross[K:2 * K] + cross[2 * K:3 * K] + cross[3 * K:]

    def fold(x):
        x = x + pltpu.roll(x, 64, 1)
        return x + pltpu.roll(x, 32, 1)

    pack = jnp.concatenate(
        [cross, jnp.broadcast_to(osq, (8, 128)), jnp.broadcast_to(fsq, (8, 128))], axis=0
    )
    snr[me_n] = fold(pack)
    cs = [
        send(snr.at[me_n], snr.at[me_n], sn_ss.at[r], sn_rs.at[r], "neuron", npeer(r))
        for r in range(1, NN)
    ]
    for c in cs:
        c.wait_recv()
    tot = snr[0]
    for p in range(1, NN):
        tot = tot + snr[p]
    sfr[me_f] = tot
    cs = [
        send(sfr.at[me_f], sfr.at[me_f], sf_ss.at[r], sf_rs.at[r], "frame", fpeer(r))
        for r in range(1, NF)
    ]
    for c in fcs:
        c.wait_recv()
    wout_ref[...] = wfin[...]
    for c in cs:
        c.wait_recv()
    tot = sfr[0]
    for p in range(1, NF):
        tot = tot + sfr[p]
    own_row = tot[K:K + 1]
    far_row = tot[K + 8:K + 9]
    rk = lax.broadcasted_iota(jnp.int32, (K, 128), 0)
    ck = lax.broadcasted_iota(jnp.int32, (K, 128), 1)
    own_col = jnp.sum(jnp.where(rk == ck, own_row, 0.0), axis=1, keepdims=True)
    sim = tot[:K] / jnp.sqrt((own_col + EPS) * (far_row + EPS))
    sim_ref[...] = sim[:, :K]
    rims[ITERS][0].wait_recv()
    for c in pending:
        c.wait_send()


def roll_right(x, s):
    return pltpu.roll(x, s, 1) if s else x


def roll_left(x, s):
    return pltpu.roll(x, x.shape[1] - s, 1) if s else x


def wide_kernel(
    NN, NF, T,
    ca_hbm, tof_hbm, th_hbm, w_hbm, prof_hbm,
    wout_ref, hout_ref, sim_ref,
    ca_ref, tof_ref, th_ref, w_ref, prof_ref, by_lag, wf,
    rim_s, rim_r, mtx, mrx, w32, wt32, hla, mla, ala, qs, ps,
    ndx, ndr, hb, hl, ml, al, dat, md, prx, acc, own, tx, rx, topx, topr,
    hg, wtx, wtr, wcx, wcr, far_s, far_r, snx, snr,
    isem, ssem, rsem,
):
    me_n = lax.axis_index("neuron")
    me_f = lax.axis_index("frame")
    me_h = lax.axis_index("half")
    me_c = lax.rem(me_n, 2)
    me_y = me_n // 2
    N = ca_ref.shape[0]
    F = NF * T
    NB = N // NF
    KC = K // 2
    TC = T // 2
    EXT = T + RIM
    pending = []

    def send(src, dst, peer):
        i = len(pending)
        c = pltpu.make_async_remote_copy(
            src_ref=src, dst_ref=dst, send_sem=ssem.at[i], recv_sem=rsem.at[i],
            device_id=peer, device_id_type=MESH,
        )
        c.start()
        pending.append(c)
        return c

    def npeer(r):
        return lax.rem(me_n + r, NN)

    def fpeer(r):
        return lax.rem(me_f + r, NF)

    core = {"neuron": me_n + 1 - 2 * me_c}
    seven = [(dy, dz) for dz in (3, 2, 1, 0) for dy in (1, 0) if dy or dz]

    def block_of(dy, dz):
        return fpeer(dz) * 2 + lax.rem(me_y + dy, 2)

    def to(dy, dz):
        return {"neuron": npeer(2 * dy), "frame": fpeer(dz)}

    others = [(dn, df) for df in (3, 2, 1, 0) for dn in (3, 2, 1, 0) if dn or df]
    barrier = pltpu.get_barrier_semaphore()
    for r in range(1, NF):
        pl.semaphore_signal(barrier, inc=1, device_id={"frame": fpeer(r)}, device_id_type=MESH)
    for r in range(1, NN):
        pl.semaphore_signal(barrier, inc=1, device_id={"neuron": npeer(r)}, device_id_type=MESH)
    pl.semaphore_signal(barrier, inc=1, device_id={"half": 1 - me_h}, device_id_type=MESH)

    loads = [
        pltpu.make_async_copy(a, b, isem.at[i])
        for i, (a, b) in enumerate([
            (th_hbm, th_ref), (tof_hbm, tof_ref), (ca_hbm, ca_ref), (prof_hbm, prof_ref), (w_hbm, w_ref),
        ])
    ]
    for c in loads:
        c.start()

    def turn(x):
        out = []
        for h in range(GW // 128):
            t = x[:, h * 128:(h + 1) * 128].T
            out.append(jnp.concatenate([t[q * K:(q + 1) * K] for q in range(4)], axis=1))
        return jnp.concatenate(out, axis=1)

    for c in loads[:-1]:
        c.wait()

    trials = th_ref.shape[1]
    rows = lax.broadcasted_iota(jnp.int32, (trials, trials), 0)
    cols = lax.broadcasted_iota(jnp.int32, (trials, trials), 1)
    thf = th_ref[...].astype(F32)
    th_col = jnp.sum(jnp.where(rows == cols, thf, 0.0), axis=1, keepdims=True)
    chosen = jnp.where(th_col == me_h.astype(F32), 1.0, 0.0)
    hit = lax.broadcasted_iota(jnp.int32, (trials, T), 0) == tof_ref[...]
    mask = jnp.sum(jnp.where(hit, chosen, 0.0), axis=0, keepdims=True)
    masked = ca_ref[...].astype(F32) * mask
    body = masked.astype(BF16)
    prof = prof_ref[...].astype(BF16)
    rim_s[0, :N] = body[:, :RIM]
    rim_s[0, N:] = prof[:, :RIM]
    rim_s[1, :K] = prof[:, T - RIM:]
    for z in range(NF):
        x = masked[z * NB:(z + 1) * NB]
        mtx[z] = jnp.concatenate([x[:, :TC], x[:, TC:]], axis=0).astype(BF16)

    loads[-1].wait()
    for j in range(K * L // 128):
        by_lag[j * 128:(j + 1) * 128, :N] = w_ref[:, j * 128:(j + 1) * 128].T

    def lay_out(lo, hi):
        for a in range(lo, hi):
            x = jnp.concatenate(
                [by_lag[pl.ds(a * GL + b, K, stride=L), :][:, :N] for b in range(GL)], axis=1
            )
            wt32[a * K:(a + 1) * K] = x.astype(BF16)
            x = turn(x)
            wf[a] = x
            w32[a * N:(a + 1) * N] = x.astype(BF16)

    pl.semaphore_wait(barrier, (NF - 1) + (NN - 1) + 1)

    to_left = send(rim_s.at[0], rim_r.at[0], {"frame": fpeer(NF - 1)})
    to_right = send(rim_s.at[1, pl.ds(0, K)], rim_r.at[1, pl.ds(0, K)], {"frame": fpeer(1)})
    mcs = [
        send(mtx.at[fpeer(r)], mrx.at[me_f], {"frame": fpeer(r)})
        for r in (3, 2, 1)
    ]
    mrx[me_f] = mtx[me_f]

    lay_out(0, GROUPS)
    mine = pl.ds(pl.multiple_of(me_f * NB, NB), NB)
    w8 = jnp.concatenate([wf[a, mine, :] for a in range(GROUPS)], axis=0)

    def lags(dst, x, roll, lo=0, hi=None, at=0):
        n = x.shape[0]
        hi = x.shape[1] if hi is None else hi
        for b in range(GL):
            dst[b * n:(b + 1) * n, at:at + hi - lo] = roll(x, b)[:, lo:hi]

    IN = T - RIM
    lags(mla, body, roll_left, 0, IN)
    qs[:, :IN] = dot(wt32[...], mla[:, :IN])
    lags(hla, prof, roll_right, RIM, T, 2 * RIM)
    ps[:, 2 * RIM:EXT] = dot(w32[...], hla[:, 2 * RIM:EXT])

    to_left.wait_recv()
    mext = jnp.concatenate([body, rim_r[0, :N]], axis=1)
    mask_ext = jnp.where(mext.astype(F32) > 0.0, 1.0, 0.0)

    def shifted_sum(q):
        s = q[:K]
        for a in range(1, GROUPS):
            s = s + roll_left(q[a * K:(a + 1) * K], a * GL)
        return s[:, :T]

    def scatter(kind, s):
        for p in range(NN):
            a, b = (p % 2) * KC, (p // 2) * TC
            ndx[kind, p] = s[a:a + KC, b:b + TC]
        return [
            send(ndx.at[kind, npeer(r)], ndr.at[kind, r - 1], {"neuron": npeer(r)})
            for r in range(1, NN)
        ]

    lags(mla, mext[:, IN:], roll_left, at=IN)
    qs[:, IN:] = dot(wt32[...], mla[:, IN:])
    lags(hla, jnp.concatenate([prof[:, IN:], rim_r[0, N:]], axis=1), roll_right, RIM, 2 * RIM, EXT)
    ps[:, EXT:] = dot(w32[...], hla[:, EXT:])
    ncs = scatter(0, shifted_sum(qs[...]))
    to_right.wait_recv()
    lags(hla, jnp.concatenate([rim_r[1, :K], prof[:, :RIM]], axis=1), roll_right)
    ps[:, :2 * RIM] = dot(w32[...], hla[:, :2 * RIM])
    p = ps[...]
    s = p[:N]
    for a in range(1, GROUPS):
        s = s + roll_right(p[a * N:(a + 1) * N], a * GL)
    approx = (s[:, RIM:].astype(BF16).astype(F32) * mask_ext).astype(BF16)
    lags(ala, approx, roll_left)
    dcs = scatter(1, shifted_sum(dot(wt32[...], ala[...])))

    own_rows = pl.ds(pl.multiple_of(me_c * KC, KC), KC)
    far_rows = pl.ds(pl.multiple_of((1 - me_c) * KC, KC), KC)
    hown = prof_ref[own_rows, pl.ds(pl.multiple_of(me_y * TC, TC), TC)]
    num = ndx[0, me_n]
    den = ndx[1, me_n]
    for r in range(1, NN):
        ncs[r - 1].wait_recv()
        num = num + ndr[0, r - 1]
    for r in range(1, NN):
        dcs[r - 1].wait_recv()
        den = den + ndr[1, r - 1]
    hown = hown * num / jnp.maximum(den, 1.0)

    def spot(c, blk):
        return pl.ds(pl.multiple_of(c * KC, KC), KC), pl.ds(pl.multiple_of(blk * TC, TC), TC)

    lane = lax.broadcasted_iota(jnp.int32, (8, 128), 1)

    def gather_h(it):
        a, b = spot(me_c, block_of(0, 0))
        hb[it, a, b] = hown.astype(BF16)
        cs = [send(hb.at[it, a, b], hb.at[it, a, b], to(dy, dz)) for dy, dz in seven]
        relays = [send(hb.at[it, a, b], hb.at[it, a, b], core)]
        return cs, relays

    def half_lags(it, rows_of, c):
        x = hb[it, rows_of, :]
        for b in range(GL):
            hl[pl.ds(pl.multiple_of(b * K + c * KC, KC), KC), :] = roll_right(x, b)

    def relay_h(it, cs, relays):
        for i in range(len(seven) - 1, -1, -1):
            cs[i].wait_recv()
            dy, dz = seven[i]
            a, b = spot(me_c, block_of(dy, NF - dz))
            relays.append(send(hb.at[it, a, b], hb.at[it, a, b], core))
        half_lags(it, own_rows, me_c)
        for c in relays:
            c.wait_recv()
        half_lags(it, far_rows, 1 - me_c)

    def squares(it):
        x = hb[it].astype(F32)
        return jnp.sum(x * x, axis=1, keepdims=True)

    cs, relays = gather_h(0)

    for c in mcs:
        c.wait_recv()
    for z in range(NF):
        x = mrx[z].astype(F32)
        md[:, z * T:z * T + TC] = x[:NB]
        md[:, z * T + TC:(z + 1) * T] = x[NB:]
    data = md[...]
    mask_all = jnp.where(data[0:1] > 0.0, 1.0, 0.0)
    rolled = [roll_left(data, a * GL) for a in range(GROUPS)]
    for a in range(GROUPS):
        dat[a * 2 * NB:a * 2 * NB + NB] = rolled[a]
    lags(ml, jnp.concatenate(rolled[:4], axis=0).astype(BF16), roll_left)

    def recon(wb):
        p = dot(wb, hl[...])
        s = p[:NB]
        for a in range(1, GROUPS):
            s = s + roll_right(p[a * NB:(a + 1) * NB], a * GL)
        return s.astype(BF16).astype(F32) * mask_all

    def corr(wt, m):
        q = dot(wt, m[...])
        return q[:K] + roll_left(q[K:], 4 * GL)

    def template_ratio():
        approx = recon(w8.astype(BF16))
        for a in range(GROUPS):
            dat[a * 2 * NB + NB:(a + 1) * 2 * NB] = roll_left(approx, a * GL)
        s = lax.dot_general(
            dat[...].astype(BF16), hl[...], (((1,), (1,)), ((), ())), preferred_element_type=F32
        )
        wnum = jnp.concatenate([s[a * 2 * NB:a * 2 * NB + NB] for a in range(GROUPS)], axis=0)
        wden = jnp.concatenate([s[a * 2 * NB + NB:(a + 1) * 2 * NB] for a in range(GROUPS)], axis=0)
        return wnum, wden

    relay_h(0, cs, relays)
    wnum, wden = template_ratio()
    w8 = w8 * wnum / wden

    wt = jnp.concatenate([turn(w8[:4 * NB]), turn(w8[4 * NB:])], axis=0).astype(BF16)

    def reduce_start(kind, s):
        acc[kind] = s
        return send(acc.at[kind, far_rows], prx.at[kind], core)

    def reduce_spread(kind, c):
        c.wait_recv()
        s = acc[kind, own_rows, :] + prx[kind]
        own[kind] = s
        top = jnp.maximum(jnp.max(s, axis=1, keepdims=True), 1e-30)
        topx[kind] = jnp.sum(jnp.where(eye, top, 0.0), axis=0, keepdims=True)
        ts = [send(topx.at[kind], topr.at[kind * 7 + i], to(dy, dz)) for i, (dy, dz) in enumerate(seven)]
        code = jnp.round(s * (65534.0 / top)) - 32767.0
        tx[kind] = jnp.minimum(code, 32767.0).astype(jnp.int32).astype(jnp.int16)
        return ts, [
            send(
                tx.at[kind, :, pl.ds(pl.multiple_of(block_of(dy, dz) * TC, TC), TC)],
                rx.at[kind, i], to(dy, dz),
            )
            for i, (dy, dz) in enumerate(seven)
        ]

    def reduce_done(kind, sent):
        ts, cs = sent
        t = own[kind, :, pl.ds(pl.multiple_of(block_of(0, 0) * TC, TC), TC)]
        for i in range(len(seven) - 1, -1, -1):
            ts[i].wait_recv()
            unit = jnp.sum(jnp.where(eye, topr[kind * 7 + i], 0.0), axis=1, keepdims=True) * (1.0 / 65534.0)
            cs[i].wait_recv()
            t = t + (rx[kind, i].astype(jnp.int32).astype(F32) + 32767.0) * unit
        return t

    eye = lax.broadcasted_iota(jnp.int32, (KC, 128), 0) == lax.broadcasted_iota(jnp.int32, (KC, 128), 1)
    nc = reduce_start(0, corr(wt, ml))
    approx = recon(w8.astype(BF16))
    ncs = reduce_spread(0, nc)
    lags(al, jnp.concatenate([roll_left(approx, a * GL) for a in range(4)], axis=0).astype(BF16), roll_left)
    dc = reduce_start(1, corr(wt, al))
    scale0 = jnp.sqrt(squares(0) + EPS)
    dcs = reduce_spread(1, dc)
    num = reduce_done(0, ncs)
    den = reduce_done(1, dcs)
    s0 = jnp.where(me_c == 0, scale0[:KC], scale0[KC:])
    hown = hown * (num * s0) / jnp.maximum(den * s0, 1.0)
    cs, relays = gather_h(1)
    relay_h(1, cs, relays)
    hg[me_n] = hown
    hcs = [send(hg.at[me_n], hg.at[me_n], {"neuron": npeer(r)}) for r in (3, 2, 1)]
    wnum, wden = template_ratio()
    scale = jnp.sqrt(squares(1) + EPS * scale0 * scale0)
    ek = lax.broadcasted_iota(jnp.int32, (K, GW), 0)
    ec = lax.broadcasted_iota(jnp.int32, (K, GW), 1) % K
    scale_row = jnp.sum(jnp.where(ek == ec, scale, 0.0), axis=0, keepdims=True)
    w8 = w8 * wnum / wden * scale_row

    far_s[...] = w8.astype(BF16)
    fc = send(far_s, far_r, {"half": 1 - me_h})
    for q in range(2):
        t = turn(w8[q * 4 * NB:(q + 1) * 4 * NB])
        for b in range(GL):
            for a in range(4):
                at = b * K + a * NB
                by_lag[pl.ds(q * 4 * GL + a * GL + b, K, stride=L), :NB] = t[:, at:at + NB]
    x = jnp.concatenate(
        [by_lag[j * 128:(j + 1) * 128, :NB].T for j in range(K * L // 128)], axis=1
    )
    top = jnp.maximum(jnp.max(x, axis=1, keepdims=True), 1e-30)
    wtx[...] = jnp.sum(jnp.where(eye[:NB], top, 0.0), axis=0, keepdims=True)
    x = jnp.minimum(jnp.round(x * (65534.0 / top)) - 32767.0, 32767.0)
    half = K * L // 2
    wcx[...] = jnp.concatenate([x[:, :half], x[:, half:]], axis=0).astype(jnp.int32).astype(jnp.int16)
    wcs = [
        (
            send(wtx, wtr.at[r - 1], {"frame": fpeer(r)}),
            send(wcx, wcr.at[r - 1], {"frame": fpeer(r)}),
        )
        for r in (3, 2, 1)
    ]

    def place(z, code, top_row):
        unit = jnp.sum(jnp.where(eye[:NB], top_row, 0.0), axis=1, keepdims=True) * (1.0 / 65534.0)
        y = (code.astype(jnp.int32).astype(F32) + 32767.0)
        at = pl.ds(pl.multiple_of(z * NB, NB), NB)
        wout_ref[at, :half] = y[:NB] * unit
        wout_ref[at, half:] = y[NB:] * unit

    place(me_f, wcx[...], wtx[...])
    for c in hcs:
        c.wait_recv()
    for p in range(NN):
        a, b = (p % 2) * KC, (p // 2) * TC
        hout_ref[a:a + KC, b:b + TC] = hg[p] / scale[a:a + KC]
    fc.wait_recv()
    far = far_r[...].astype(F32)

    def split(x):
        parts = []
        for _ in range(3):
            parts.append(x.astype(BF16))
            x = x - parts[-1].astype(F32)
        return parts

    cross = jnp.zeros((128, 128), F32)
    osq = jnp.zeros((1, 128), F32)
    fsq = jnp.zeros((1, 128), F32)
    for h in range(GW // 128):
        a = w8[:, h * 128:(h + 1) * 128]
        b = far[:, h * 128:(h + 1) * 128]
        for part in split(a):
            cross = cross + lax.dot_general(
                part, b.astype(BF16), (((0,), (0,)), ((), ())), preferred_element_type=F32
            )
        osq = osq + jnp.sum(a * a, axis=0, keepdims=True)
        fsq = fsq + jnp.sum(b * b, axis=0, keepdims=True)
    ri = lax.broadcasted_iota(jnp.int32, (128, 128), 0)
    ci = lax.broadcasted_iota(jnp.int32, (128, 128), 1)
    cross = jnp.where(ri // K == ci // K, cross, 0.0)
    cross = cross[0:K] + cross[K:2 * K] + cross[2 * K:3 * K] + cross[3 * K:]

    def fold(x):
        x = x + pltpu.roll(x, 64, 1)
        return x + pltpu.roll(x, 32, 1)

    cross = fold(cross)
    quad = lane // K
    pack = cross[:8]
    for q in range(1, 4):
        pack = jnp.where(quad == q, cross[q * 8:(q + 1) * 8], pack)
    for q in range(8):
        snx[:, q * 128:(q + 1) * 128] = pack[q:q + 1]
    snx[:, 8 * 128:] = jnp.where(quad[:1] < 2, fold(osq), fold(fsq))
    scs = [
        send(snx, snr.at[i], {"neuron": npeer(dn), "frame": fpeer(df)})
        for i, (dn, df) in enumerate(others)
    ]
    for i, r in enumerate((3, 2, 1)):
        for c in wcs[i]:
            c.wait_recv()
        place(fpeer(NF - r), wcr[r - 1], wtr[r - 1])
    tot = snx[...]
    for i in range(len(others) - 1, -1, -1):
        scs[i].wait_recv()
        tot = tot + snr[i]
    own_row = tot[:, 8 * 128:]
    far_row = pltpu.roll(own_row, 64, 1)
    tot = jnp.concatenate([tot[:, q * 128:(q + 1) * 128] for q in range(8)], axis=0)
    rk = lax.broadcasted_iota(jnp.int32, (K, 128), 0)
    ck = lax.broadcasted_iota(jnp.int32, (K, 128), 1)
    own_col = jnp.sum(jnp.where(rk == ck, own_row, 0.0), axis=1, keepdims=True)
    full = jnp.concatenate(
        [tot] + [pltpu.roll(tot, 128 - q * K, 1) for q in range(1, 4)], axis=0
    )
    sim = full / jnp.sqrt((own_col + EPS) * (far_row + EPS))
    sim_ref[...] = sim[:, :K]
    for c in pending:
        c.wait_send()


def wide_call(NN, NF, T, N, trials):
    F = NF * T
    NB = N // NF
    KC = K // 2
    TC = T // 2
    EXT = T + RIM
    V = pltpu.VMEM
    D = pltpu.SemaphoreType.DMA
    vmem = pl.BlockSpec(memory_space=pltpu.VMEM)
    return pl.pallas_call(
        functools.partial(wide_kernel, NN, NF, T),
        out_shape=(
            jax.ShapeDtypeStruct((N, K * L), F32),
            jax.ShapeDtypeStruct((K, T), F32),
            jax.ShapeDtypeStruct((K, K), F32),
        ),
        in_specs=[pl.BlockSpec(memory_space=pl.ANY)] * 5,
        out_specs=(vmem,) * 3,
        scratch_shapes=[
            V((N, T), BF16),
            V((1, T), jnp.int32),
            V((1, trials), jnp.int32),
            V((N, K * L), F32),
            V((K, T), F32),
            V((K * L, 128), F32),
            V((GROUPS, N, GW), F32),
            V((2, N + K, RIM), BF16),
            V((2, N + K, RIM), BF16),
            V((NF, 2 * NB, TC), BF16),
            V((NF, 2 * NB, TC), BF16),
            V((GROUPS * N, GW), BF16),
            V((GROUPS * K, GW), BF16),
            V((GW, EXT + RIM), BF16),
            V((GW, EXT), BF16),
            V((GW, EXT), BF16),
            V((GROUPS * K, EXT), F32),
            V((GROUPS * N, EXT + RIM), F32),
            V((2, NN, KC, TC), F32),
            V((2, NN - 1, KC, TC), F32),
            V((ITERS, K, F), BF16),
            V((GW, F), BF16),
            V((GW, F), BF16),
            V((GW, F), BF16),
            V((2 * GROUPS * NB, F), F32),
            V((NB, F), F32),
            V((2, KC, F), F32),
            V((2, K, F), F32),
            V((2, KC, F), F32),
            V((2, KC, F), jnp.int16),
            V((2, 7, KC, TC), jnp.int16),
            V((2, 1, 128), F32),
            V((14, 1, 128), F32),
            V((NN, KC, TC), F32),
            V((1, 128), F32),
            V((NF - 1, 1, 128), F32),
            V((2 * NB, K * L // 2), jnp.int16),
            V((NF - 1, 2 * NB, K * L // 2), jnp.int16),
            V((GROUPS * NB, GW), BF16),
            V((GROUPS * NB, GW), BF16),
            V((1, 9 * 128), F32),
            V((NN * NF - 1, 1, 9 * 128), F32),
            D((5,)),
            D((104,)),
            D((104,)),
        ],
        compiler_params=pltpu.CompilerParams(
            collective_id=1, has_side_effects=True, vmem_limit_bytes=56 << 20
        ),
    )


def emit_kernel(w_ref, h_ref, s_ref, w_out, h_out, s_out, sem):
    pairs = [(h_ref, h_out.at[0]), (s_ref, s_out.at[0])]
    step = w_ref.shape[1] // 2
    for r in range(w_ref.shape[0] // 8):
        for q in range(2):
            part = (pl.ds(r * 8, 8), pl.ds(q * step, step))
            pairs.append((w_ref.at[part], w_out.at[0].at[part]))
    cs = [pltpu.make_async_copy(a, b, sem.at[i]) for i, (a, b) in enumerate(pairs)]
    for c in cs:
        c.start()
    for c in cs:
        c.wait()


def emit(*arrays):
    return pl.pallas_call(
        emit_kernel,
        out_shape=tuple(jax.ShapeDtypeStruct((1, *x.shape), F32) for x in arrays),
        in_specs=[pl.BlockSpec(memory_space=pltpu.VMEM)] * 3,
        out_specs=(pl.BlockSpec(memory_space=pl.ANY),) * 3,
        scratch_shapes=[pltpu.SemaphoreType.DMA((2 + arrays[0].shape[0] // 4,))],
    )(*arrays)


def tall_call(NN, NF, T, N):
    gp = GROUPS // NF
    rg = K // 8
    w = T * rg // NN
    EXT = T + RIM
    V = pltpu.VMEM
    D = pltpu.SemaphoreType.DMA
    vmem = pl.BlockSpec(memory_space=pltpu.VMEM)
    return pl.pallas_call(
        functools.partial(kernel, NN, NF, T),
        out_shape=(
            jax.ShapeDtypeStruct((GROUPS, N, GW), F32),
            jax.ShapeDtypeStruct((K, T), F32),
            jax.ShapeDtypeStruct((K, K), F32),
        ),
        in_specs=[vmem] * 5,
        out_specs=(vmem,) * 3,
        scratch_shapes=[
            V((K, 2 * RIM + T + RIM), BF16),
            V((L * K, EXT), BF16),
            V((N, EXT), BF16),
            V((N, EXT + RIM), BF16),
            V((L * N, T), BF16),
            V((L * N, T), BF16),
            V((N, EXT), F32),
            V((K, T), F32),
            V((K, T), F32),
            V((K, T), F32),
            V((GROUPS, N, GW), BF16),
            V((GROUPS, K, GW), BF16),
            V((gp, N, GW), F32),
            V((2 * N, T), BF16),
            V((N, RIM), BF16),
            V((N, RIM), BF16),
            V((ITERS + 1, 2, K, RIM), F32),
            V((ITERS + 1, 2, K, RIM), F32),
            V((ITERS, 2, NN, 8, w), F32),
            V((ITERS, 2, NN - 1, 8, w), F32),
            V((ITERS, NN, 8, w), F32),
            V((ITERS, NF, K, 128), F32),
            V((ITERS, NF - 1, gp, 2 * N, GW), jnp.int16),
            V((ITERS, NF - 1, gp, 2 * N, GW), jnp.int16),
            V((ITERS, NF - 1, 2 * N // 4, 128), F32),
            V((ITERS, NF - 1, 2 * N // 4, 128), F32),
            V((ITERS - 1, GROUPS, N, GW), BF16),
            V((GROUPS, N, GW), F32),
            V((gp, N, GW), BF16),
            V((gp, N, GW), BF16),
            V((NN, K + 16, 128), F32),
            V((NF, K + 16, 128), F32),
            D((2,)),
            D((ITERS + 1, 2)),
            D((ITERS + 1, 2)),
            D((2 * ITERS, NN)),
            D((2 * ITERS, NN)),
            D((ITERS, NN)),
            D((ITERS, NN)),
            D((ITERS, NF)),
            D((ITERS, NF)),
            D((ITERS, NF)),
            D((ITERS, NF)),
            D((ITERS, NF)),
            D((ITERS, NF)),
            D((ITERS, NF)),
            D((ITERS, NF)),
            D((2,)),
            D((NN,)),
            D((NN,)),
            D((NF,)),
            D((NF,)),
        ],
        compiler_params=pltpu.CompilerParams(
            collective_id=0, has_side_effects=True, vmem_limit_bytes=50 << 20
        ),
    )


def per_device(calcium, trial_of_frame, trial_half, loadings, profiles):
    NN = lax.axis_size("neuron")
    NF = lax.axis_size("frame")
    N, T = calcium.shape
    small = (calcium, trial_of_frame.reshape(1, T), trial_half.reshape(1, -1))
    if NN == 4 and NF == 4 and N == K:
        call = wide_call(NN, NF, T, N, trial_half.shape[0])
        return emit(*call(*small, loadings[0], profiles[0]))
    w_groups = loadings[0].reshape(N, K, GROUPS, GL).transpose(2, 0, 3, 1).reshape(GROUPS, N, GW)
    wout, hout, sim = tall_call(NN, NF, T, N)(*small, w_groups, profiles[0])
    loads = wout.reshape(GROUPS, N, GL, K).transpose(1, 3, 0, 2).reshape(1, N, K * L)
    return loads, hout[None], sim[None]


def solution(mesh):
    placed = (
        P("neuron", "frame"),
        P("frame"),
        P(),
        P("half", "neuron", None),
        P("half", None, "frame"),
    )
    return jax.shard_map(
        per_device,
        mesh=mesh,
        in_specs=placed,
        out_specs=(P("half", "neuron", None), P("half", None, "frame"), P("half", None, None)),
        check_vma=False,
    )
```

```python
import functools

import jax
import jax.numpy as jnp
from jax import lax
from jax.experimental import pallas as pl
from jax.experimental.pallas import tpu as pltpu
from jax.sharding import PartitionSpec as P

K = 32
L = 64
ITERS = 2
EPS = 1e-06
RIM = 128
GROUPS = 8
GL = L // GROUPS
GW = GL * K
MESH = pl.DeviceIdType.MESH
F32 = jnp.float32
BF16 = jnp.bfloat16


def dot(a, b):
    return jnp.dot(a, b, preferred_element_type=F32)


def kernel(
    NN, NF, T,
    ca_ref, tof_ref, th_ref, w_ref, prof_ref,
    wout_ref, hout_ref, sim_ref,
    hs, hlag, mext, ms, mlag, alag, acc, accn, accd, hf, wg, wt, wown, stk,
    mrim_s, mrim_r, rim_s, rim_r, ndx, ndr, hall, ssr, wqx, wqr, wqs, wqt, wgb, wfin, pts, ptr, snr, sfr,
    mr_sem, rim_ss, rim_rs, nd_ss, nd_rs, hg_ss, hg_rs, ss_ss, ss_rs,
    ws_ss, ws_rs, wt_ss, wt_rs, wg_ss, wg_rs, pt_sem, sn_ss, sn_rs, sf_ss, sf_rs,
):
    me_n = lax.axis_index("neuron")
    me_f = lax.axis_index("frame")
    me_h = lax.axis_index("half")
    N = ca_ref.shape[0]
    EXT = T + RIM
    gp = GROUPS // NF
    rg = K // 8
    w = T * rg // NN
    pending = []

    def send(src, dst, ssem, rsem, axis, peer):
        c = pltpu.make_async_remote_copy(
            src_ref=src, dst_ref=dst, send_sem=ssem, recv_sem=rsem,
            device_id={axis: peer}, device_id_type=MESH,
        )
        c.start()
        pending.append(c)
        return c

    def npeer(r):
        return lax.rem(me_n + r, NN)

    def fpeer(r):
        return lax.rem(me_f + r, NF)

    barrier = pltpu.get_barrier_semaphore()
    for r in range(1, NN):
        pl.semaphore_signal(barrier, inc=1, device_id={"neuron": npeer(r)}, device_id_type=MESH)
    for r in range(1, NF):
        pl.semaphore_signal(barrier, inc=1, device_id={"frame": fpeer(r)}, device_id_type=MESH)
    pl.semaphore_signal(barrier, inc=1, device_id={"half": 1 - me_h}, device_id_type=MESH)

    trials = th_ref.shape[1]
    rows = lax.broadcasted_iota(jnp.int32, (trials, trials), 0)
    cols = lax.broadcasted_iota(jnp.int32, (trials, trials), 1)
    thf = th_ref[...].astype(F32)
    th_col = jnp.sum(jnp.where(rows == cols, thf, 0.0), axis=1, keepdims=True)
    chosen = jnp.where(th_col == me_h.astype(F32), 1.0, 0.0)
    hit = lax.broadcasted_iota(jnp.int32, (trials, T), 0) == tof_ref[...]
    mask = jnp.sum(jnp.where(hit, chosen, 0.0), axis=0, keepdims=True)
    masked = (ca_ref[...].astype(F32) * mask).astype(BF16)
    mext[:, :T] = masked
    mrim_s[...] = masked[:, :RIM]
    hf[...] = prof_ref[...]
    rim_s[0, 0] = prof_ref[:, :RIM]
    rim_s[0, 1] = prof_ref[:, T - RIM:]

    pl.semaphore_wait(barrier, (NN - 1) + (NF - 1) + 1)

    left = fpeer(NF - 1)
    right = fpeer(1)
    rims = {}

    def send_rims(i):
        rims[i] = (
            send(rim_s.at[i, 0], rim_r.at[i, 0], rim_ss.at[i, 0], rim_rs.at[i, 0], "frame", left),
            send(rim_s.at[i, 1], rim_r.at[i, 1], rim_ss.at[i, 1], rim_rs.at[i, 1], "frame", right),
        )

    send_rims(0)
    mcopy = send(mrim_s, mrim_r, mr_sem.at[0], mr_sem.at[1], "frame", left)

    for g in range(GROUPS):
        wg[g] = w_ref[g].astype(BF16)
    wown[...] = w_ref[pl.ds(me_f * gp, gp)]

    crow = (me_n % rg) * 8
    ccol = (me_n // rg) * w
    if NN == rg:
        hown = prof_ref[pl.ds(pl.multiple_of(crow, 8), 8), :]
    else:
        hown = prof_ref[pl.ds(pl.multiple_of(crow, 8), 8), pl.ds(pl.multiple_of(ccol, 128), w)]

    def own_rows(col):
        out = col[0:8]
        for q in range(1, rg):
            out = jnp.where(me_n % rg == q, col[q * 8:(q + 1) * 8], out)
        return out

    def build_right(width, lo=0, hi=GROUPS, extra=None):
        def body(g, _):
            v = hs[...]
            for b in range(GL):
                hlag[pl.ds(pl.multiple_of(g * GW + b * K, K), K), :width] = (
                    v[:, 2 * RIM - b:2 * RIM - b + width]
                )
            hs[:, RIM:] = v[:, RIM - GL:hs.shape[1] - GL]
            part = dot(wg[g], hlag[pl.ds(pl.multiple_of(g * GW, GW), GW), :width])
            acc[:, :width] = acc[:, :width] + part
            if extra is not None:
                extra(g)
            return 0

        if lo == 0:
            acc[...] = jnp.zeros_like(acc)
        lax.fori_loop(lo, hi, body, 0)

    def fill_hs(left_rim, body, right_rim):
        hs[:, :RIM] = jnp.zeros((K, RIM), BF16)
        hs[:, RIM:2 * RIM] = left_rim.astype(BF16)
        hs[:, 2 * RIM:2 * RIM + T] = body.astype(BF16)
        hs[:, 2 * RIM + T:] = right_rim.astype(BF16)

    def build_left(dst, g):
        v = ms[...]
        for b in range(GL):
            dst[pl.ds(pl.multiple_of(g * GW + b * N, N), N), :] = v[:, b:b + T]
        ms[:, :EXT] = v[:, GL:EXT + GL]

    mcopy.wait_recv()
    mext[:, T:] = mrim_r[...]
    ms[:, :EXT] = mext[...]
    ms[:, EXT:] = jnp.zeros((N, RIM), BF16)

    def mbody(g, _):
        build_left(mlag, g)
        return 0

    lax.fori_loop(0, GROUPS, mbody, 0)
    stk[:N] = mext[:, :T]
    mask_ext = jnp.where(mext[...].astype(F32) > 0.0, 1.0, 0.0)

    def send_sums(it, kind, src):
        for p in range(NN):
            a, b = (p % rg) * 8, (p // rg) * w
            ndx[it, kind, p] = src[a:a + 8, b:b + w]
        at = 2 * it + kind
        return [
            send(ndx.at[it, kind, npeer(r)], ndr.at[it, kind, r - 1], nd_ss.at[at, r], nd_rs.at[at, r],
                 "neuron", npeer(r))
            for r in range(1, NN)
        ]

    RQ = 2 * N // 4
    quad = lax.broadcasted_iota(jnp.int32, (RQ, 128), 1) // K
    wcs = {}

    def contract(rows_bf, g):
        rws = pl.ds(pl.multiple_of(g * GW, GW), GW)
        return lax.dot_general(
            rows_bf, hlag[rws, :T], (((1,), (1,)), ((), ())), preferred_element_type=F32
        )

    scale = None
    for it in range(ITERS):
        last = it == ITERS - 1
        def tbody(g, _):
            x = wg[g].astype(F32)
            for h in range(GW // 128):
                t = x[:, h * 128:(h + 1) * 128].T
                wt[g, :, h * 128:(h + 1) * 128] = jnp.concatenate(
                    [t[q * K:(q + 1) * K] for q in range(4)], axis=1
                ).astype(BF16)
            return 0

        lax.fori_loop(0, GROUPS, tbody, 0)

        accn[...] = jnp.zeros_like(accn)

        def nbody(g, _):
            accn[...] = accn[...] + dot(wt[g], mlag[pl.ds(pl.multiple_of(g * GW, GW), GW), :])
            return 0

        lax.fori_loop(0, GROUPS, nbody, 0)
        ncs = send_sums(it, 0, accn)
        if it == 0:
            for c in rims[it]:
                c.wait_recv()
            fill_hs(rim_r[it, 1], hf[...], rim_r[it, 0])
        else:
            rims[it][0].wait_recv()
            fill_hs(rim_r[it, 1] / scale, hf[...] / scale, rim_r[it, 0] / scale)
        build_right(EXT)
        approx = (acc[...].astype(BF16).astype(F32) * mask_ext).astype(BF16)
        ms[:, :EXT] = approx

        accd[...] = jnp.zeros_like(accd)

        def dbody(g, _):
            build_left(alag, g)
            rws = pl.ds(pl.multiple_of(g * GW, GW), GW)
            accd[...] = accd[...] + dot(wt[g], alag[rws, :])
            return 0

        lax.fori_loop(0, GROUPS, dbody, 0)
        dcs = send_sums(it, 1, accd)
        num = ndx[it, 0, me_n]
        den = ndx[it, 1, me_n]
        for r in range(1, NN):
            ncs[r - 1].wait_recv()
            num = num + ndr[it, 0, r - 1]
        for r in range(1, NN):
            dcs[r - 1].wait_recv()
            den = den + ndr[it, 1, r - 1]
        hown = hown * num / jnp.maximum(den, 1.0)
        hall[it, me_n] = hown
        cs = [
            send(hall.at[it, me_n], hall.at[it, me_n], hg_ss.at[it, r], hg_rs.at[it, r], "neuron", npeer(r))
            for r in range(1, NN)
        ]
        for c in cs:
            c.wait_recv()
        for p in range(NN):
            a, b = (p % rg) * 8, (p // rg) * w
            hf[a:a + 8, b:b + w] = hall[it, p]
        hnew = hf[...]
        rim_s[it + 1, 0] = hnew[:, :RIM]
        rim_s[it + 1, 1] = hnew[:, T - RIM:]
        send_rims(it + 1)
        sq = jnp.sum(hnew * hnew, axis=1, keepdims=True)
        ssr[it, me_f] = jnp.broadcast_to(sq, (K, 128))
        ssc = [
            send(ssr.at[it, me_f], ssr.at[it, me_f], ss_ss.at[it, r], ss_rs.at[it, r], "frame", fpeer(r))
            for r in range(1, NF)
        ]
        rims[it + 1][1].wait_recv()
        fill_hs(rim_r[it + 1, 1], hnew, hnew[:, :RIM])
        build_right(T)
        approx2 = (acc[:, :T].astype(BF16).astype(F32) * mask_ext[:, :T]).astype(BF16)
        stk[N:] = approx2
        for r in list(range(1, NF)) + [0]:
            p = fpeer(r)
            sums = [contract(stk[...], p * gp + q) for q in range(gp)]
            if r:
                top = sums[0][:, :128]
                for x in sums:
                    for h in range(GW // 128):
                        top = jnp.maximum(top, x[:, h * 128:(h + 1) * 128])
                top = jnp.maximum(top, pltpu.roll(top, 64, 1))
                top = jnp.maximum(top, pltpu.roll(top, 32, 1))
                inv = 65534.0 / jnp.maximum(top, 1e-30)
                inv = jnp.concatenate([inv] * (GW // 128), axis=1)
                for q in range(gp):
                    code = jnp.minimum(jnp.round(sums[q] * inv) - 32767.0, 32767.0)
                    wqx[it, r - 1, q] = code.astype(jnp.int32).astype(jnp.int16)
                packed = top[:RQ]
                for j in range(1, 4):
                    packed = jnp.where(quad == j, top[j * RQ:(j + 1) * RQ], packed)
                wqs[it, r - 1] = packed
                wcs[r - 1] = (
                    send(wqs.at[it, r - 1], wqt.at[it, r - 1], wt_ss.at[it, r], wt_rs.at[it, r], "frame", p),
                    send(wqx.at[it, r - 1], wqr.at[it, r - 1], ws_ss.at[it, r], ws_rs.at[it, r], "frame", p),
                )
            else:
                wtot = sums
        for c in ssc:
            c.wait_recv()
        total = ssr[it, 0]
        for p in range(1, NF):
            total = total + ssr[it, p]
        scale_wide = jnp.sqrt(total + EPS)
        scale = scale_wide[:, 0:1]
        ek = lax.broadcasted_iota(jnp.int32, (K, GW), 0)
        ec = lax.broadcasted_iota(jnp.int32, (K, GW), 1) % K
        scale_row = jnp.sum(jnp.where(ek == ec, scale, 0.0), axis=0, keepdims=True)
        hown = hown / own_rows(scale)
        for r in range(1, NF):
            for c in wcs[r - 1]:
                c.wait_recv()
            packed = wqt[it, r - 1]
            tops = []
            for j in range(4):
                t = jnp.where(quad == j, packed, 0.0)
                t = t + pltpu.roll(t, 64, 1)
                tops.append(t + pltpu.roll(t, 32, 1))
            unit = jnp.concatenate(tops, axis=0) * (1.0 / 65534.0)
            unit = jnp.concatenate([unit] * (GW // 128), axis=1)
            wtot = [
                wtot[q] + (wqr[it, r - 1, q].astype(jnp.int32).astype(F32) + 32767.0) * unit
                for q in range(gp)
            ]
        wnew = jnp.stack([wown[q] * wtot[q][:N] / wtot[q][N:] * scale_row for q in range(gp)])
        wown[...] = wnew
        mine = pl.ds(me_f * gp, gp)
        if not last:
            wgb[it, mine] = wnew.astype(BF16)
            cs = [
                send(wgb.at[it, mine], wgb.at[it, mine], wg_ss.at[it, r], wg_rs.at[it, r], "frame", fpeer(r))
                for r in range(1, NF)
            ]
            for c in cs:
                c.wait_recv()
            wg[...] = wgb[it]

    pts[...] = wnew.astype(BF16)
    ptc = send(pts, ptr, pt_sem.at[0], pt_sem.at[1], "half", 1 - me_h)
    wfin[mine] = wnew
    fcs = [
        send(wfin.at[mine], wfin.at[mine], wg_ss.at[ITERS - 1, r], wg_rs.at[ITERS - 1, r], "frame", fpeer(r))
        for r in range(1, NF)
    ]
    hout_ref[...] = hf[...] / scale
    ptc.wait_recv()
    far = ptr[...].astype(F32)
    cross = jnp.zeros((128, 128), F32)
    osq = jnp.zeros((1, 128), F32)
    fsq = jnp.zeros((1, 128), F32)
    for q in range(gp):
        for h in range(GW // 128):
            a = wnew[q, :, h * 128:(h + 1) * 128]
            b = far[q, :, h * 128:(h + 1) * 128]
            cross = cross + lax.dot_general(
                a, b, (((0,), (0,)), ((), ())),
                preferred_element_type=F32, precision=lax.Precision.HIGHEST,
            )
            osq = osq + jnp.sum(a * a, axis=0, keepdims=True)
            fsq = fsq + jnp.sum(b * b, axis=0, keepdims=True)
    ri = lax.broadcasted_iota(jnp.int32, (128, 128), 0)
    ci = lax.broadcasted_iota(jnp.int32, (128, 128), 1)
    cross = jnp.where(ri // K == ci // K, cross, 0.0)
    cross = cross[0:K] + cross[K:2 * K] + cross[2 * K:3 * K] + cross[3 * K:]

    def fold(x):
        x = x + pltpu.roll(x, 64, 1)
        return x + pltpu.roll(x, 32, 1)

    pack = jnp.concatenate(
        [cross, jnp.broadcast_to(osq, (8, 128)), jnp.broadcast_to(fsq, (8, 128))], axis=0
    )
    snr[me_n] = fold(pack)
    cs = [
        send(snr.at[me_n], snr.at[me_n], sn_ss.at[r], sn_rs.at[r], "neuron", npeer(r))
        for r in range(1, NN)
    ]
    for c in cs:
        c.wait_recv()
    tot = snr[0]
    for p in range(1, NN):
        tot = tot + snr[p]
    sfr[me_f] = tot
    cs = [
        send(sfr.at[me_f], sfr.at[me_f], sf_ss.at[r], sf_rs.at[r], "frame", fpeer(r))
        for r in range(1, NF)
    ]
    for c in fcs:
        c.wait_recv()
    wout_ref[...] = wfin[...]
    for c in cs:
        c.wait_recv()
    tot = sfr[0]
    for p in range(1, NF):
        tot = tot + sfr[p]
    own_row = tot[K:K + 1]
    far_row = tot[K + 8:K + 9]
    rk = lax.broadcasted_iota(jnp.int32, (K, 128), 0)
    ck = lax.broadcasted_iota(jnp.int32, (K, 128), 1)
    own_col = jnp.sum(jnp.where(rk == ck, own_row, 0.0), axis=1, keepdims=True)
    sim = tot[:K] / jnp.sqrt((own_col + EPS) * (far_row + EPS))
    sim_ref[...] = sim[:, :K]
    rims[ITERS][0].wait_recv()
    for c in pending:
        c.wait_send()


def roll_right(x, s):
    return pltpu.roll(x, s, 1) if s else x


def roll_left(x, s):
    return pltpu.roll(x, x.shape[1] - s, 1) if s else x


def wide_kernel(
    NN, NF, T,
    ca_hbm, tof_hbm, th_hbm, w_hbm, prof_hbm,
    wout_ref, hout_ref, sim_ref,
    ca_ref, tof_ref, th_ref, w_ref, prof_ref, by_lag, wf,
    rim_s, rim_r, mtx, mrx, w32, wt32, hla, mla, ala, qs, ps,
    ndx, ndr, hb, hl, ml, al, dat, md, prx, acc, own, tx, rx, topx, topr,
    hg, wtx, wtr, wcx, wcr, far_s, far_r, snx, snr,
    isem, ssem, rsem,
):
    me_n = lax.axis_index("neuron")
    me_f = lax.axis_index("frame")
    me_h = lax.axis_index("half")
    me_c = lax.rem(me_n, 2)
    me_y = me_n // 2
    N = ca_ref.shape[0]
    F = NF * T
    NB = N // NF
    KC = K // 2
    TC = T // 2
    EXT = T + RIM
    pending = []

    def send(src, dst, peer):
        i = len(pending)
        c = pltpu.make_async_remote_copy(
            src_ref=src, dst_ref=dst, send_sem=ssem.at[i], recv_sem=rsem.at[i],
            device_id=peer, device_id_type=MESH,
        )
        c.start()
        pending.append(c)
        return c

    def npeer(r):
        return lax.rem(me_n + r, NN)

    def fpeer(r):
        return lax.rem(me_f + r, NF)

    core = {"neuron": me_n + 1 - 2 * me_c}
    seven = [(dy, dz) for dz in (3, 2, 1, 0) for dy in (1, 0) if dy or dz]

    def block_of(dy, dz):
        return fpeer(dz) * 2 + lax.rem(me_y + dy, 2)

    def to(dy, dz):
        return {"neuron": npeer(2 * dy), "frame": fpeer(dz)}

    others = [(dn, df) for df in (3, 2, 1, 0) for dn in (3, 2, 1, 0) if dn or df]
    barrier = pltpu.get_barrier_semaphore()
    for r in range(1, NF):
        pl.semaphore_signal(barrier, inc=1, device_id={"frame": fpeer(r)}, device_id_type=MESH)
    for r in range(1, NN):
        pl.semaphore_signal(barrier, inc=1, device_id={"neuron": npeer(r)}, device_id_type=MESH)
    pl.semaphore_signal(barrier, inc=1, device_id={"half": 1 - me_h}, device_id_type=MESH)

    loads = [
        pltpu.make_async_copy(a, b, isem.at[i])
        for i, (a, b) in enumerate([
            (th_hbm, th_ref), (tof_hbm, tof_ref), (ca_hbm, ca_ref), (prof_hbm, prof_ref), (w_hbm, w_ref),
        ])
    ]
    for c in loads:
        c.start()

    def turn(x):
        out = []
        for h in range(GW // 128):
            t = x[:, h * 128:(h + 1) * 128].T
            out.append(jnp.concatenate([t[q * K:(q + 1) * K] for q in range(4)], axis=1))
        return jnp.concatenate(out, axis=1)

    for c in loads[:-1]:
        c.wait()

    trials = th_ref.shape[1]
    rows = lax.broadcasted_iota(jnp.int32, (trials, trials), 0)
    cols = lax.broadcasted_iota(jnp.int32, (trials, trials), 1)
    thf = th_ref[...].astype(F32)
    th_col = jnp.sum(jnp.where(rows == cols, thf, 0.0), axis=1, keepdims=True)
    chosen = jnp.where(th_col == me_h.astype(F32), 1.0, 0.0)
    hit = lax.broadcasted_iota(jnp.int32, (trials, T), 0) == tof_ref[...]
    mask = jnp.sum(jnp.where(hit, chosen, 0.0), axis=0, keepdims=True)
    masked = ca_ref[...].astype(F32) * mask
    body = masked.astype(BF16)
    prof = prof_ref[...].astype(BF16)
    rim_s[0, :N] = body[:, :RIM]
    rim_s[0, N:] = prof[:, :RIM]
    rim_s[1, :K] = prof[:, T - RIM:]
    for z in range(NF):
        x = masked[z * NB:(z + 1) * NB]
        mtx[z] = jnp.concatenate([x[:, :TC], x[:, TC:]], axis=0).astype(BF16)

    loads[-1].wait()
    for j in range(K * L // 128):
        by_lag[j * 128:(j + 1) * 128, :N] = w_ref[:, j * 128:(j + 1) * 128].T

    def lay_out(lo, hi):
        for a in range(lo, hi):
            x = jnp.concatenate(
                [by_lag[pl.ds(a * GL + b, K, stride=L), :][:, :N] for b in range(GL)], axis=1
            )
            wt32[a * K:(a + 1) * K] = x.astype(BF16)
            x = turn(x)
            wf[a] = x
            w32[a * N:(a + 1) * N] = x.astype(BF16)

    pl.semaphore_wait(barrier, (NF - 1) + (NN - 1) + 1)

    to_left = send(rim_s.at[0], rim_r.at[0], {"frame": fpeer(NF - 1)})
    to_right = send(rim_s.at[1, pl.ds(0, K)], rim_r.at[1, pl.ds(0, K)], {"frame": fpeer(1)})
    mcs = [
        send(mtx.at[fpeer(r)], mrx.at[me_f], {"frame": fpeer(r)})
        for r in (3, 2, 1)
    ]
    mrx[me_f] = mtx[me_f]

    lay_out(0, GROUPS)
    mine = pl.ds(pl.multiple_of(me_f * NB, NB), NB)
    w8 = jnp.concatenate([wf[a, mine, :] for a in range(GROUPS)], axis=0)

    def lags(dst, x, roll, lo=0, hi=None, at=0):
        n = x.shape[0]
        hi = x.shape[1] if hi is None else hi
        for b in range(GL):
            dst[b * n:(b + 1) * n, at:at + hi - lo] = roll(x, b)[:, lo:hi]

    IN = T - RIM
    lags(mla, body, roll_left, 0, IN)
    qs[:, :IN] = dot(wt32[...], mla[:, :IN])
    lags(hla, prof, roll_right, RIM, T, 2 * RIM)
    ps[:, 2 * RIM:EXT] = dot(w32[...], hla[:, 2 * RIM:EXT])

    to_left.wait_recv()
    mext = jnp.concatenate([body, rim_r[0, :N]], axis=1)
    mask_ext = jnp.where(mext.astype(F32) > 0.0, 1.0, 0.0)

    def shifted_sum(q):
        s = q[:K]
        for a in range(1, GROUPS):
            s = s + roll_left(q[a * K:(a + 1) * K], a * GL)
        return s[:, :T]

    def scatter(kind, s):
        for p in range(NN):
            a, b = (p % 2) * KC, (p // 2) * TC
            ndx[kind, p] = s[a:a + KC, b:b + TC]
        return [
            send(ndx.at[kind, npeer(r)], ndr.at[kind, r - 1], {"neuron": npeer(r)})
            for r in range(1, NN)
        ]

    lags(mla, mext[:, IN:], roll_left, at=IN)
    qs[:, IN:] = dot(wt32[...], mla[:, IN:])
    lags(hla, jnp.concatenate([prof[:, IN:], rim_r[0, N:]], axis=1), roll_right, RIM, 2 * RIM, EXT)
    ps[:, EXT:] = dot(w32[...], hla[:, EXT:])
    ncs = scatter(0, shifted_sum(qs[...]))
    to_right.wait_recv()
    lags(hla, jnp.concatenate([rim_r[1, :K], prof[:, :RIM]], axis=1), roll_right)
    ps[:, :2 * RIM] = dot(w32[...], hla[:, :2 * RIM])
    p = ps[...]
    s = p[:N]
    for a in range(1, GROUPS):
        s = s + roll_right(p[a * N:(a + 1) * N], a * GL)
    approx = (s[:, RIM:].astype(BF16).astype(F32) * mask_ext).astype(BF16)
    lags(ala, approx, roll_left)
    dcs = scatter(1, shifted_sum(dot(wt32[...], ala[...])))

    own_rows = pl.ds(pl.multiple_of(me_c * KC, KC), KC)
    far_rows = pl.ds(pl.multiple_of((1 - me_c) * KC, KC), KC)
    hown = prof_ref[own_rows, pl.ds(pl.multiple_of(me_y * TC, TC), TC)]
    num = ndx[0, me_n]
    den = ndx[1, me_n]
    for r in range(1, NN):
        ncs[r - 1].wait_recv()
        num = num + ndr[0, r - 1]
    for r in range(1, NN):
        dcs[r - 1].wait_recv()
        den = den + ndr[1, r - 1]
    hown = hown * num / jnp.maximum(den, 1.0)

    def spot(c, blk):
        return pl.ds(pl.multiple_of(c * KC, KC), KC), pl.ds(pl.multiple_of(blk * TC, TC), TC)

    lane = lax.broadcasted_iota(jnp.int32, (8, 128), 1)

    def gather_h(it):
        a, b = spot(me_c, block_of(0, 0))
        hb[it, a, b] = hown.astype(BF16)
        cs = [send(hb.at[it, a, b], hb.at[it, a, b], to(dy, dz)) for dy, dz in seven]
        relays = [send(hb.at[it, a, b], hb.at[it, a, b], core)]
        return cs, relays

    def half_lags(it, rows_of, c):
        x = hb[it, rows_of, :]
        for b in range(GL):
            hl[pl.ds(pl.multiple_of(b * K + c * KC, KC), KC), :] = roll_right(x, b)

    def relay_h(it, cs, relays):
        for i in range(len(seven) - 1, -1, -1):
            cs[i].wait_recv()
            dy, dz = seven[i]
            a, b = spot(me_c, block_of(dy, NF - dz))
            relays.append(send(hb.at[it, a, b], hb.at[it, a, b], core))
        half_lags(it, own_rows, me_c)
        for c in relays:
            c.wait_recv()
        half_lags(it, far_rows, 1 - me_c)

    def squares(it):
        x = hb[it].astype(F32)
        return jnp.sum(x * x, axis=1, keepdims=True)

    cs, relays = gather_h(0)

    for c in mcs:
        c.wait_recv()
    for z in range(NF):
        x = mrx[z].astype(F32)
        md[:, z * T:z * T + TC] = x[:NB]
        md[:, z * T + TC:(z + 1) * T] = x[NB:]
    data = md[...]
    mask_all = jnp.where(data[0:1] > 0.0, 1.0, 0.0)
    rolled = [roll_left(data, a * GL) for a in range(GROUPS)]
    for a in range(GROUPS):
        dat[a * 2 * NB:a * 2 * NB + NB] = rolled[a]
    lags(ml, jnp.concatenate(rolled[:4], axis=0).astype(BF16), roll_left)

    def recon(wb):
        p = dot(wb, hl[...])
        s = p[:NB]
        for a in range(1, GROUPS):
            s = s + roll_right(p[a * NB:(a + 1) * NB], a * GL)
        return s.astype(BF16).astype(F32) * mask_all

    def corr(wt, m):
        q = dot(wt, m[...])
        return q[:K] + roll_left(q[K:], 4 * GL)

    def template_ratio():
        approx = recon(w8.astype(BF16))
        for a in range(GROUPS):
            dat[a * 2 * NB + NB:(a + 1) * 2 * NB] = roll_left(approx, a * GL)
        s = lax.dot_general(
            dat[...].astype(BF16), hl[...], (((1,), (1,)), ((), ())), preferred_element_type=F32
        )
        wnum = jnp.concatenate([s[a * 2 * NB:a * 2 * NB + NB] for a in range(GROUPS)], axis=0)
        wden = jnp.concatenate([s[a * 2 * NB + NB:(a + 1) * 2 * NB] for a in range(GROUPS)], axis=0)
        return wnum, wden

    relay_h(0, cs, relays)
    wnum, wden = template_ratio()
    w8 = w8 * wnum / wden

    wt = jnp.concatenate([turn(w8[:4 * NB]), turn(w8[4 * NB:])], axis=0).astype(BF16)

    def reduce_start(kind, s):
        acc[kind] = s
        return send(acc.at[kind, far_rows], prx.at[kind], core)

    def reduce_spread(kind, c):
        c.wait_recv()
        s = acc[kind, own_rows, :] + prx[kind]
        own[kind] = s
        top = jnp.maximum(jnp.max(s, axis=1, keepdims=True), 1e-30)
        topx[kind] = jnp.sum(jnp.where(eye, top, 0.0), axis=0, keepdims=True)
        ts = [send(topx.at[kind], topr.at[kind * 7 + i], to(dy, dz)) for i, (dy, dz) in enumerate(seven)]
        code = jnp.round(s * (65534.0 / top)) - 32767.0
        tx[kind] = jnp.minimum(code, 32767.0).astype(jnp.int32).astype(jnp.int16)
        return ts, [
            send(
                tx.at[kind, :, pl.ds(pl.multiple_of(block_of(dy, dz) * TC, TC), TC)],
                rx.at[kind, i], to(dy, dz),
            )
            for i, (dy, dz) in enumerate(seven)
        ]

    def reduce_done(kind, sent):
        ts, cs = sent
        t = own[kind, :, pl.ds(pl.multiple_of(block_of(0, 0) * TC, TC), TC)]
        for i in range(len(seven) - 1, -1, -1):
            ts[i].wait_recv()
            unit = jnp.sum(jnp.where(eye, topr[kind * 7 + i], 0.0), axis=1, keepdims=True) * (1.0 / 65534.0)
            cs[i].wait_recv()
            t = t + (rx[kind, i].astype(jnp.int32).astype(F32) + 32767.0) * unit
        return t

    eye = lax.broadcasted_iota(jnp.int32, (KC, 128), 0) == lax.broadcasted_iota(jnp.int32, (KC, 128), 1)
    nc = reduce_start(0, corr(wt, ml))
    approx = recon(w8.astype(BF16))
    ncs = reduce_spread(0, nc)
    lags(al, jnp.concatenate([roll_left(approx, a * GL) for a in range(4)], axis=0).astype(BF16), roll_left)
    dc = reduce_start(1, corr(wt, al))
    scale0 = jnp.sqrt(squares(0) + EPS)
    dcs = reduce_spread(1, dc)
    num = reduce_done(0, ncs)
    den = reduce_done(1, dcs)
    s0 = jnp.where(me_c == 0, scale0[:KC], scale0[KC:])
    hown = hown * (num * s0) / jnp.maximum(den * s0, 1.0)
    cs, relays = gather_h(1)
    relay_h(1, cs, relays)
    hg[me_n] = hown
    hcs = [send(hg.at[me_n], hg.at[me_n], {"neuron": npeer(r)}) for r in (3, 2, 1)]
    wnum, wden = template_ratio()
    scale = jnp.sqrt(squares(1) + EPS * scale0 * scale0)
    ek = lax.broadcasted_iota(jnp.int32, (K, GW), 0)
    ec = lax.broadcasted_iota(jnp.int32, (K, GW), 1) % K
    scale_row = jnp.sum(jnp.where(ek == ec, scale, 0.0), axis=0, keepdims=True)
    w8 = w8 * wnum / wden * scale_row

    far_s[...] = w8.astype(BF16)
    fc = send(far_s, far_r, {"half": 1 - me_h})
    rows8 = GROUPS * NB
    eye8 = lax.broadcasted_iota(jnp.int32, (rows8, 128), 0) == lax.broadcasted_iota(jnp.int32, (rows8, 128), 1)
    top = jnp.maximum(jnp.max(w8, axis=1, keepdims=True), 1e-30)
    wtx[...] = jnp.sum(jnp.where(eye8, top, 0.0), axis=0, keepdims=True)
    x = jnp.minimum(jnp.round(w8 * (65534.0 / top)) - 32767.0, 32767.0)
    wcx[...] = x.astype(jnp.int32).astype(jnp.int16)
    wcs = [
        (
            send(wtx, wtr.at[r - 1], {"frame": fpeer(r)}),
            send(wcx, wcr.at[r - 1], {"frame": fpeer(r)}),
        )
        for r in (3, 2, 1)
    ]

    def place(z, code, top_row):
        unit = jnp.sum(jnp.where(eye8, top_row, 0.0), axis=1, keepdims=True) * (1.0 / 65534.0)
        y = (code.astype(jnp.int32).astype(F32) + 32767.0) * unit
        at = pl.ds(pl.multiple_of(z * NB, NB), NB)
        for a in range(GROUPS):
            wf[a, at, :] = y[a * NB:(a + 1) * NB]

    place(me_f, wcx[...], wtx[...])
    for c in hcs:
        c.wait_recv()
    for p in range(NN):
        a, b = (p % 2) * KC, (p // 2) * TC
        hout_ref[a:a + KC, b:b + TC] = hg[p] / scale[a:a + KC]
    fc.wait_recv()
    far = far_r[...].astype(F32)

    def split(x):
        parts = []
        for _ in range(3):
            parts.append(x.astype(BF16))
            x = x - parts[-1].astype(F32)
        return parts

    cross = jnp.zeros((128, 128), F32)
    osq = jnp.zeros((1, 128), F32)
    fsq = jnp.zeros((1, 128), F32)
    for h in range(GW // 128):
        a = w8[:, h * 128:(h + 1) * 128]
        b = far[:, h * 128:(h + 1) * 128]
        for part in split(a):
            cross = cross + lax.dot_general(
                part, b.astype(BF16), (((0,), (0,)), ((), ())), preferred_element_type=F32
            )
        osq = osq + jnp.sum(a * a, axis=0, keepdims=True)
        fsq = fsq + jnp.sum(b * b, axis=0, keepdims=True)
    ri = lax.broadcasted_iota(jnp.int32, (128, 128), 0)
    ci = lax.broadcasted_iota(jnp.int32, (128, 128), 1)
    cross = jnp.where(ri // K == ci // K, cross, 0.0)
    cross = cross[0:K] + cross[K:2 * K] + cross[2 * K:3 * K] + cross[3 * K:]

    def fold(x):
        x = x + pltpu.roll(x, 64, 1)
        return x + pltpu.roll(x, 32, 1)

    cross = fold(cross)
    quad = lane // K
    pack = cross[:8]
    for q in range(1, 4):
        pack = jnp.where(quad == q, cross[q * 8:(q + 1) * 8], pack)
    for q in range(8):
        snx[:, q * 128:(q + 1) * 128] = pack[q:q + 1]
    snx[:, 8 * 128:] = jnp.where(quad[:1] < 2, fold(osq), fold(fsq))
    scs = [
        send(snx, snr.at[i], {"neuron": npeer(dn), "frame": fpeer(df)})
        for i, (dn, df) in enumerate(others)
    ]
    for i, r in enumerate((3, 2, 1)):
        for c in wcs[i]:
            c.wait_recv()
        place(fpeer(NF - r), wcr[r - 1], wtr[r - 1])
    for a in range(GROUPS):
        t = turn(wf[a])
        for b in range(GL):
            by_lag[pl.ds(a * GL + b, K, stride=L), :N] = t[:, b * K:(b + 1) * K]
    for j in range(K * L // 128):
        wout_ref[:, j * 128:(j + 1) * 128] = by_lag[j * 128:(j + 1) * 128, :N].T
    tot = snx[...]
    for i in range(len(others) - 1, -1, -1):
        scs[i].wait_recv()
        tot = tot + snr[i]
    own_row = tot[:, 8 * 128:]
    far_row = pltpu.roll(own_row, 64, 1)
    tot = jnp.concatenate([tot[:, q * 128:(q + 1) * 128] for q in range(8)], axis=0)
    rk = lax.broadcasted_iota(jnp.int32, (K, 128), 0)
    ck = lax.broadcasted_iota(jnp.int32, (K, 128), 1)
    own_col = jnp.sum(jnp.where(rk == ck, own_row, 0.0), axis=1, keepdims=True)
    full = jnp.concatenate(
        [tot] + [pltpu.roll(tot, 128 - q * K, 1) for q in range(1, 4)], axis=0
    )
    sim = full / jnp.sqrt((own_col + EPS) * (far_row + EPS))
    sim_ref[...] = sim[:, :K]
    for c in pending:
        c.wait_send()


def wide_call(NN, NF, T, N, trials):
    F = NF * T
    NB = N // NF
    KC = K // 2
    TC = T // 2
    EXT = T + RIM
    V = pltpu.VMEM
    D = pltpu.SemaphoreType.DMA
    vmem = pl.BlockSpec(memory_space=pltpu.VMEM)
    return pl.pallas_call(
        functools.partial(wide_kernel, NN, NF, T),
        out_shape=(
            jax.ShapeDtypeStruct((N, K * L), F32),
            jax.ShapeDtypeStruct((K, T), F32),
            jax.ShapeDtypeStruct((K, K), F32),
        ),
        in_specs=[pl.BlockSpec(memory_space=pl.ANY)] * 5,
        out_specs=(vmem,) * 3,
        scratch_shapes=[
            V((N, T), BF16),
            V((1, T), jnp.int32),
            V((1, trials), jnp.int32),
            V((N, K * L), F32),
            V((K, T), F32),
            V((K * L, 128), F32),
            V((GROUPS, N, GW), F32),
            V((2, N + K, RIM), BF16),
            V((2, N + K, RIM), BF16),
            V((NF, 2 * NB, TC), BF16),
            V((NF, 2 * NB, TC), BF16),
            V((GROUPS * N, GW), BF16),
            V((GROUPS * K, GW), BF16),
            V((GW, EXT + RIM), BF16),
            V((GW, EXT), BF16),
            V((GW, EXT), BF16),
            V((GROUPS * K, EXT), F32),
            V((GROUPS * N, EXT + RIM), F32),
            V((2, NN, KC, TC), F32),
            V((2, NN - 1, KC, TC), F32),
            V((ITERS, K, F), BF16),
            V((GW, F), BF16),
            V((GW, F), BF16),
            V((GW, F), BF16),
            V((2 * GROUPS * NB, F), F32),
            V((NB, F), F32),
            V((2, KC, F), F32),
            V((2, K, F), F32),
            V((2, KC, F), F32),
            V((2, KC, F), jnp.int16),
            V((2, 7, KC, TC), jnp.int16),
            V((2, 1, 128), F32),
            V((14, 1, 128), F32),
            V((NN, KC, TC), F32),
            V((1, 128), F32),
            V((NF - 1, 1, 128), F32),
            V((GROUPS * NB, GW), jnp.int16),
            V((NF - 1, GROUPS * NB, GW), jnp.int16),
            V((GROUPS * NB, GW), BF16),
            V((GROUPS * NB, GW), BF16),
            V((1, 9 * 128), F32),
            V((NN * NF - 1, 1, 9 * 128), F32),
            D((5,)),
            D((104,)),
            D((104,)),
        ],
        compiler_params=pltpu.CompilerParams(
            collective_id=1, has_side_effects=True, vmem_limit_bytes=56 << 20
        ),
    )


def emit_kernel(w_ref, h_ref, s_ref, w_out, h_out, s_out, sem):
    pairs = [(h_ref, h_out.at[0]), (s_ref, s_out.at[0])]
    step = w_ref.shape[1] // 2
    for r in range(w_ref.shape[0] // 8):
        for q in range(2):
            part = (pl.ds(r * 8, 8), pl.ds(q * step, step))
            pairs.append((w_ref.at[part], w_out.at[0].at[part]))
    cs = [pltpu.make_async_copy(a, b, sem.at[i]) for i, (a, b) in enumerate(pairs)]
    for c in cs:
        c.start()
    for c in cs:
        c.wait()


def emit(*arrays):
    return pl.pallas_call(
        emit_kernel,
        out_shape=tuple(jax.ShapeDtypeStruct((1, *x.shape), F32) for x in arrays),
        in_specs=[pl.BlockSpec(memory_space=pltpu.VMEM)] * 3,
        out_specs=(pl.BlockSpec(memory_space=pl.ANY),) * 3,
        scratch_shapes=[pltpu.SemaphoreType.DMA((2 + arrays[0].shape[0] // 4,))],
    )(*arrays)


def tall_call(NN, NF, T, N):
    gp = GROUPS // NF
    rg = K // 8
    w = T * rg // NN
    EXT = T + RIM
    V = pltpu.VMEM
    D = pltpu.SemaphoreType.DMA
    vmem = pl.BlockSpec(memory_space=pltpu.VMEM)
    return pl.pallas_call(
        functools.partial(kernel, NN, NF, T),
        out_shape=(
            jax.ShapeDtypeStruct((GROUPS, N, GW), F32),
            jax.ShapeDtypeStruct((K, T), F32),
            jax.ShapeDtypeStruct((K, K), F32),
        ),
        in_specs=[vmem] * 5,
        out_specs=(vmem,) * 3,
        scratch_shapes=[
            V((K, 2 * RIM + T + RIM), BF16),
            V((L * K, EXT), BF16),
            V((N, EXT), BF16),
            V((N, EXT + RIM), BF16),
            V((L * N, T), BF16),
            V((L * N, T), BF16),
            V((N, EXT), F32),
            V((K, T), F32),
            V((K, T), F32),
            V((K, T), F32),
            V((GROUPS, N, GW), BF16),
            V((GROUPS, K, GW), BF16),
            V((gp, N, GW), F32),
            V((2 * N, T), BF16),
            V((N, RIM), BF16),
            V((N, RIM), BF16),
            V((ITERS + 1, 2, K, RIM), F32),
            V((ITERS + 1, 2, K, RIM), F32),
            V((ITERS, 2, NN, 8, w), F32),
            V((ITERS, 2, NN - 1, 8, w), F32),
            V((ITERS, NN, 8, w), F32),
            V((ITERS, NF, K, 128), F32),
            V((ITERS, NF - 1, gp, 2 * N, GW), jnp.int16),
            V((ITERS, NF - 1, gp, 2 * N, GW), jnp.int16),
            V((ITERS, NF - 1, 2 * N // 4, 128), F32),
            V((ITERS, NF - 1, 2 * N // 4, 128), F32),
            V((ITERS - 1, GROUPS, N, GW), BF16),
            V((GROUPS, N, GW), F32),
            V((gp, N, GW), BF16),
            V((gp, N, GW), BF16),
            V((NN, K + 16, 128), F32),
            V((NF, K + 16, 128), F32),
            D((2,)),
            D((ITERS + 1, 2)),
            D((ITERS + 1, 2)),
            D((2 * ITERS, NN)),
            D((2 * ITERS, NN)),
            D((ITERS, NN)),
            D((ITERS, NN)),
            D((ITERS, NF)),
            D((ITERS, NF)),
            D((ITERS, NF)),
            D((ITERS, NF)),
            D((ITERS, NF)),
            D((ITERS, NF)),
            D((ITERS, NF)),
            D((ITERS, NF)),
            D((2,)),
            D((NN,)),
            D((NN,)),
            D((NF,)),
            D((NF,)),
        ],
        compiler_params=pltpu.CompilerParams(
            collective_id=0, has_side_effects=True, vmem_limit_bytes=50 << 20
        ),
    )


def per_device(calcium, trial_of_frame, trial_half, loadings, profiles):
    NN = lax.axis_size("neuron")
    NF = lax.axis_size("frame")
    N, T = calcium.shape
    small = (calcium, trial_of_frame.reshape(1, T), trial_half.reshape(1, -1))
    if NN == 4 and NF == 4 and N == K:
        call = wide_call(NN, NF, T, N, trial_half.shape[0])
        return emit(*call(*small, loadings[0], profiles[0]))
    w_groups = loadings[0].reshape(N, K, GROUPS, GL).transpose(2, 0, 3, 1).reshape(GROUPS, N, GW)
    wout, hout, sim = tall_call(NN, NF, T, N)(*small, w_groups, profiles[0])
    loads = wout.reshape(GROUPS, N, GL, K).transpose(1, 3, 0, 2).reshape(1, N, K * L)
    return loads, hout[None], sim[None]


def solution(mesh):
    placed = (
        P("neuron", "frame"),
        P("frame"),
        P(),
        P("half", "neuron", None),
        P("half", None, "frame"),
    )
    return jax.shard_map(
        per_device,
        mesh=mesh,
        in_specs=placed,
        out_specs=(P("half", "neuron", None), P("half", None, "frame"), P("half", None, None)),
        check_vma=False,
    )
```
